32 devices in a mesh: fsdp: 8 (over z, x), dp: 4 (over y, core).
Axes of the slice: x: 2, y: 2, z: 4, core: 2. Of those that a mesh axis runs over, the one named last changes fastest.
Arguments:
- hidden: bfloat16 [2, 32, 384, 1536], P(None, ('fsdp', 'dp')), may hold values from -6 to 6
- teacher: bfloat16 [2, 32, 384, 1536], P(None, ('fsdp', 'dp')), may hold values from -6 to 6
- cotangent: bfloat16 [2, 32, 384, 1536], P(None, ('fsdp', 'dp')), may hold values from -6.3329935e-07 to 6.3329935e-07
- valid_mask: int32 [2, 32, 384], P(None, ('fsdp', 'dp')), may hold values from 0 to 1, as said below
- blocks: int32 [2, 32, 384], P(None, ('fsdp', 'dp')), may hold values from 0 to 2, never falling along the last dimension, each value on 1 to 256 neighbouring positions
- buckets: int32 [384, 384], replicated, may hold values from 0 to 31
- first_gain: bfloat16 [1536], P(('fsdp', 'dp')), may hold values from 0.25 to 1.75
- query_weight: bfloat16 [1536, 768], P('fsdp', 'dp'), may hold values from -0.0390625 to 0.0390625
- key_weight: bfloat16 [1536, 768], P('fsdp', 'dp'), may hold values from -0.15625 to 0.15625
- value_weight: bfloat16 [1536, 768], P('fsdp', 'dp'), may hold values from -0.15625 to 0.15625
- output_weight: bfloat16 [1536, 768], P('fsdp', 'dp'), may hold values from -1.25 to 1.25
- second_gain: bfloat16 [1536], P(('fsdp', 'dp')), may hold values from 0.25 to 1.75
- gate_weight: bfloat16 [1536, 3968], P('fsdp', 'dp'), may hold values from -0.15625 to 0.15625
- up_weight: bfloat16 [1536, 3968], P('fsdp', 'dp'), may hold values from -0.15625 to 0.15625
- down_weight: bfloat16 [1536, 3968], P('fsdp', 'dp'), may hold values from -0.1875 to 0.1875
- bias_table: bfloat16 [32, 12], replicated, may hold values from -5 to 5
Outputs:
- layer_output: bfloat16 [2, 32, 384, 1536], P(None, ('fsdp', 'dp'))
- loss_value: float32 [], replicated
- hidden_grad: bfloat16 [2, 32, 384, 1536], P(None, ('fsdp', 'dp'))
- first_gain_grad: float32 [1536], P(('fsdp', 'dp'))
- query_grad: float32 [1536, 768], P('fsdp', 'dp')
- key_grad: float32 [1536, 768], P('fsdp', 'dp')
- value_grad: float32 [1536, 768], P('fsdp', 'dp')
- output_grad: float32 [1536, 768], P('fsdp', 'dp')
- second_gain_grad: float32 [1536], P(('fsdp', 'dp'))
- gate_grad: float32 [1536, 3968], P('fsdp', 'dp')
- up_grad: float32 [1536, 3968], P('fsdp', 'dp')
- down_grad: float32 [1536, 3968], P('fsdp', 'dp')
- bias_grad: float32 [32, 12], replicated
The draws below stay inside these ranges and needn't reach their ends.
Inputs may be any that keep to these rules, and one draw needn't show every extreme that they name: `valid_mask`: 1 marks a valid token. `blocks`: never falls along a sequence; every block number up to the largest occurs, each block has 1 to 256 positions and some block has exactly 256.
All inputs are finite; a program needn't handle non-finite values.
Results may differ from the reference program's by a relative error of at most 0.013.
The reference program's roundings to bfloat16 on the way count: a program that leaves them out, or rounds other values in their place, can miss the bound.
Values may be sent and summed in bfloat16 or wider, within the bound.
A program may use at most 320 MiB of HBM per device.

```python
import math
import jax
import jax.numpy as jnp
import numpy as np
from jax import lax

D = 1536
HEADS = 12
HEAD = 64
FF = 3968
BUCKETS = 32
SEQ = 384
BLOCK = 256
MICRO = 2
INNER = 768
SEQUENCES = 32
LOSS_SCALE = 37748736


def draw_valid_mask(key, part):
    ranks = jnp.arange(SEQUENCES, dtype=jnp.int32)
    limits = 300 + 600 * ranks // max(SEQUENCES - 1, 1)
    rolls = jax.random.randint(key, (MICRO, SEQUENCES, SEQ), 0, 1000)
    return (rolls < limits[None, :, None]).astype(jnp.int32)


def set_ends(values, own_key, least, high):
    longest = values.shape.index(max(values.shape))
    spots = []
    for shift in (0, 1):
        where = [jax.random.randint(jax.random.fold_in(own_key, axis), (), 0, length) for axis, length in enumerate(values.shape)]
        where[longest] = (where[longest] + shift) % values.shape[longest]
        spots.append(tuple(where))
    return values.at[spots[0]].set(least).at[spots[1]].set(high)


def level_of(rng, shape, shards, smallest, largest):
    loudness = 1.0
    for axis_at, blocks in shards:
        steps = jax.random.uniform(jax.random.fold_in(jax.random.fold_in(rng, 6), axis_at), (blocks,), jnp.float32, smallest / len(shards), largest / len(shards))
        loudness = loudness * jnp.repeat(jnp.exp(steps), shape[axis_at] // blocks).reshape((-1,) + (1,) * (len(shape) - 1 - axis_at))
    return loudness


def length_profile(amount, total, reach, lean):
    portions = [(1 << 20) // math.isqrt(standing ** lean) + 1 for standing in range(2, amount + 1)]
    surplus, counts = total - reach - (amount - 1), [1] * (amount - 1)
    while surplus > 0:
        free = [i for i in range(amount - 1) if counts[i] < reach]
        pool, budget = sum([portions[i] for i in free]), surplus
        for i in free:
            addition = min(reach - counts[i], max(1, budget * portions[i] // pool), surplus)
            counts[i] = counts[i] + addition
            surplus = surplus - addition
    return np.array([reach] + counts)


def uneven_parts(key, number_of, total, bound, slope):
    if number_of == 2:
        one = jax.random.randint(key, (), max(1, total - bound), min(bound, total - 1) + 1)
        return jnp.stack([one, total - one])
    sizes = jnp.asarray(length_profile(number_of, total, bound, slope), jnp.int32)
    pairs = (number_of - 1) // 2
    giver, receiver = sizes[1:1 + 2 * pairs:2], sizes[2:2 + 2 * pairs:2]
    margin = jnp.minimum(giver - 1, bound - receiver)
    passed = jax.random.randint(jax.random.fold_in(key, 1), (pairs,), 0, 1 << 20) % (margin + 1)
    sizes = sizes.at[1:1 + 2 * pairs:2].set(giver - passed).at[2:2 + 2 * pairs:2].set(receiver + passed)
    return sizes[jax.random.permutation(jax.random.fold_in(key, 2), number_of)]


def scatter_about(stream_key, shape, deviation, bound, split=(), held_as=jnp.bfloat16):
    entries = deviation * jax.random.normal(stream_key, shape, jnp.float32)
    if split:
        entries = entries * level_of(stream_key, shape, split, -0.22, 0.18)
    return jnp.clip(entries, -bound, bound).astype(held_as)


def setup_inputs(seed: int = 0) -> dict:
    splits = jax.random.split(jax.random.key(seed), 17)
    return {
        "hidden": scatter_about(splits[0], (MICRO, SEQUENCES, SEQ, D), 1.0, 6.0, ((1, 32),)),
        "teacher": scatter_about(splits[1], (MICRO, SEQUENCES, SEQ, D), 1.0, 6.0, ((1, 32),)),
        "cotangent": scatter_about(splits[2], (MICRO, SEQUENCES, SEQ, D), (4 * LOSS_SCALE ** -1), 6.332993507385254e-07, ((1, 32),)),
        "valid_mask": draw_valid_mask(jax.random.fold_in(splits[16], 71), 0),
        "blocks": jax.vmap(lambda own: jnp.searchsorted(jnp.cumsum(uneven_parts(own, 2 * SEQ // BLOCK, SEQ, BLOCK, 1)), jnp.arange(SEQ), side="right"))(jax.random.split(splits[4], MICRO * SEQUENCES)).reshape((MICRO, SEQUENCES, SEQ)).astype(jnp.int32),
        "buckets": set_ends(jax.random.randint(splits[5], (SEQ, SEQ), 0, BUCKETS), jax.random.fold_in(splits[5], 1), 0, BUCKETS - 1).astype(jnp.int32),
        "first_gain": jnp.clip(1.0 + 0.15 * jax.random.normal(splits[6], (D,), jnp.float32), 0.25, 1.75).astype(jnp.bfloat16),
        "query_weight": scatter_about(splits[7], (D, INNER), (16 * D) ** -0.5, 0.0390625, ((0, 8), (1, 4))),
        "key_weight": scatter_about(splits[8], (D, INNER), D ** -0.5, 0.15625, ((0, 8), (1, 4))),
        "value_weight": scatter_about(splits[9], (D, INNER), D ** -0.5, 0.15625, ((0, 8), (1, 4))),
        "output_weight": scatter_about(splits[10], (D, INNER), (INNER // 32) ** -0.5, 1.25, ((0, 8), (1, 4))),
        "second_gain": jnp.clip(1.0 + 0.15 * jax.random.normal(splits[11], (D,), jnp.float32), 0.25, 1.75).astype(jnp.bfloat16),
        "gate_weight": scatter_about(splits[12], (D, FF), D ** -0.5, 0.15625, ((0, 8), (1, 4))),
        "up_weight": scatter_about(splits[13], (D, FF), D ** -0.5, 0.15625, ((0, 8), (1, 4))),
        "down_weight": scatter_about(splits[14], (D, FF), (FF // 4) ** -0.5, 0.1875, ((0, 8), (1, 4))),
        "bias_table": scatter_about(splits[15], (BUCKETS, HEADS), 1.0, 5.0),
    }


EPS = 1e-06
NEG = -1000000000.0
HIGH = lax.Precision.HIGHEST

@jax.custom_vjp
def low(v):
    return lax.optimization_barrier(v.astype(jnp.bfloat16)).astype(jnp.float32)

@jax.custom_vjp
def low_back(v):
    return v

def low_keep(v):
    return (low(v), None)

def low_pass(kept, grad):
    return (grad,)

def back_keep(v):
    return (v, None)

def back_low(kept, grad):
    return (low(grad),)
low.defvjp(low_keep, low_pass)
low_back.defvjp(back_keep, back_low)

def matmul_high(former, latter):
    return jnp.matmul(former, latter, precision=HIGH)

def rms_norm(inputs, norm_gain):
    return inputs * lax.rsqrt(lax.optimization_barrier(jnp.mean(inputs * inputs, axis=-1, keepdims=True)) + EPS) * norm_gain

def layer(inputs, param_set, allowed, buckets):
    gain_one, query_mat, key_mat, value_mat, output_mat, gain_two, gate_mat, up_mat, down_mat, table_full = param_set
    head_shape = inputs.shape[:2] + (HEADS, HEAD)
    normed_one = low(rms_norm(inputs, gain_one))
    queries = low_back(low(matmul_high(normed_one, query_mat))).reshape(head_shape)
    key_heads = low_back(low(matmul_high(normed_one, key_mat))).reshape(head_shape)
    value_heads = low_back(low(matmul_high(normed_one, value_mat))).reshape(head_shape)
    position_bias = jnp.transpose(table_full[buckets], (2, 0, 1))
    scores = jnp.einsum('rqhd,rkhd->rhqk', queries, key_heads, precision=HIGH)
    scores = low_back(scores + position_bias[None])
    scores = jnp.where(allowed[:, None], scores, NEG)
    softmax_low = low(jax.nn.softmax(scores, axis=-1))
    attended = jnp.einsum('rhqk,rkhd->rqhd', softmax_low, value_heads, precision=HIGH)
    attended = low_back(low(attended.reshape(inputs.shape[:2] + (INNER,))))
    attention_out = low_back(matmul_high(attended, output_mat.T))
    middle = inputs + attention_out
    normed_two = low(rms_norm(middle, gain_two))
    gate_pre = low_back(matmul_high(normed_two, gate_mat))
    up_pre = low_back(matmul_high(normed_two, up_mat))
    hidden_act = low(jax.nn.gelu(gate_pre, approximate=True) * up_pre)
    ffn_out = low_back(matmul_high(hidden_act, down_mat.T))
    return middle + ffn_out

def reference(hidden, teacher, cotangent, valid_mask, blocks, buckets, first_gain, query_weight, key_weight, value_weight, output_weight, second_gain, gate_weight, up_weight, down_weight, bias_table):
    sequences_all = MICRO * SEQUENCES
    members = max((candidate for candidate in range(1, sequences_all + 1) if sequences_all % candidate == 0 and candidate * SEQ <= 4096))
    rounds = sequences_all // members
    scale_factor = jnp.float32(LOSS_SCALE)

    def regroup(array):
        return array.reshape((rounds, members) + array.shape[2:])
    valid_total = jnp.sum(valid_mask.astype(jnp.float32))
    param_set = jax.tree.map(lambda weight_in: weight_in.astype(jnp.float32), (first_gain, query_weight, key_weight, value_weight, output_weight, second_gain, gate_weight, up_weight, down_weight, bias_table))
    rows_iota = lax.broadcasted_iota(jnp.int32, (SEQ, SEQ), 0)
    cols_iota = lax.broadcasted_iota(jnp.int32, (SEQ, SEQ), 1)
    diagonal = rows_iota == cols_iota

    def one_round(carry, batch):
        grad_sums, loss_sum = carry
        inputs_low, target_low, upstream_low, valid_round, block_round = batch
        inputs = inputs_low.astype(jnp.float32)
        target = target_low.astype(jnp.float32)
        upstream = upstream_low.astype(jnp.float32)
        valid_float = valid_round.astype(jnp.float32)
        allowed = (block_round[:, None, :] <= block_round[:, :, None]) & (valid_round[:, None, :] == 1) | diagonal[None]

        def objective(params_in, inputs_in):
            layer_full = layer(inputs_in, params_in, allowed, buckets)
            residual_gap = layer_full - target
            loss_part = jnp.sum(valid_float[..., None] * residual_gap * residual_gap) / (valid_total * D)
            return (scale_factor * (jnp.sum(layer_full * upstream) + loss_part), (layer_full, loss_part))
        _, pullback, extras = jax.vjp(objective, param_set, inputs, has_aux=True)
        param_grads, input_grad = pullback(jnp.float32(1.0))
        grad_sums = jax.tree.map(jnp.add, grad_sums, param_grads)
        return ((grad_sums, loss_sum + extras[1]), (extras[0].astype(jnp.bfloat16), input_grad.astype(jnp.bfloat16)))
    zero_grads = jax.tree.map(jnp.zeros_like, param_set)
    batches = (regroup(hidden), regroup(teacher), regroup(cotangent), regroup(valid_mask), regroup(blocks))
    (grad_sums, loss_value), (outputs_all, grads_all) = lax.scan(one_round, (zero_grads, jnp.float32(0.0)), batches)
    full_shape = (MICRO, SEQUENCES, SEQ, D)
    return (outputs_all.reshape(full_shape), loss_value, grads_all.reshape(full_shape), grad_sums[0], grad_sums[1], grad_sums[2], grad_sums[3], grad_sums[4], grad_sums[5], grad_sums[6], grad_sums[7], grad_sums[8], grad_sums[9])
```

```python
import functools
import jax
import jax.numpy as jnp
from jax import lax
from jax.experimental import pallas as pl
from jax.experimental.pallas import tpu as pltpu
from jax.sharding import PartitionSpec as P

EPS = 1e-06
NEG = -1000000000.0
HIGH = lax.Precision.HIGHEST


def times_rows(former, latter):
    return jnp.dot(former, latter, preferred_element_type=jnp.float32)


def times_transpose(former, latter):
    return lax.dot_general(
        former, latter, (((1,), (1,)), ((), ())), preferred_element_type=jnp.float32
    )


def over_tokens(former, latter):
    return lax.dot_general(
        former, latter, (((0,), (0,)), ((), ())), preferred_element_type=jnp.float32
    )


def assemble(gathered, fsdp_count, dp_count):
    row_block = gathered.shape[0] // (fsdp_count * dp_count)
    col_block = gathered.shape[1]
    shaped = gathered.reshape(fsdp_count, dp_count, row_block, col_block)
    return jnp.transpose(shaped, (0, 2, 1, 3)).reshape(fsdp_count * row_block, dp_count * col_block)


def disperse(gradient, fsdp_count, dp_count):
    row_block = gradient.shape[0] // fsdp_count
    col_block = gradient.shape[1] // dp_count
    shaped = gradient.reshape(fsdp_count, row_block, dp_count, col_block)
    return jnp.transpose(shaped, (0, 2, 1, 3)).reshape(fsdp_count * dp_count * row_block, col_block)


def norm_forward(inputs, norm_gain):
    row_scale = lax.rsqrt(jnp.mean(inputs * inputs, axis=-1, keepdims=True) + EPS)
    return (inputs * row_scale * norm_gain, row_scale)


def norm_backward(inputs, row_scale, norm_gain, upstream):
    scaled = upstream * norm_gain
    gain_grad = jnp.sum(upstream * inputs * row_scale, axis=0)
    mean_term = jnp.mean(scaled * inputs, axis=-1, keepdims=True)
    return (
        row_scale * scaled - inputs * (row_scale * row_scale * row_scale) * mean_term,
        gain_grad,
    )


def gelu_tanh(values_in):
    return jax.nn.gelu(values_in, approximate=True)


def masked_scores(queries, key_heads, position_bias, allowed):
    products = jnp.einsum("qhd,khd->hqk", queries, key_heads, preferred_element_type=jnp.float32)
    return jnp.where(allowed[None], products + position_bias, NEG)


def body(
    hidden,
    teacher,
    cotangent,
    valid_mask,
    blocks,
    buckets,
    first_gain,
    query_weight,
    key_weight,
    value_weight,
    output_weight,
    second_gain,
    gate_weight,
    up_weight,
    down_weight,
    bias_table,
):
    fsdp_count = lax.axis_size("fsdp")
    dp_count = lax.axis_size("dp")
    micro_count = hidden.shape[0]
    seq_len = hidden.shape[2]
    model_width = hidden.shape[3]
    bucket_count = bias_table.shape[0]
    head_count = bias_table.shape[1]
    scale_factor = jnp.float32(
        float(micro_count * lax.axis_size(("fsdp", "dp")) * hidden.shape[1] * seq_len * model_width)
    )
    valid_float = valid_mask.astype(jnp.float32)
    valid_total = lax.psum(jnp.sum(valid_float), ("fsdp", "dp"))
    places = lax.broadcasted_iota(jnp.int32, (1, 1, bucket_count), 2)
    onehot = (buckets[:, :, None] == places).astype(jnp.float32)
    position_bias = jnp.einsum(
        "qkb,bh->hqk", onehot, bias_table.astype(jnp.float32), precision=HIGH
    )
    onehot_low = onehot.astype(jnp.bfloat16)
    rows_iota = lax.broadcasted_iota(jnp.int32, (seq_len, seq_len), 0)
    cols_iota = lax.broadcasted_iota(jnp.int32, (seq_len, seq_len), 1)
    diagonal = rows_iota == cols_iota

    def rebuild(gathered):
        return (gathered[0],) + tuple(
            (assemble(matrix, fsdp_count, dp_count) for matrix in gathered[1:])
        )

    def spread_out(grads):
        return (
            (grads[0],)
            + tuple((disperse(matrix, fsdp_count, dp_count) for matrix in grads[1:5]))
            + (grads[5],)
            + tuple((disperse(matrix, fsdp_count, dp_count) for matrix in grads[6:]))
        )

    outputs_list = []
    input_grads = []
    squares = jnp.float32(0.0)
    table_grad = jnp.zeros((bucket_count, head_count), jnp.float32)
    totals = None
    for step_index in range(micro_count):
        inputs = hidden[step_index, 0].astype(jnp.float32)
        target = teacher[step_index, 0].astype(jnp.float32)
        upstream = cotangent[step_index, 0].astype(jnp.float32)
        token_valid = valid_float[step_index, 0]
        block_ids = blocks[step_index, 0]
        allowed = (block_ids[None, :] <= block_ids[:, None]) & (
            valid_mask[step_index, 0][None, :] == 1
        ) | diagonal
        first_block = rebuild(
            (
                lax.all_gather(first_gain, ("fsdp", "dp"), axis=0, tiled=True),
                lax.all_gather(query_weight, ("fsdp", "dp"), axis=0, tiled=True),
                lax.all_gather(key_weight, ("fsdp", "dp"), axis=0, tiled=True),
                lax.all_gather(value_weight, ("fsdp", "dp"), axis=0, tiled=True),
                lax.all_gather(output_weight, ("fsdp", "dp"), axis=0, tiled=True),
            )
        )
        gain_one = first_block[0].astype(jnp.float32)
        normed_full, scale_one = norm_forward(inputs, gain_one)
        normed_one = normed_full.astype(jnp.bfloat16)
        head_size = first_block[1].shape[1] // head_count
        head_split = (seq_len, head_count, head_size)
        queries = times_rows(normed_one, first_block[1]).astype(jnp.bfloat16).reshape(head_split)
        key_heads = times_rows(normed_one, first_block[2]).astype(jnp.bfloat16).reshape(head_split)
        value_heads = (
            times_rows(normed_one, first_block[3]).astype(jnp.bfloat16).reshape(head_split)
        )
        scores = masked_scores(queries, key_heads, position_bias, allowed)
        row_max = jnp.max(scores, axis=-1, keepdims=True)
        exponent = jnp.exp(scores - row_max)
        row_total = jnp.sum(exponent, axis=-1, keepdims=True)
        log_total = row_max + jnp.log(row_total)
        softmax_low = (exponent / row_total).astype(jnp.bfloat16)
        attended = jnp.einsum(
            "hqk,khd->qhd", softmax_low, value_heads, preferred_element_type=jnp.float32
        )
        attended = attended.astype(jnp.bfloat16).reshape(seq_len, head_count * head_size)
        middle = inputs + times_transpose(attended, first_block[4])
        second_block = rebuild(
            (
                lax.all_gather(second_gain, ("fsdp", "dp"), axis=0, tiled=True),
                lax.all_gather(gate_weight, ("fsdp", "dp"), axis=0, tiled=True),
                lax.all_gather(up_weight, ("fsdp", "dp"), axis=0, tiled=True),
                lax.all_gather(down_weight, ("fsdp", "dp"), axis=0, tiled=True),
            )
        )
        gain_two = second_block[0].astype(jnp.float32)
        normed_mid, scale_two = norm_forward(middle, gain_two)
        normed_two = normed_mid.astype(jnp.bfloat16)
        gate_pre = times_rows(normed_two, second_block[1])
        up_pre = times_rows(normed_two, second_block[2])
        gate_act, gelu_pullback = jax.vjp(gelu_tanh, gate_pre)
        hidden_act = (gate_act * up_pre).astype(jnp.bfloat16)
        layer_full = middle + times_transpose(hidden_act, second_block[3])
        outputs_list.append(layer_full.astype(jnp.bfloat16))
        residual_gap = layer_full - target
        weighted_gap = token_valid[:, None] * residual_gap
        squares = squares + jnp.sum(weighted_gap * residual_gap)
        grad_out = scale_factor * upstream + scale_factor * (
            2.0 * weighted_gap / (valid_total * model_width)
        )
        back_second = rebuild(
            (
                lax.all_gather(second_gain, ("fsdp", "dp"), axis=0, tiled=True),
                lax.all_gather(gate_weight, ("fsdp", "dp"), axis=0, tiled=True),
                lax.all_gather(up_weight, ("fsdp", "dp"), axis=0, tiled=True),
                lax.all_gather(down_weight, ("fsdp", "dp"), axis=0, tiled=True),
            )
        )
        grad_ffn = grad_out.astype(jnp.bfloat16)
        down_part = over_tokens(grad_ffn, hidden_act)
        grad_hidden_act = times_rows(grad_ffn, back_second[3])
        grad_gate = gelu_pullback(grad_hidden_act * up_pre)[0].astype(jnp.bfloat16)
        grad_up = (grad_hidden_act * gate_act).astype(jnp.bfloat16)
        gate_part = over_tokens(normed_two, grad_gate)
        up_part = over_tokens(normed_two, grad_up)
        grad_normed_two = times_transpose(grad_gate, back_second[1]) + times_transpose(
            grad_up, back_second[2]
        )
        middle_term, gain_two_part = norm_backward(
            middle, scale_two, back_second[0].astype(jnp.float32), grad_normed_two
        )
        grad_middle = grad_out + middle_term
        grad_attn = grad_middle.astype(jnp.bfloat16)
        back_first = rebuild(
            (
                lax.all_gather(first_gain, ("fsdp", "dp"), axis=0, tiled=True),
                lax.all_gather(query_weight, ("fsdp", "dp"), axis=0, tiled=True),
                lax.all_gather(key_weight, ("fsdp", "dp"), axis=0, tiled=True),
                lax.all_gather(value_weight, ("fsdp", "dp"), axis=0, tiled=True),
                lax.all_gather(output_weight, ("fsdp", "dp"), axis=0, tiled=True),
            )
        )
        output_part = over_tokens(grad_attn, attended)
        grad_attended = (
            times_rows(grad_attn, back_first[4]).astype(jnp.bfloat16).reshape(head_split)
        )
        scores_again = masked_scores(queries, key_heads, position_bias, allowed)
        softmax_again = jnp.exp(scores_again - log_total)
        grad_probs = jnp.einsum(
            "qhd,khd->hqk", grad_attended, value_heads, preferred_element_type=jnp.float32
        )
        grad_scores = softmax_again * (
            grad_probs - jnp.sum(softmax_again * grad_probs, axis=-1, keepdims=True)
        )
        grad_scores = grad_scores.astype(jnp.bfloat16)
        table_grad = table_grad + jnp.einsum(
            "hqk,qkb->bh", grad_scores, onehot_low, preferred_element_type=jnp.float32
        )
        flat_width = head_count * head_size
        grad_queries = (
            jnp.einsum("hqk,khd->qhd", grad_scores, key_heads, preferred_element_type=jnp.float32)
            .astype(jnp.bfloat16)
            .reshape(seq_len, flat_width)
        )
        grad_keys = (
            jnp.einsum("hqk,qhd->khd", grad_scores, queries, preferred_element_type=jnp.float32)
            .astype(jnp.bfloat16)
            .reshape(seq_len, flat_width)
        )
        grad_values = (
            jnp.einsum(
                "hqk,qhd->khd",
                softmax_again.astype(jnp.bfloat16),
                grad_attended,
                preferred_element_type=jnp.float32,
            )
            .astype(jnp.bfloat16)
            .reshape(seq_len, flat_width)
        )
        query_part = over_tokens(normed_one, grad_queries)
        key_part = over_tokens(normed_one, grad_keys)
        value_part = over_tokens(normed_one, grad_values)
        grad_normed_one = (
            times_transpose(grad_queries, back_first[1])
            + times_transpose(grad_keys, back_first[2])
            + times_transpose(grad_values, back_first[3])
        )
        input_term, gain_one_part = norm_backward(
            inputs, scale_one, back_first[0].astype(jnp.float32), grad_normed_one
        )
        input_grads.append((grad_middle + input_term).astype(jnp.bfloat16))
        step_set = spread_out(
            (
                gain_one_part,
                query_part,
                key_part,
                value_part,
                output_part,
                gain_two_part,
                gate_part,
                up_part,
                down_part,
            )
        )
        totals = step_set if totals is None else jax.tree.map(jnp.add, totals, step_set)
    shards = (
        lax.psum_scatter(totals[0], ("fsdp", "dp"), scatter_dimension=0, tiled=True),
        lax.psum_scatter(totals[1], ("fsdp", "dp"), scatter_dimension=0, tiled=True),
        lax.psum_scatter(totals[2], ("fsdp", "dp"), scatter_dimension=0, tiled=True),
        lax.psum_scatter(totals[3], ("fsdp", "dp"), scatter_dimension=0, tiled=True),
        lax.psum_scatter(totals[4], ("fsdp", "dp"), scatter_dimension=0, tiled=True),
        lax.psum_scatter(totals[5], ("fsdp", "dp"), scatter_dimension=0, tiled=True),
        lax.psum_scatter(totals[6], ("fsdp", "dp"), scatter_dimension=0, tiled=True),
        lax.psum_scatter(totals[7], ("fsdp", "dp"), scatter_dimension=0, tiled=True),
        lax.psum_scatter(totals[8], ("fsdp", "dp"), scatter_dimension=0, tiled=True),
    )
    total_squares, table_all = lax.psum((squares, table_grad), ("fsdp", "dp"))
    loss_value = total_squares / (valid_total * model_width)
    layer_output = jnp.stack(outputs_list)[:, None]
    hidden_grad = jnp.stack(input_grads)[:, None]
    return (
        layer_output,
        loss_value,
        hidden_grad,
        shards[0],
        shards[1],
        shards[2],
        shards[3],
        shards[4],
        shards[5],
        shards[6],
        shards[7],
        shards[8],
        table_all,
    )


MESH_ID = pl.DeviceIdType.MESH
LANES = 768
ROWS = 192


def place():
    f = lax.axis_index("fsdp")
    d = lax.axis_index("dp")
    return f // 2, f % 2, d // 2, d % 2


def device(z, x, y, c):
    return (z * 2 + x, y * 2 + c)


def start_barrier():
    f = lax.axis_index("fsdp")
    d = lax.axis_index("dp")
    barrier = pltpu.get_barrier_semaphore()

    def tell(step, carry):
        other = (f * 4 + d + step) % 32
        pl.semaphore_signal(
            barrier, inc=1, device_id=(other // 4, other % 4), device_id_type=MESH_ID
        )
        return carry

    lax.fori_loop(1, 32, tell, 0)
    pl.semaphore_wait(barrier, 31)


def exchange(tile_of, table, send, recv):
    f = lax.axis_index("fsdp")
    d = lax.axis_index("dp")
    me = f * 4 + d

    def one(step, carry):
        other = (me + step) % 32
        pltpu.make_async_remote_copy(
            tile_of(other), table.at[me], send, recv,
            device_id=(other // 4, other % 4), device_id_type=MESH_ID,
        ).start()
        return carry

    lax.fori_loop(1, 32, one, 0)
    view = table.at[pl.ds(0, 31)]
    return pltpu.make_async_remote_copy(
        view, view, send, recv, device_id=(f, (d + 1) % 4), device_id_type=MESH_ID
    )


def lanes_of(pack):
    return pl.ds(pl.multiple_of(pack * LANES, 128), LANES)


def rows_of(z, x, first, count):
    return pl.ds(pl.multiple_of((z * 2 + x) * ROWS + first, 32), count)


G_Z, G_X0, G_Y0, G_XZ, G_YZ, G_DY, G_DX = 0, 3, 4, 5, 8, 11, 15
G_XA, G_XB, G_YA, G_YB, G_C = 19, 22, 25, 28, 31
G_COUNT = 47
G_ROWS = (
    [192] * 3 + [192, 192] + [32] * 6 + [96] * 8 + [64] * 3 + [96] * 3 + [64] * 3 + [96] * 3 + [192] * 16
)


class Gather:
    def __init__(self, own, whole, send, recv, packs):
        self.own, self.whole, self.send, self.recv, self.packs = own, whole, send, recv, packs
        self.z, self.x, self.y, self.c = place()

    def put(self, pack, slot, shard, first, count, target, own=False):
        zz, xx, yy = shard
        there = self.whole.at[yy * 2 + self.c, rows_of(zz, xx, first, count), lanes_of(pack)]
        here = self.own.at[pl.ds(first, count), lanes_of(pack)] if own else there
        pltpu.make_async_remote_copy(
            here, there, self.send.at[pack, slot], self.recv.at[pack, slot],
            device_id=device(*target), device_id_type=MESH_ID,
        ).start()

    def some(self, pack, slot):
        count = G_ROWS[slot]
        view = self.whole.at[0, pl.ds(0, count), lanes_of(pack)]
        return pltpu.make_async_remote_copy(
            view, view, self.send.at[pack, slot], self.recv.at[pack, slot],
            device_id=device(self.z, self.x, self.y, 1 - self.c), device_id_type=MESH_ID,
        )

    def got(self, pack, slot):
        self.some(pack, slot).wait_recv()

    def launch(self, pack):
        z, x, y, c = self.z, self.x, self.y, self.c
        for k in (1, 2, 3):
            self.put(pack, G_Z + k - 1, (z, x, y), 0, 192, ((z + k) % 4, x, y, c), own=True)

    def first(self, pack, k):
        z, x, y, c = self.z, self.x, self.y, self.c
        xn, yn, cn = (z, 1 - x, y, c), (z, x, 1 - y, c), (z, x, y, 1 - c)
        zz = (z - k + 4) % 4
        mine = (zz, x, y)
        if k == 0:
            self.put(pack, G_X0, mine, 0, 192, xn, own=True)
            self.put(pack, G_Y0, mine, 0, 192, yn, own=True)
            self.put(pack, G_C, mine, 0, 192, cn, own=True)
        else:
            self.got(pack, G_Z + k - 1)
            self.put(pack, G_XA + k - 1, mine, 0, 64, xn)
            self.put(pack, G_YA + k - 1, mine, 128, 64, yn)
            self.put(pack, G_XB + k - 1, mine, 96, 96, xn)
            self.put(pack, G_YB + k - 1, mine, 0, 96, yn)
            self.put(pack, G_C + 4 * k, mine, 0, 192, cn)

    def second(self, pack, k):
        z, x, y, c = self.z, self.x, self.y, self.c
        xn, yn, cn = (z, 1 - x, y, c), (z, x, 1 - y, c), (z, x, y, 1 - c)
        zz = (z - k + 4) % 4
        across_x, across_y = (zz, 1 - x, y), (zz, x, 1 - y)
        if k == 0:
            self.got(pack, G_X0)
            for j in (1, 2, 3):
                self.put(pack, G_XZ + j - 1, across_x, 64, 32, ((z + j) % 4, x, y, c))
            self.put(pack, G_DY, across_x, 0, 96, yn)
            self.put(pack, G_C + 1, across_x, 0, 192, cn)
            self.got(pack, G_Y0)
            for j in (1, 2, 3):
                self.put(pack, G_YZ + j - 1, across_y, 96, 32, ((z + j) % 4, x, y, c))
            self.put(pack, G_DX, across_y, 96, 96, xn)
            self.put(pack, G_C + 2, across_y, 0, 192, cn)
        else:
            self.got(pack, G_XZ + k - 1)
            self.got(pack, G_XA + k - 1)
            self.put(pack, G_DY + k, across_x, 0, 96, yn)
            self.got(pack, G_YZ + k - 1)
            self.got(pack, G_YA + k - 1)
            self.put(pack, G_DX + k, across_y, 96, 96, xn)
            self.got(pack, G_XB + k - 1)
            self.put(pack, G_C + 4 * k + 1, across_x, 0, 192, cn)
            self.got(pack, G_YB + k - 1)
            self.put(pack, G_C + 4 * k + 2, across_y, 0, 192, cn)

    def third(self, pack, k):
        z, x, y, c = self.z, self.x, self.y, self.c
        zz = (z - k + 4) % 4
        self.got(pack, G_DY + k)
        self.got(pack, G_DX + k)
        self.put(pack, G_C + 4 * k + 3, (zz, 1 - x, 1 - y), 0, 192, (z, x, y, 1 - c))

    def step(self, pack, k):
        self.first(pack, k)
        if k == 3:
            pl.when(pack + 1 < self.packs)(lambda: self.launch(pack + 1))
        if k >= 1:
            self.second(pack, k - 1)
        else:
            pl.when(pack >= 1)(lambda: self.second(pack - 1, 3))
        if k >= 2:
            self.third(pack, k - 2)
        else:
            pl.when(pack >= 1)(lambda: self.third(pack - 1, k + 2))

    def drain(self):
        last = self.packs - 1
        self.second(last, 3)
        self.third(last, 2)
        self.third(last, 3)

    def arrived(self, pack):
        for slot in range(G_C, G_C + 16):
            self.got(pack, slot)

    def finish(self):
        def one(pack, carry):
            for slot in range(G_COUNT):
                self.some(pack, slot).wait_send()
            return carry
        lax.fori_loop(0, self.packs, one, 0)


def gather_kernel(packs, own, tile, whole, table, send, recv, local, tile_send, tile_recv, tile_local):
    f = lax.axis_index("fsdp")
    d = lax.axis_index("dp")
    start_barrier()
    tiles = exchange(lambda other: tile, table, tile_send, tile_recv)
    tile_keep = pltpu.make_async_copy(tile, table.at[f * 4 + d], tile_local)
    tile_keep.start()
    g = Gather(own, whole, send, recv, packs)
    keep = pltpu.make_async_copy(
        own, whole.at[d, pl.ds(pl.multiple_of(f * ROWS, ROWS), ROWS)], local
    )
    g.launch(0)
    keep.start()

    def one(pack, carry):
        for k in range(4):
            g.step(pack, k)
        return carry

    lax.fori_loop(0, packs, one, 0)
    g.drain()
    lax.fori_loop(0, packs, lambda p, s: (g.arrived(p), s)[1], 0)
    g.finish()
    keep.wait()
    tiles.wait()
    tile_keep.wait()


def gather(own, tile):
    packs = own.shape[1] // LANES
    return pl.pallas_call(
        functools.partial(gather_kernel, packs),
        out_shape=(
            jax.ShapeDtypeStruct((4, 8 * ROWS, own.shape[1]), own.dtype),
            jax.ShapeDtypeStruct((32, 8, 128), jnp.float32),
        ),
        in_specs=[pl.BlockSpec(memory_space=pl.ANY)] * 2,
        out_specs=[pl.BlockSpec(memory_space=pl.ANY)] * 2,
        scratch_shapes=[
            pltpu.SemaphoreType.DMA((packs, G_COUNT)),
            pltpu.SemaphoreType.DMA((packs, G_COUNT)),
        ] + [pltpu.SemaphoreType.DMA] * 4,
        compiler_params=pltpu.CompilerParams(collective_id=1, has_side_effects=True),
    )(own, tile)


R_C, R_V, R_U, R_ZC, R_Z, R_F = 0, 16, 32, 38, 44, 47
R_COUNT = 49
R_ROWS = [192] * 16 + [96] * 16 + [64] * 6 + [32] * 6 + [192] * 3 + [96] * 2
ORDER = (1, 2, 3, 0)
TILE = 32


def add_rows(into, what, count):
    def one(t, carry):
        r = pl.ds(pl.multiple_of(t * TILE, TILE), TILE)
        into[r] = (into[r].astype(jnp.float32) + what[r].astype(jnp.float32)).astype(into.dtype)
        return carry
    lax.fori_loop(0, count // TILE, one, 0)


class Scatter:
    def __init__(self, part, out, mine, buf_c, buf_v, buf_u, buf_zc, buf_z, buf_f, send, recv, load, credit, packs):
        self.part, self.out, self.mine = part, out, mine
        self.buf_c, self.buf_v, self.buf_u, self.buf_zc, self.buf_z, self.buf_f = buf_c, buf_v, buf_u, buf_zc, buf_z, buf_f
        self.send, self.recv, self.load, self.credit, self.packs = send, recv, load, credit, packs
        self.z, self.x, self.y, self.c = place()
        z, x, y, c = place()
        self.xn, self.yn, self.cn = (z, 1 - x, y, c), (z, x, 1 - y, c), (z, x, y, 1 - c)

    def at(self, par, shard, first, count):
        zz, xx, yy = shard
        return self.mine.at[par, yy, rows_of(zz, xx, first, count)]

    def put(self, par, slot, here, there, target):
        pltpu.make_async_remote_copy(
            here, there, self.send.at[par, slot], self.recv.at[par, slot],
            device_id=device(*target), device_id_type=MESH_ID,
        ).start()

    def some(self, par, slot):
        view = self.mine.at[par, 0, pl.ds(0, R_ROWS[slot])]
        return pltpu.make_async_remote_copy(
            view, view, self.send.at[par, slot], self.recv.at[par, slot],
            device_id=device(*self.cn), device_id_type=MESH_ID,
        )

    def got(self, par, slot):
        self.some(par, slot).wait_recv()

    def shards(self, k):
        zz = (self.z + k) % 4
        return ((zz, 1 - self.x, 1 - self.y), (zz, self.x, 1 - self.y), (zz, 1 - self.x, self.y), (zz, self.x, self.y))

    def loads(self, pack):
        par = pack % 2
        return [
            pltpu.make_async_copy(
                self.part.at[yy * 2 + self.c, :, lanes_of(pack)], self.mine.at[par, yy], self.load.at[yy]
            )
            for yy in range(2)
        ]

    def launch(self, pack):
        par = pack % 2
        pl.when(pack >= 2)(lambda: pl.semaphore_wait(self.credit.at[pack - 2], 6))
        for r in self.loads(pack):
            r.start()
        for k in ORDER:
            for i, (zz, xx, yy) in enumerate(self.shards(k)):
                rows = rows_of(zz, xx, 0, 192)
                self.put(
                    par, R_C + 4 * k + i,
                    self.part.at[yy * 2 + 1 - self.c, rows, lanes_of(pack)],
                    self.buf_c.at[par, yy, rows], self.cn,
                )

    def core(self, pack, k):
        par = pack % 2
        sh = self.shards(k)
        if k == ORDER[0]:
            for r in self.loads(pack):
                r.wait()
        for i, (zz, xx, yy) in enumerate(sh):
            self.got(par, R_C + 4 * k + i)
            add_rows(self.at(par, sh[i], 0, 192), self.buf_c.at[par, yy, rows_of(zz, xx, 0, 192)], 192)
        v = self.buf_v
        self.put(par, R_V + 4 * k, self.at(par, sh[0], 0, 96), v.at[par, k, 0], self.yn)
        self.put(par, R_V + 4 * k + 1, self.at(par, sh[0], 96, 96), v.at[par, k, 1], self.xn)
        self.put(par, R_V + 4 * k + 2, self.at(par, sh[1], 0, 96), v.at[par, k, 2], self.yn)
        self.put(par, R_V + 4 * k + 3, self.at(par, sh[2], 96, 96), v.at[par, k, 3], self.xn)

    def vees(self, pack, k):
        par = pack % 2
        sh = self.shards(k)
        zz = (self.z + k) % 4
        peer = (zz, self.x, self.y, self.c)
        v = self.buf_v
        self.got(par, R_V + 4 * k)
        add_rows(self.at(par, sh[2], 0, 96), v.at[par, k, 0], 96)
        if k:
            self.put(par, R_U + 2 * (k - 1), self.at(par, sh[2], 0, 64), self.buf_u.at[par, k - 1, 0], self.xn)
            self.put(par, R_ZC + 2 * (k - 1), self.at(par, sh[2], 64, 32), self.buf_zc.at[par, k - 1, 0], peer)
        self.got(par, R_V + 4 * k + 1)
        add_rows(self.at(par, sh[1], 96, 96), v.at[par, k, 1], 96)
        if k:
            self.put(par, R_U + 2 * (k - 1) + 1, self.at(par, sh[1], 128, 64), self.buf_u.at[par, k - 1, 1], self.yn)
            self.put(par, R_ZC + 2 * (k - 1) + 1, self.at(par, sh[1], 96, 32), self.buf_zc.at[par, k - 1, 1], peer)
            self.got(par, R_V + 4 * k + 2)
            add_rows(self.at(par, sh[3], 0, 96), v.at[par, k, 2], 96)
            self.got(par, R_V + 4 * k + 3)
            add_rows(self.at(par, sh[3], 96, 96), v.at[par, k, 3], 96)

    def yous(self, pack, k):
        par = pack % 2
        sh = self.shards(k)
        peer = ((self.z + k) % 4, self.x, self.y, self.c)
        self.got(par, R_U + 2 * (k - 1))
        add_rows(self.at(par, sh[3], 0, 64), self.buf_u.at[par, k - 1, 0], 64)
        self.got(par, R_U + 2 * (k - 1) + 1)
        add_rows(self.at(par, sh[3], 128, 64), self.buf_u.at[par, k - 1, 1], 64)
        self.put(par, R_Z + k - 1, self.at(par, sh[3], 0, 192), self.buf_z.at[par, k - 1], peer)

    def near(self, pack):
        par = pack % 2
        sh = self.shards(0)
        for j, (shard, first, whole, nb) in enumerate(((sh[2], 64, 0, self.xn), (sh[1], 96, 96, self.yn))):
            for k in range(3):
                self.got(par, R_ZC + 2 * k + j)
            into = self.at(par, shard, first, 32)
            b = self.buf_zc
            into[...] = (
                into[...].astype(jnp.float32)
                + b[par, 0, j].astype(jnp.float32)
                + b[par, 1, j].astype(jnp.float32)
                + b[par, 2, j].astype(jnp.float32)
            ).astype(into.dtype)
            self.put(par, R_F + j, self.at(par, shard, whole, 96), self.buf_f.at[par, j], nb)

    def final(self, pack):
        par = pack % 2
        own = self.at(par, self.shards(0)[3], 0, 192)
        self.got(par, R_V + 2)
        self.got(par, R_V + 3)
        for k in range(3):
            self.got(par, R_Z + k)
        for j in range(2):
            self.got(par, R_F + j)
        for j in range(2):
            def one(t, carry, j=j):
                r = pl.ds(pl.multiple_of(t * TILE, TILE), TILE)
                rr = pl.ds(pl.multiple_of(j * 96 + t * TILE, TILE), TILE)
                total = own[rr].astype(jnp.float32) + self.buf_v[par, 0, 2 + j, r].astype(jnp.float32)
                total = total + self.buf_f[par, j, r].astype(jnp.float32)
                for k in range(3):
                    total = total + self.buf_z[par, k, rr].astype(jnp.float32)
                self.out[rr, lanes_of(pack)] = total
                return carry
            lax.fori_loop(0, 96 // TILE, one, 0)
        for slot in range(R_COUNT):
            self.some(par, slot).wait_send()

        @pl.when(pack + 2 < self.packs)
        def _():
            z, x, y, c = self.z, self.x, self.y, self.c
            for t in (self.xn, self.yn, self.cn) + tuple(((z + k) % 4, x, y, c) for k in (1, 2, 3)):
                pl.semaphore_signal(self.credit.at[pack], inc=1, device_id=device(*t), device_id_type=MESH_ID)

    def step(self, pack, r):
        self.core(pack, ORDER[r])
        if r == 0:
            @pl.when(pack >= 1)
            def _():
                self.vees(pack - 1, ORDER[3])
                self.yous(pack - 1, ORDER[2])
                self.near(pack - 1)
        else:
            self.vees(pack, ORDER[r - 1])
        if r == 1:
            pl.when(pack >= 1)(lambda: self.final(pack - 1))
        if r == 2:
            pl.when(pack + 1 < self.packs)(lambda: self.launch(pack + 1))
        if r >= 2:
            self.yous(pack, ORDER[r - 2])

    def drain(self):
        last = self.packs - 1
        self.vees(last, ORDER[3])
        self.yous(last, ORDER[2])
        self.near(last)
        self.final(last)


def scatter_scratch(packs):
    bf = jnp.bfloat16
    return [
        pltpu.VMEM((2, 2, 8 * ROWS, LANES), bf),
        pltpu.VMEM((2, 2, 8 * ROWS, LANES), bf),
        pltpu.VMEM((2, 4, 4, 96, LANES), bf),
        pltpu.VMEM((2, 3, 2, 64, LANES), bf),
        pltpu.VMEM((2, 3, 2, 32, LANES), bf),
        pltpu.VMEM((2, 3, 192, LANES), bf),
        pltpu.VMEM((2, 2, 96, LANES), bf),
        pltpu.SemaphoreType.DMA((2, R_COUNT)),
        pltpu.SemaphoreType.DMA((2, R_COUNT)),
        pltpu.SemaphoreType.DMA((2,)),
        pltpu.SemaphoreType.REGULAR((packs,)),
    ]


def scatter_kernel(packs, part, tile, out, table, tile_send, tile_recv, tile_local, *scratch):
    start_barrier()
    me = lax.axis_index("fsdp") * 4 + lax.axis_index("dp")
    tiles = exchange(lambda other: tile.at[other], table, tile_send, tile_recv)
    tile_keep = pltpu.make_async_copy(tile.at[me], table.at[me], tile_local)
    tile_keep.start()
    s = Scatter(part, out, *scratch, packs)
    s.launch(0)

    def one(pack, carry):
        for r in range(4):
            s.step(pack, r)
        return carry

    lax.fori_loop(0, packs, one, 0)
    s.drain()
    tiles.wait()
    tile_keep.wait()


def scatter(part, tile):
    packs = part.shape[2] // LANES
    return pl.pallas_call(
        functools.partial(scatter_kernel, packs),
        out_shape=(
            jax.ShapeDtypeStruct((ROWS, part.shape[2]), jnp.float32),
            jax.ShapeDtypeStruct((32, 8, 128), jnp.float32),
        ),
        in_specs=[pl.BlockSpec(memory_space=pl.ANY)] * 2,
        out_specs=[pl.BlockSpec(memory_space=pltpu.VMEM), pl.BlockSpec(memory_space=pl.ANY)],
        scratch_shapes=[pltpu.SemaphoreType.DMA] * 3 + scatter_scratch(packs),
        compiler_params=pltpu.CompilerParams(
            collective_id=2, has_side_effects=True, vmem_limit_bytes=60 * 1024 * 1024
        ),
    )(part, tile)


BF = jnp.bfloat16
F32 = jnp.float32


def tuned_body(
    hidden, teacher, cotangent, valid_mask, blocks, buckets, first_gain, query_weight, key_weight, value_weight,
    output_weight, second_gain, gate_weight, up_weight, down_weight, bias_table,
):
    micro, _, seq, width = hidden.shape
    tokens = micro * seq
    cols = query_weight.shape[1]
    part = gate_weight.shape[1]
    wide = -(-part // 128) * 128
    bucket_count, heads = bias_table.shape
    scale = F32(float(tokens * 32 * width))

    def pad(m):
        return jnp.pad(m, ((0, 0), (0, wide - part)))

    own = jnp.concatenate(
        [query_weight, key_weight, value_weight, output_weight, pad(gate_weight), pad(up_weight), pad(down_weight)], axis=1
    )
    valid = valid_mask.reshape(tokens).astype(F32)
    per = first_gain.shape[0]
    tile = jnp.zeros((8, 128), F32)
    tile = tile.at[0, :per].set(first_gain.astype(F32)).at[1, :per].set(second_gain.astype(F32))
    tile = tile.at[2, 0].set(jnp.sum(valid))
    packs, table = gather(own, tile)
    gain_one = table[:, 0, :per].reshape(width)
    gain_two = table[:, 1, :per].reshape(width)
    valid_total = jnp.sum(table[:, 2, 0])
    dp = packs.shape[0]

    def piece(d, name):
        first, count = {"q": (0, cols), "k": (cols, cols), "v": (2 * cols, cols), "o": (3 * cols, cols),
                        "gate": (4 * cols, wide), "up": (4 * cols + wide, wide), "down": (4 * cols + 2 * wide, wide)}[name]
        return lax.slice(packs, (d, 0, first), (d + 1, width, first + count))[0]

    x = hidden.reshape(tokens, width).astype(F32)
    target = teacher.reshape(tokens, width).astype(F32)
    upstream = cotangent.reshape(tokens, width).astype(F32)
    places = lax.broadcasted_iota(jnp.int32, (1, 1, bucket_count), 2)
    onehot = (buckets[:, :, None] == places).astype(F32)
    position_bias = jnp.einsum("qkb,bh->hqk", onehot, bias_table.astype(F32), precision=HIGH)
    onehot_low = onehot.astype(BF)
    diagonal = lax.broadcasted_iota(jnp.int32, (seq, seq), 0) == lax.broadcasted_iota(jnp.int32, (seq, seq), 1)
    block_ids = blocks.reshape(micro, seq)
    allowed = (block_ids[:, None, :] <= block_ids[:, :, None]) & (valid_mask.reshape(micro, seq)[:, None, :] == 1) | diagonal
    normed_full, scale_one = norm_forward(x, gain_one)
    normed_one = normed_full.astype(BF)
    per_dp = heads // dp
    head = cols // per_dp

    def heads_of(name):
        return jnp.stack([times_rows(normed_one, piece(d, name)).astype(BF) for d in range(dp)], axis=1).reshape(micro, seq, heads, head)

    queries, key_heads, value_heads = heads_of("q"), heads_of("k"), heads_of("v")

    def masked(queries, key_heads):
        products = jnp.einsum("mqhd,mkhd->mhqk", queries, key_heads, preferred_element_type=F32)
        return jnp.where(allowed[:, None], products + position_bias[None], NEG)

    scores = masked(queries, key_heads)
    row_max = jnp.max(scores, axis=-1, keepdims=True)
    exponent = jnp.exp(scores - row_max)
    row_total = jnp.sum(exponent, axis=-1, keepdims=True)
    probs = exponent / row_total
    softmax_low = probs.astype(BF)
    attended = jnp.einsum("mhqk,mkhd->mqhd", softmax_low, value_heads, preferred_element_type=F32).astype(BF)
    attended = attended.reshape(tokens, dp, cols)
    middle = x
    for d in range(dp):
        middle = middle + times_transpose(attended[:, d], piece(d, "o"))
    normed_mid, scale_two = norm_forward(middle, gain_two)
    normed_two = normed_mid.astype(BF)
    gate_pre = [times_rows(normed_two, piece(d, "gate")) for d in range(dp)]
    up_pre = [times_rows(normed_two, piece(d, "up")) for d in range(dp)]
    acts = [jax.vjp(gelu_tanh, g) for g in gate_pre]
    hidden_act = [(a[0] * u).astype(BF) for a, u in zip(acts, up_pre)]
    layer_full = middle
    for d in range(dp):
        layer_full = layer_full + times_transpose(hidden_act[d], piece(d, "down"))
    gap = layer_full - target
    weighted = valid[:, None] * gap
    squares = jnp.sum(weighted * gap)
    grad_out = scale * upstream + scale * (2.0 * weighted / (valid_total * width))
    grad_ffn = grad_out.astype(BF)
    pieces = [[None] * 7 for _ in range(dp)]
    grad_normed_two = jnp.zeros((tokens, width), F32)
    for d in range(dp):
        pieces[d][6] = over_tokens(grad_ffn, hidden_act[d]).astype(BF)
        grad_hidden = times_rows(grad_ffn, piece(d, "down"))
        grad_gate = acts[d][1](grad_hidden * up_pre[d])[0].astype(BF)
        grad_up = (grad_hidden * acts[d][0]).astype(BF)
        pieces[d][4] = over_tokens(normed_two, grad_gate).astype(BF)
        pieces[d][5] = over_tokens(normed_two, grad_up).astype(BF)
        grad_normed_two = grad_normed_two + times_transpose(grad_gate, piece(d, "gate")) + times_transpose(grad_up, piece(d, "up"))
    middle_term, gain_two_part = norm_backward(middle, scale_two, gain_two, grad_normed_two)
    grad_middle = grad_out + middle_term
    grad_attn = grad_middle.astype(BF)
    grad_attended = []
    for d in range(dp):
        pieces[d][3] = over_tokens(grad_attn, attended[:, d]).astype(BF)
        grad_attended.append(times_rows(grad_attn, piece(d, "o")).astype(BF))
    grad_attended = jnp.stack(grad_attended, axis=1).reshape(micro, seq, heads, head)
    grad_probs = jnp.einsum("mqhd,mkhd->mhqk", grad_attended, value_heads, preferred_element_type=F32)
    grad_scores = (probs * (grad_probs - jnp.sum(probs * grad_probs, axis=-1, keepdims=True))).astype(BF)
    table_part = jnp.einsum("mhqk,qkb->bh", grad_scores, onehot_low, preferred_element_type=F32)
    grads = (
        jnp.einsum("mhqk,mkhd->mqhd", grad_scores, key_heads, preferred_element_type=F32),
        jnp.einsum("mhqk,mqhd->mkhd", grad_scores, queries, preferred_element_type=F32),
        jnp.einsum("mhqk,mqhd->mkhd", softmax_low, grad_attended, preferred_element_type=F32),
    )
    grad_normed_one = jnp.zeros((tokens, width), F32)
    for i, (name, g) in enumerate(zip("qkv", grads)):
        g = g.astype(BF).reshape(tokens, dp, cols)
        for d in range(dp):
            pieces[d][i] = over_tokens(normed_one, g[:, d]).astype(BF)
            grad_normed_one = grad_normed_one + times_transpose(g[:, d], piece(d, name))
    input_term, gain_one_part = norm_backward(x, scale_one, gain_one, grad_normed_one)
    hidden_grad = (grad_middle + input_term).astype(BF)
    partial = jnp.stack([jnp.concatenate(pieces[d], axis=1) for d in range(dp)])
    tiles = jnp.zeros((32, 8, 128), F32)
    tiles = tiles.at[:, 0, :per].set(gain_one_part.reshape(32, per)).at[:, 1, :per].set(gain_two_part.reshape(32, per))
    lines = bucket_count * heads // 128
    tiles = tiles.at[:, 3:3 + lines].set(table_part.reshape(1, lines, 128)).at[:, 2, 0].set(squares)
    shard, sums = scatter(partial, tiles)
    sums = jnp.sum(sums, axis=0)
    cuts = (0, cols, 2 * cols, 3 * cols, 4 * cols, 4 * cols + wide, 4 * cols + 2 * wide)
    sizes = (cols,) * 4 + (part,) * 3
    grad = [shard[:, a:a + s] for a, s in zip(cuts, sizes)]
    return (
        layer_full.astype(BF).reshape(hidden.shape),
        sums[2, 0] / (valid_total * width),
        hidden_grad.reshape(hidden.shape),
        sums[0, :per], grad[0], grad[1], grad[2], grad[3], sums[1, :per], grad[4], grad[5], grad[6],
        sums[3:3 + lines].reshape(bucket_count, heads),
    )

def solution(mesh):
    in_specs = (
        P(None, ("fsdp", "dp"), None, None),
        P(None, ("fsdp", "dp"), None, None),
        P(None, ("fsdp", "dp"), None, None),
        P(None, ("fsdp", "dp"), None),
        P(None, ("fsdp", "dp"), None),
        P(),
        P(("fsdp", "dp")),
        P("fsdp", "dp"),
        P("fsdp", "dp"),
        P("fsdp", "dp"),
        P("fsdp", "dp"),
        P(("fsdp", "dp")),
        P("fsdp", "dp"),
        P("fsdp", "dp"),
        P("fsdp", "dp"),
        P(),
    )
    out_specs = (
        P(None, ("fsdp", "dp"), None, None),
        P(),
        P(None, ("fsdp", "dp"), None, None),
        P(("fsdp", "dp")),
        P("fsdp", "dp"),
        P("fsdp", "dp"),
        P("fsdp", "dp"),
        P("fsdp", "dp"),
        P(("fsdp", "dp")),
        P("fsdp", "dp"),
        P("fsdp", "dp"),
        P("fsdp", "dp"),
        P(),
    )
    chosen = tuned_body if dict(mesh.shape) == {"fsdp": 8, "dp": 4} else body
    return jax.shard_map(chosen, mesh=mesh, in_specs=in_specs, out_specs=out_specs, check_vma=False)
```

```python
import functools
import jax
import jax.numpy as jnp
from jax import lax
from jax.experimental import pallas as pl
from jax.experimental.pallas import tpu as pltpu
from jax.sharding import PartitionSpec as P

EPS = 1e-06
NEG = -1000000000.0
HIGH = lax.Precision.HIGHEST


def times_rows(former, latter):
    return jnp.dot(former, latter, preferred_element_type=jnp.float32)


def times_transpose(former, latter):
    return lax.dot_general(
        former, latter, (((1,), (1,)), ((), ())), preferred_element_type=jnp.float32
    )


def over_tokens(former, latter):
    return lax.dot_general(
        former, latter, (((0,), (0,)), ((), ())), preferred_element_type=jnp.float32
    )


def assemble(gathered, fsdp_count, dp_count):
    row_block = gathered.shape[0] // (fsdp_count * dp_count)
    col_block = gathered.shape[1]
    shaped = gathered.reshape(fsdp_count, dp_count, row_block, col_block)
    return jnp.transpose(shaped, (0, 2, 1, 3)).reshape(fsdp_count * row_block, dp_count * col_block)


def disperse(gradient, fsdp_count, dp_count):
    row_block = gradient.shape[0] // fsdp_count
    col_block = gradient.shape[1] // dp_count
    shaped = gradient.reshape(fsdp_count, row_block, dp_count, col_block)
    return jnp.transpose(shaped, (0, 2, 1, 3)).reshape(fsdp_count * dp_count * row_block, col_block)


def norm_forward(inputs, norm_gain):
    row_scale = lax.rsqrt(jnp.mean(inputs * inputs, axis=-1, keepdims=True) + EPS)
    return (inputs * row_scale * norm_gain, row_scale)


def norm_backward(inputs, row_scale, norm_gain, upstream):
    scaled = upstream * norm_gain
    gain_grad = jnp.sum(upstream * inputs * row_scale, axis=0)
    mean_term = jnp.mean(scaled * inputs, axis=-1, keepdims=True)
    return (
        row_scale * scaled - inputs * (row_scale * row_scale * row_scale) * mean_term,
        gain_grad,
    )


def gelu_tanh(values_in):
    return jax.nn.gelu(values_in, approximate=True)


def masked_scores(queries, key_heads, position_bias, allowed):
    products = jnp.einsum("qhd,khd->hqk", queries, key_heads, preferred_element_type=jnp.float32)
    return jnp.where(allowed[None], products + position_bias, NEG)


def body(
    hidden,
    teacher,
    cotangent,
    valid_mask,
    blocks,
    buckets,
    first_gain,
    query_weight,
    key_weight,
    value_weight,
    output_weight,
    second_gain,
    gate_weight,
    up_weight,
    down_weight,
    bias_table,
):
    fsdp_count = lax.axis_size("fsdp")
    dp_count = lax.axis_size("dp")
    micro_count = hidden.shape[0]
    seq_len = hidden.shape[2]
    model_width = hidden.shape[3]
    bucket_count = bias_table.shape[0]
    head_count = bias_table.shape[1]
    scale_factor = jnp.float32(
        float(micro_count * lax.axis_size(("fsdp", "dp")) * hidden.shape[1] * seq_len * model_width)
    )
    valid_float = valid_mask.astype(jnp.float32)
    valid_total = lax.psum(jnp.sum(valid_float), ("fsdp", "dp"))
    places = lax.broadcasted_iota(jnp.int32, (1, 1, bucket_count), 2)
    onehot = (buckets[:, :, None] == places).astype(jnp.float32)
    position_bias = jnp.einsum(
        "qkb,bh->hqk", onehot, bias_table.astype(jnp.float32), precision=HIGH
    )
    onehot_low = onehot.astype(jnp.bfloat16)
    rows_iota = lax.broadcasted_iota(jnp.int32, (seq_len, seq_len), 0)
    cols_iota = lax.broadcasted_iota(jnp.int32, (seq_len, seq_len), 1)
    diagonal = rows_iota == cols_iota

    def rebuild(gathered):
        return (gathered[0],) + tuple(
            (assemble(matrix, fsdp_count, dp_count) for matrix in gathered[1:])
        )

    def spread_out(grads):
        return (
            (grads[0],)
            + tuple((disperse(matrix, fsdp_count, dp_count) for matrix in grads[1:5]))
            + (grads[5],)
            + tuple((disperse(matrix, fsdp_count, dp_count) for matrix in grads[6:]))
        )

    outputs_list = []
    input_grads = []
    squares = jnp.float32(0.0)
    table_grad = jnp.zeros((bucket_count, head_count), jnp.float32)
    totals = None
    for step_index in range(micro_count):
        inputs = hidden[step_index, 0].astype(jnp.float32)
        target = teacher[step_index, 0].astype(jnp.float32)
        upstream = cotangent[step_index, 0].astype(jnp.float32)
        token_valid = valid_float[step_index, 0]
        block_ids = blocks[step_index, 0]
        allowed = (block_ids[None, :] <= block_ids[:, None]) & (
            valid_mask[step_index, 0][None, :] == 1
        ) | diagonal
        first_block = rebuild(
            (
                lax.all_gather(first_gain, ("fsdp", "dp"), axis=0, tiled=True),
                lax.all_gather(query_weight, ("fsdp", "dp"), axis=0, tiled=True),
                lax.all_gather(key_weight, ("fsdp", "dp"), axis=0, tiled=True),
                lax.all_gather(value_weight, ("fsdp", "dp"), axis=0, tiled=True),
                lax.all_gather(output_weight, ("fsdp", "dp"), axis=0, tiled=True),
            )
        )
        gain_one = first_block[0].astype(jnp.float32)
        normed_full, scale_one = norm_forward(inputs, gain_one)
        normed_one = normed_full.astype(jnp.bfloat16)
        head_size = first_block[1].shape[1] // head_count
        head_split = (seq_len, head_count, head_size)
        queries = times_rows(normed_one, first_block[1]).astype(jnp.bfloat16).reshape(head_split)
        key_heads = times_rows(normed_one, first_block[2]).astype(jnp.bfloat16).reshape(head_split)
        value_heads = (
            times_rows(normed_one, first_block[3]).astype(jnp.bfloat16).reshape(head_split)
        )
        scores = masked_scores(queries, key_heads, position_bias, allowed)
        row_max = jnp.max(scores, axis=-1, keepdims=True)
        exponent = jnp.exp(scores - row_max)
        row_total = jnp.sum(exponent, axis=-1, keepdims=True)
        log_total = row_max + jnp.log(row_total)
        softmax_low = (exponent / row_total).astype(jnp.bfloat16)
        attended = jnp.einsum(
            "hqk,khd->qhd", softmax_low, value_heads, preferred_element_type=jnp.float32
        )
        attended = attended.astype(jnp.bfloat16).reshape(seq_len, head_count * head_size)
        middle = inputs + times_transpose(attended, first_block[4])
        second_block = rebuild(
            (
                lax.all_gather(second_gain, ("fsdp", "dp"), axis=0, tiled=True),
                lax.all_gather(gate_weight, ("fsdp", "dp"), axis=0, tiled=True),
                lax.all_gather(up_weight, ("fsdp", "dp"), axis=0, tiled=True),
                lax.all_gather(down_weight, ("fsdp", "dp"), axis=0, tiled=True),
            )
        )
        gain_two = second_block[0].astype(jnp.float32)
        normed_mid, scale_two = norm_forward(middle, gain_two)
        normed_two = normed_mid.astype(jnp.bfloat16)
        gate_pre = times_rows(normed_two, second_block[1])
        up_pre = times_rows(normed_two, second_block[2])
        gate_act, gelu_pullback = jax.vjp(gelu_tanh, gate_pre)
        hidden_act = (gate_act * up_pre).astype(jnp.bfloat16)
        layer_full = middle + times_transpose(hidden_act, second_block[3])
        outputs_list.append(layer_full.astype(jnp.bfloat16))
        residual_gap = layer_full - target
        weighted_gap = token_valid[:, None] * residual_gap
        squares = squares + jnp.sum(weighted_gap * residual_gap)
        grad_out = scale_factor * upstream + scale_factor * (
            2.0 * weighted_gap / (valid_total * model_width)
        )
        back_second = rebuild(
            (
                lax.all_gather(second_gain, ("fsdp", "dp"), axis=0, tiled=True),
                lax.all_gather(gate_weight, ("fsdp", "dp"), axis=0, tiled=True),
                lax.all_gather(up_weight, ("fsdp", "dp"), axis=0, tiled=True),
                lax.all_gather(down_weight, ("fsdp", "dp"), axis=0, tiled=True),
            )
        )
        grad_ffn = grad_out.astype(jnp.bfloat16)
        down_part = over_tokens(grad_ffn, hidden_act)
        grad_hidden_act = times_rows(grad_ffn, back_second[3])
        grad_gate = gelu_pullback(grad_hidden_act * up_pre)[0].astype(jnp.bfloat16)
        grad_up = (grad_hidden_act * gate_act).astype(jnp.bfloat16)
        gate_part = over_tokens(normed_two, grad_gate)
        up_part = over_tokens(normed_two, grad_up)
        grad_normed_two = times_transpose(grad_gate, back_second[1]) + times_transpose(
            grad_up, back_second[2]
        )
        middle_term, gain_two_part = norm_backward(
            middle, scale_two, back_second[0].astype(jnp.float32), grad_normed_two
        )
        grad_middle = grad_out + middle_term
        grad_attn = grad_middle.astype(jnp.bfloat16)
        back_first = rebuild(
            (
                lax.all_gather(first_gain, ("fsdp", "dp"), axis=0, tiled=True),
                lax.all_gather(query_weight, ("fsdp", "dp"), axis=0, tiled=True),
                lax.all_gather(key_weight, ("fsdp", "dp"), axis=0, tiled=True),
                lax.all_gather(value_weight, ("fsdp", "dp"), axis=0, tiled=True),
                lax.all_gather(output_weight, ("fsdp", "dp"), axis=0, tiled=True),
            )
        )
        output_part = over_tokens(grad_attn, attended)
        grad_attended = (
            times_rows(grad_attn, back_first[4]).astype(jnp.bfloat16).reshape(head_split)
        )
        scores_again = masked_scores(queries, key_heads, position_bias, allowed)
        softmax_again = jnp.exp(scores_again - log_total)
        grad_probs = jnp.einsum(
            "qhd,khd->hqk", grad_attended, value_heads, preferred_element_type=jnp.float32
        )
        grad_scores = softmax_again * (
            grad_probs - jnp.sum(softmax_again * grad_probs, axis=-1, keepdims=True)
        )
        grad_scores = grad_scores.astype(jnp.bfloat16)
        table_grad = table_grad + jnp.einsum(
            "hqk,qkb->bh", grad_scores, onehot_low, preferred_element_type=jnp.float32
        )
        flat_width = head_count * head_size
        grad_queries = (
            jnp.einsum("hqk,khd->qhd", grad_scores, key_heads, preferred_element_type=jnp.float32)
            .astype(jnp.bfloat16)
            .reshape(seq_len, flat_width)
        )
        grad_keys = (
            jnp.einsum("hqk,qhd->khd", grad_scores, queries, preferred_element_type=jnp.float32)
            .astype(jnp.bfloat16)
            .reshape(seq_len, flat_width)
        )
        grad_values = (
            jnp.einsum(
                "hqk,qhd->khd",
                softmax_again.astype(jnp.bfloat16),
                grad_attended,
                preferred_element_type=jnp.float32,
            )
            .astype(jnp.bfloat16)
            .reshape(seq_len, flat_width)
        )
        query_part = over_tokens(normed_one, grad_queries)
        key_part = over_tokens(normed_one, grad_keys)
        value_part = over_tokens(normed_one, grad_values)
        grad_normed_one = (
            times_transpose(grad_queries, back_first[1])
            + times_transpose(grad_keys, back_first[2])
            + times_transpose(grad_values, back_first[3])
        )
        input_term, gain_one_part = norm_backward(
            inputs, scale_one, back_first[0].astype(jnp.float32), grad_normed_one
        )
        input_grads.append((grad_middle + input_term).astype(jnp.bfloat16))
        step_set = spread_out(
            (
                gain_one_part,
                query_part,
                key_part,
                value_part,
                output_part,
                gain_two_part,
                gate_part,
                up_part,
                down_part,
            )
        )
        totals = step_set if totals is None else jax.tree.map(jnp.add, totals, step_set)
    shards = (
        lax.psum_scatter(totals[0], ("fsdp", "dp"), scatter_dimension=0, tiled=True),
        lax.psum_scatter(totals[1], ("fsdp", "dp"), scatter_dimension=0, tiled=True),
        lax.psum_scatter(totals[2], ("fsdp", "dp"), scatter_dimension=0, tiled=True),
        lax.psum_scatter(totals[3], ("fsdp", "dp"), scatter_dimension=0, tiled=True),
        lax.psum_scatter(totals[4], ("fsdp", "dp"), scatter_dimension=0, tiled=True),
        lax.psum_scatter(totals[5], ("fsdp", "dp"), scatter_dimension=0, tiled=True),
        lax.psum_scatter(totals[6], ("fsdp", "dp"), scatter_dimension=0, tiled=True),
        lax.psum_scatter(totals[7], ("fsdp", "dp"), scatter_dimension=0, tiled=True),
        lax.psum_scatter(totals[8], ("fsdp", "dp"), scatter_dimension=0, tiled=True),
    )
    total_squares, table_all = lax.psum((squares, table_grad), ("fsdp", "dp"))
    loss_value = total_squares / (valid_total * model_width)
    layer_output = jnp.stack(outputs_list)[:, None]
    hidden_grad = jnp.stack(input_grads)[:, None]
    return (
        layer_output,
        loss_value,
        hidden_grad,
        shards[0],
        shards[1],
        shards[2],
        shards[3],
        shards[4],
        shards[5],
        shards[6],
        shards[7],
        shards[8],
        table_all,
    )


MESH_ID = pl.DeviceIdType.MESH
LANES = 768
ROWS = 192


def place():
    f = lax.axis_index("fsdp")
    d = lax.axis_index("dp")
    return f // 2, f % 2, d // 2, d % 2


def device(z, x, y, c):
    return (z * 2 + x, y * 2 + c)


def start_barrier():
    f = lax.axis_index("fsdp")
    d = lax.axis_index("dp")
    barrier = pltpu.get_barrier_semaphore()

    def tell(step, carry):
        other = (f * 4 + d + step) % 32
        pl.semaphore_signal(
            barrier, inc=1, device_id=(other // 4, other % 4), device_id_type=MESH_ID
        )
        return carry

    lax.fori_loop(1, 32, tell, 0)
    pl.semaphore_wait(barrier, 31)


def exchange(tile_of, table, send, recv):
    f = lax.axis_index("fsdp")
    d = lax.axis_index("dp")
    me = f * 4 + d

    def one(step, carry):
        other = (me + step) % 32
        pltpu.make_async_remote_copy(
            tile_of(other), table.at[me], send, recv,
            device_id=(other // 4, other % 4), device_id_type=MESH_ID,
        ).start()
        return carry

    lax.fori_loop(1, 32, one, 0)
    view = table.at[pl.ds(0, 31)]
    return pltpu.make_async_remote_copy(
        view, view, send, recv, device_id=(f, (d + 1) % 4), device_id_type=MESH_ID
    )


def lanes_of(pack):
    return pl.ds(pl.multiple_of(pack * LANES, 128), LANES)


def rows_of(z, x, first, count):
    return pl.ds(pl.multiple_of((z * 2 + x) * ROWS + first, 32), count)


G_Z, G_X0, G_Y0, G_XZ, G_YZ, G_DY, G_DX = 0, 3, 4, 5, 8, 11, 15
G_XA, G_XB, G_YA, G_YB, G_C = 19, 22, 25, 28, 31
G_COUNT = 47
G_ROWS = (
    [192] * 3 + [192, 192] + [32] * 6 + [96] * 8 + [64] * 3 + [96] * 3 + [64] * 3 + [96] * 3 + [192] * 16
)


class Gather:
    def __init__(self, own, whole, send, recv, packs):
        self.own, self.whole, self.send, self.recv, self.packs = own, whole, send, recv, packs
        self.z, self.x, self.y, self.c = place()

    def put(self, pack, slot, shard, first, count, target, own=False):
        zz, xx, yy = shard
        there = self.whole.at[yy * 2 + self.c, rows_of(zz, xx, first, count), lanes_of(pack)]
        here = self.own.at[pl.ds(first, count), lanes_of(pack)] if own else there
        pltpu.make_async_remote_copy(
            here, there, self.send.at[pack, slot], self.recv.at[pack, slot],
            device_id=device(*target), device_id_type=MESH_ID,
        ).start()

    def some(self, pack, slot, count):
        view = self.whole.at[0, pl.ds(0, count), lanes_of(pack)]
        return pltpu.make_async_remote_copy(
            view, view, self.send.at[pack, slot], self.recv.at[pack, slot],
            device_id=device(self.z, self.x, self.y, 1 - self.c), device_id_type=MESH_ID,
        )

    def got(self, pack, slot, count):
        self.some(pack, slot, count).wait_recv()

    def launch(self, pack):
        z, x, y, c = self.z, self.x, self.y, self.c
        for k in (1, 2, 3):
            self.put(pack, G_Z + k - 1, (z, x, y), 0, 192, ((z + k) % 4, x, y, c), own=True)

    def first(self, pack, k):
        z, x, y, c = self.z, self.x, self.y, self.c
        xn, yn, cn = (z, 1 - x, y, c), (z, x, 1 - y, c), (z, x, y, 1 - c)
        mine = ((z - k + 4) % 4, x, y)

        @pl.when(k == 0)
        def _():
            self.put(pack, G_X0, (z, x, y), 0, 192, xn, own=True)
            self.put(pack, G_Y0, (z, x, y), 0, 192, yn, own=True)
            self.put(pack, G_C, (z, x, y), 0, 192, cn, own=True)

        @pl.when(k > 0)
        def _():
            self.got(pack, G_Z + k - 1, 192)
            self.put(pack, G_XA + k - 1, mine, 0, 64, xn)
            self.put(pack, G_YA + k - 1, mine, 128, 64, yn)
            self.put(pack, G_XB + k - 1, mine, 96, 96, xn)
            self.put(pack, G_YB + k - 1, mine, 0, 96, yn)
            self.put(pack, G_C + 4 * k, mine, 0, 192, cn)

    def second(self, pack, k):
        z, x, y, c = self.z, self.x, self.y, self.c
        xn, yn, cn = (z, 1 - x, y, c), (z, x, 1 - y, c), (z, x, y, 1 - c)
        zz = (z - k + 4) % 4
        across_x, across_y = (zz, 1 - x, y), (zz, x, 1 - y)

        @pl.when(k == 0)
        def _():
            self.got(pack, G_X0, 192)
            for j in (1, 2, 3):
                self.put(pack, G_XZ + j - 1, (z, 1 - x, y), 64, 32, ((z + j) % 4, x, y, c))
            self.put(pack, G_DY, (z, 1 - x, y), 0, 96, yn)
            self.put(pack, G_C + 1, (z, 1 - x, y), 0, 192, cn)
            self.got(pack, G_Y0, 192)
            for j in (1, 2, 3):
                self.put(pack, G_YZ + j - 1, (z, x, 1 - y), 96, 32, ((z + j) % 4, x, y, c))
            self.put(pack, G_DX, (z, x, 1 - y), 96, 96, xn)
            self.put(pack, G_C + 2, (z, x, 1 - y), 0, 192, cn)

        @pl.when(k > 0)
        def _():
            self.got(pack, G_XZ + k - 1, 32)
            self.got(pack, G_XA + k - 1, 64)
            self.put(pack, G_DY + k, across_x, 0, 96, yn)
            self.got(pack, G_YZ + k - 1, 32)
            self.got(pack, G_YA + k - 1, 64)
            self.put(pack, G_DX + k, across_y, 96, 96, xn)
            self.got(pack, G_XB + k - 1, 96)
            self.put(pack, G_C + 4 * k + 1, across_x, 0, 192, cn)
            self.got(pack, G_YB + k - 1, 96)
            self.put(pack, G_C + 4 * k + 2, across_y, 0, 192, cn)

    def third(self, pack, k):
        z, x, y, c = self.z, self.x, self.y, self.c
        zz = (z - k + 4) % 4
        self.got(pack, G_DY + k, 96)
        self.got(pack, G_DX + k, 96)
        self.put(pack, G_C + 4 * k + 3, (zz, 1 - x, 1 - y), 0, 192, (z, x, y, 1 - c))

    def step(self, s):
        total = 4 * self.packs

        @pl.when(s < total)
        def _():
            self.first(s // 4, s % 4)
            pl.when((s % 4 == 3) & (s + 1 < total))(lambda: self.launch(s // 4 + 1))

        pl.when((s >= 1) & (s <= total))(lambda: self.second((s + 3) // 4 - 1, (s + 3) % 4))
        pl.when((s >= 2) & (s <= total + 1))(lambda: self.third((s + 2) // 4 - 1, (s + 2) % 4))

    def arrived(self, pack):
        for slot in range(G_C, G_C + 16):
            self.got(pack, slot, 192)

    def finish(self):
        def one(pack, carry):
            for slot in range(G_COUNT):
                self.some(pack, slot, G_ROWS[slot]).wait_send()
            return carry
        lax.fori_loop(0, self.packs, one, 0)


R_C, R_V, R_U, R_ZC, R_Z, R_F = 0, 16, 32, 38, 44, 47
R_COUNT = 49
R_ROWS = [192] * 16 + [96] * 16 + [64] * 6 + [32] * 6 + [192] * 3 + [96] * 2
ORDER = (1, 2, 3, 0)
TILE = 32


def add_rows(into, what, count):
    def one(t, carry):
        r = pl.ds(pl.multiple_of(t * TILE, TILE), TILE)
        into[r] = (into[r].astype(jnp.float32) + what[r].astype(jnp.float32)).astype(into.dtype)
        return carry
    lax.fori_loop(0, count // TILE, one, 0)


class Scatter:
    def __init__(self, part, out, mine, buf_c, buf_v, buf_u, buf_zc, buf_z, buf_f, send, recv, load, credit, stage, out_sem, packs):
        self.stage, self.out_sem = stage, out_sem
        self.part, self.out, self.mine = part, out, mine
        self.buf_c, self.buf_v, self.buf_u, self.buf_zc, self.buf_z, self.buf_f = buf_c, buf_v, buf_u, buf_zc, buf_z, buf_f
        self.send, self.recv, self.load, self.credit, self.packs = send, recv, load, credit, packs
        self.z, self.x, self.y, self.c = place()
        z, x, y, c = place()
        self.xn, self.yn, self.cn = (z, 1 - x, y, c), (z, x, 1 - y, c), (z, x, y, 1 - c)

    def at(self, par, shard, first, count):
        zz, xx, yy = shard
        return self.mine.at[par, yy, rows_of(zz, xx, first, count)]

    def put(self, par, slot, here, there, target):
        pltpu.make_async_remote_copy(
            here, there, self.send.at[par, slot], self.recv.at[par, slot],
            device_id=device(*target), device_id_type=MESH_ID,
        ).start()

    def some(self, par, slot, count):
        view = self.mine.at[par, 0, pl.ds(0, count)]
        return pltpu.make_async_remote_copy(
            view, view, self.send.at[par, slot], self.recv.at[par, slot],
            device_id=device(*self.cn), device_id_type=MESH_ID,
        )

    def got(self, par, slot, count):
        self.some(par, slot, count).wait_recv()

    def lane_pack(self, pack):
        return (pack + 1) % self.packs

    def shards(self, k):
        zz = (self.z + k) % 4
        return ((zz, 1 - self.x, 1 - self.y), (zz, self.x, 1 - self.y), (zz, 1 - self.x, self.y), (zz, self.x, self.y))

    def loads(self, pack):
        par = pack % 2
        return [
            pltpu.make_async_copy(
                self.part.at[yy * 2 + self.c, :, lanes_of(self.lane_pack(pack))], self.mine.at[par, yy], self.load.at[yy]
            )
            for yy in range(2)
        ]

    def launch(self, pack):
        par = pack % 2
        pl.when(pack >= 2)(lambda: pl.semaphore_wait(self.credit.at[pack - 2], 6))
        for r in self.loads(pack):
            r.start()
        for k in ORDER:
            for i, (zz, xx, yy) in enumerate(self.shards(k)):
                rows = rows_of(zz, xx, 0, 192)
                self.put(
                    par, R_C + 4 * k + i,
                    self.part.at[yy * 2 + 1 - self.c, rows, lanes_of(self.lane_pack(pack))],
                    self.buf_c.at[par, yy, rows], self.cn,
                )

    def core(self, pack, k):
        par = pack % 2
        sh = self.shards(k)

        @pl.when(k == ORDER[0])
        def _():
            for r in self.loads(pack):
                r.wait()

        for i, (zz, xx, yy) in enumerate(sh):
            self.got(par, R_C + 4 * k + i, 192)
            add_rows(self.at(par, sh[i], 0, 192), self.buf_c.at[par, yy, rows_of(zz, xx, 0, 192)], 192)
        v = self.buf_v
        self.put(par, R_V + 4 * k, self.at(par, sh[0], 0, 96), v.at[par, k, 0], self.yn)
        self.put(par, R_V + 4 * k + 1, self.at(par, sh[0], 96, 96), v.at[par, k, 1], self.xn)
        self.put(par, R_V + 4 * k + 2, self.at(par, sh[1], 0, 96), v.at[par, k, 2], self.yn)
        self.put(par, R_V + 4 * k + 3, self.at(par, sh[2], 96, 96), v.at[par, k, 3], self.xn)

    def vees(self, pack, k):
        par = pack % 2
        sh = self.shards(k)
        peer = ((self.z + k) % 4, self.x, self.y, self.c)
        v = self.buf_v
        self.got(par, R_V + 4 * k, 96)
        add_rows(self.at(par, sh[2], 0, 96), v.at[par, k, 0], 96)

        @pl.when(k > 0)
        def _():
            self.put(par, R_U + 2 * (k - 1), self.at(par, sh[2], 0, 64), self.buf_u.at[par, k - 1, 0], self.xn)
            self.put(par, R_ZC + 2 * (k - 1), self.at(par, sh[2], 64, 32), self.buf_zc.at[par, k - 1, 0], peer)

        self.got(par, R_V + 4 * k + 1, 96)
        add_rows(self.at(par, sh[1], 96, 96), v.at[par, k, 1], 96)

        @pl.when(k > 0)
        def _():
            self.put(par, R_U + 2 * (k - 1) + 1, self.at(par, sh[1], 128, 64), self.buf_u.at[par, k - 1, 1], self.yn)
            self.put(par, R_ZC + 2 * (k - 1) + 1, self.at(par, sh[1], 96, 32), self.buf_zc.at[par, k - 1, 1], peer)
            self.got(par, R_V + 4 * k + 2, 96)
            add_rows(self.at(par, sh[3], 0, 96), v.at[par, k, 2], 96)
            self.got(par, R_V + 4 * k + 3, 96)
            add_rows(self.at(par, sh[3], 96, 96), v.at[par, k, 3], 96)

    def yous(self, pack, k):
        par = pack % 2
        sh = self.shards(k)
        peer = ((self.z + k) % 4, self.x, self.y, self.c)
        self.got(par, R_U + 2 * (k - 1), 64)
        add_rows(self.at(par, sh[3], 0, 64), self.buf_u.at[par, k - 1, 0], 64)
        self.got(par, R_U + 2 * (k - 1) + 1, 64)
        add_rows(self.at(par, sh[3], 128, 64), self.buf_u.at[par, k - 1, 1], 64)
        self.put(par, R_Z + k - 1, self.at(par, sh[3], 0, 192), self.buf_z.at[par, k - 1], peer)

    def near(self, pack):
        par = pack % 2
        sh = self.shards(0)
        for j, (shard, first, whole, nb) in enumerate(((sh[2], 64, 0, self.xn), (sh[1], 96, 96, self.yn))):
            for k in range(3):
                self.got(par, R_ZC + 2 * k + j, 32)
            into = self.at(par, shard, first, 32)
            b = self.buf_zc
            into[...] = (
                into[...].astype(jnp.float32)
                + b[par, 0, j].astype(jnp.float32)
                + b[par, 1, j].astype(jnp.float32)
                + b[par, 2, j].astype(jnp.float32)
            ).astype(into.dtype)
            self.put(par, R_F + j, self.at(par, shard, whole, 96), self.buf_f.at[par, j], nb)

    def out_copy(self, pack):
        return pltpu.make_async_copy(self.stage, self.out.at[:, lanes_of(self.lane_pack(pack))], self.out_sem)

    def final(self, pack):
        par = pack % 2
        own = self.at(par, self.shards(0)[3], 0, 192)
        self.got(par, R_V + 2, 96)
        self.got(par, R_V + 3, 96)
        for k in range(3):
            self.got(par, R_Z + k, 192)
        for j in range(2):
            self.got(par, R_F + j, 96)
        pl.when(pack > 0)(lambda: self.out_copy(pack).wait())
        for j in range(2):
            def one(t, carry, j=j):
                r = pl.ds(pl.multiple_of(t * TILE, TILE), TILE)
                rr = pl.ds(pl.multiple_of(j * 96 + t * TILE, TILE), TILE)
                total = own[rr].astype(jnp.float32) + self.buf_v[par, 0, 2 + j, r].astype(jnp.float32)
                total = total + self.buf_f[par, j, r].astype(jnp.float32)
                for k in range(3):
                    total = total + self.buf_z[par, k, rr].astype(jnp.float32)
                self.stage[rr] = total
                return carry
            lax.fori_loop(0, 96 // TILE, one, 0)
        self.out_copy(pack).start()
        for slot in range(R_COUNT):
            self.some(par, slot, R_ROWS[slot]).wait_send()

        @pl.when(pack + 2 < self.packs)
        def _():
            z, x, y, c = self.z, self.x, self.y, self.c
            for t in (self.xn, self.yn, self.cn) + tuple(((z + k) % 4, x, y, c) for k in (1, 2, 3)):
                pl.semaphore_signal(self.credit.at[pack], inc=1, device_id=device(*t), device_id_type=MESH_ID)

    def step(self, s):
        total = 4 * self.packs
        pl.when(s < total)(lambda: self.core(s // 4, (s % 4 + 1) % 4))

        @pl.when((s >= 1) & (s <= total))
        def _():
            self.vees((s + 3) // 4 - 1, s % 4)

        @pl.when((s >= 2) & (s <= total + 1))
        def _():
            before = (s + 2) // 4 - 1
            k = (s + 3) % 4
            pl.when(k > 0)(lambda: self.yous(before, k))
            pl.when(k == 0)(lambda: self.final(before))

        pl.when((s >= 4) & (s % 4 == 0))(lambda: self.near(s // 4 - 1))
        pl.when((s % 4 == 2) & (s // 4 + 1 < self.packs))(lambda: self.launch(s // 4 + 1))

    def finish(self):
        self.out_copy(self.packs - 1).wait()


def scatter_scratch(packs):
    bf = jnp.bfloat16
    return [
        pltpu.VMEM((2, 2, 8 * ROWS, LANES), bf),
        pltpu.VMEM((2, 2, 8 * ROWS, LANES), bf),
        pltpu.VMEM((2, 4, 4, 96, LANES), bf),
        pltpu.VMEM((2, 3, 2, 64, LANES), bf),
        pltpu.VMEM((2, 3, 2, 32, LANES), bf),
        pltpu.VMEM((2, 3, 192, LANES), bf),
        pltpu.VMEM((2, 2, 96, LANES), bf),
        pltpu.SemaphoreType.DMA((2, R_COUNT)),
        pltpu.SemaphoreType.DMA((2, R_COUNT)),
        pltpu.SemaphoreType.DMA((2,)),
        pltpu.SemaphoreType.REGULAR((packs,)),
        pltpu.VMEM((ROWS, LANES), jnp.float32),
        pltpu.SemaphoreType.DMA,
    ]


BF = jnp.bfloat16
F32 = jnp.float32
CHUNK = 256


def gain_rows(table, line, into):
    lines = [None] * 13
    for i in range(32):
        first = (48 * i) // 128
        for j in range(2):
            got = table[i, line + j : line + j + 1, :]
            lines[first + j] = got if lines[first + j] is None else lines[first + j] + got
    for r in range(12):
        into[:, 128 * r : 128 * (r + 1)] = lines[r]


def loop(count, body):
    def one(t, carry):
        body(t)
        return carry

    lax.fori_loop(0, count, one, 0)


def tile_rows(t, size):
    return pl.ds(pl.multiple_of(t * size, size), size)


def norm_rows(src, gain, into, tokens):
    def one(t):
        r = tile_rows(t, 32)
        v = src[r].astype(F32)
        scale = lax.rsqrt(jnp.mean(v * v, axis=-1, keepdims=True) + EPS)
        into[r] = (v * scale * gain[...]).astype(BF)

    loop(tokens // 32, one)


def gelu_parts(u):
    root = 0.7978845608028654
    t = jnp.tanh(root * (u + 0.044715 * (u * u * u)))
    return 0.5 * u * (1.0 + t), t


def nt(a, b):
    return lax.dot_general(a, b, (((1,), (1,)), ((), ())), preferred_element_type=F32)


def tn(a, b):
    return lax.dot_general(a, b, (((0,), (0,)), ((), ())), preferred_element_type=F32)


def nn(a, b):
    return jnp.dot(a, b, preferred_element_type=F32)


def forward_kernel(
    packs, tokens, width, seq, heads, scale,
    own, tile, x_any, teacher_any, cotangent_any, buckets, bias_smem, blocks_row, blocks_col, valid_row, valid_col,
    whole, table, n1_out, n2_out, qkv_out, probs_out, pre_out, act_out, middle_out, layer_out, grad_out, gffn_out, loss_out,
    x, n1, n2, acc, bias, mask, wbuf, qs, ps, pre, act, tabv, gain1, gain2, teach, cot, lossv,
    send, recv, local, tile_send, tile_recv, tile_local, in_sem, w_sem, p_sem, q_sem, pre_sem, act_sem, out_sem,
):
    f = lax.axis_index("fsdp")
    d = lax.axis_index("dp")
    micro = tokens // seq
    per = heads // 4
    size = 192 // per
    start_barrier()
    g = Gather(own, whole, send, recv, packs)
    g.launch(0)
    tiles = exchange(lambda other: tile, table, tile_send, tile_recv)
    tile_keep = pltpu.make_async_copy(tile, table.at[f * 4 + d], tile_local)
    tile_keep.start()
    bounce = [
        pltpu.make_async_copy(own.at[:, pl.ds(p * LANES, LANES)], wbuf.at[1, pl.ds(p * ROWS, ROWS)], local.at[p])
        for p in range(packs)
    ]
    keep = [
        pltpu.make_async_copy(
            wbuf.at[1, pl.ds(p * ROWS, ROWS)],
            whole.at[d, pl.ds(pl.multiple_of(f * ROWS, ROWS), ROWS), pl.ds(p * LANES, LANES)],
            local.at[p],
        )
        for p in range(packs)
    ]
    for r in bounce:
        r.start()
    load_x = pltpu.make_async_copy(x_any, x, in_sem.at[0])
    load_x.start()
    g.step(0)
    for a, b in zip(bounce, keep):
        a.wait()
        b.start()
    rows_i = lax.broadcasted_iota(jnp.int32, (seq, seq), 0)
    cols_i = lax.broadcasted_iota(jnp.int32, (seq, seq), 1)
    for m in range(micro):
        ok = (blocks_row[m : m + 1, :] <= blocks_col[m * seq : (m + 1) * seq, :]) & (valid_row[m : m + 1, :] == 1)
        mask[m] = jnp.where(ok | (rows_i == cols_i), 1.0, 0.0)

    def bias_tile(t):
        r = tile_rows(t, 8)
        b = buckets[r]
        totals = [jnp.zeros((8, seq), F32)] * heads
        for k in range(32):
            here = b == k
            totals = [jnp.where(here, bias_smem[k, h], v) for h, v in enumerate(totals)]
        for h in range(heads):
            bias[h, r] = totals[h]

    step_tiles = -(-(seq // 8) // 5)

    def early(s):
        def some(i):
            t = s * step_tiles + i
            pl.when(t < seq // 8)(lambda: bias_tile(t))

        loop(step_tiles, some)
        g.step(s + 1)

    loop(5, early)
    tile_keep.wait()
    tiles.wait()
    load_table = pltpu.make_async_copy(table, tabv, in_sem.at[1])
    load_table.start()
    load_x.wait()
    load_table.wait()
    gain_rows(tabv, 0, gain1)
    gain_rows(tabv, 2, gain2)
    load_t = pltpu.make_async_copy(teacher_any, teach, in_sem.at[2])
    load_t.start()
    load_c = pltpu.make_async_copy(cotangent_any, cot, in_sem.at[3])
    load_c.start()
    norm_rows(x, gain1, n1, tokens)

    def copy_x(t):
        r = tile_rows(t, 32)
        acc[r] = x[r].astype(F32)

    loop(tokens // 32, copy_x)
    n1_copy = pltpu.make_async_copy(n1, n1_out, out_sem.at[0])
    n1_copy.start()
    for r in keep:
        r.wait()
    g.arrived(0)

    def load_w(i, slot):
        return pltpu.make_async_copy(
            whole.at[i % 4, :, lanes_of(i // 4)], wbuf.at[slot], w_sem.at[slot]
        )

    load_w(0, 0).start()

    def probs_copy(dd, m, slot):
        return pltpu.make_async_copy(ps.at[slot], probs_out.at[dd * micro + m], p_sem.at[slot])

    def attention(dd):
        slot = dd % 2
        pl.when(dd < 3)(lambda: load_w(dd + 1, 1 - slot).start())
        load_w(dd, slot).wait()
        pl.when(dd > 0)(lambda: pltpu.make_async_copy(qs, qkv_out.at[dd], q_sem).wait())
        qs[:, 0:576] = nn(n1[...], wbuf[slot, :, 0:576]).astype(BF)
        g.step(6 + 2 * dd)
        for m in range(micro):
            r = slice(m * seq, (m + 1) * seq)
            pl.when(dd > 0)(lambda: probs_copy(dd, m, m).wait())
            for hh in range(per):
                a = hh * size
                s = nt(qs[r, a : a + size], qs[r, 192 + a : 192 + a + size]) + bias[dd * per + hh]
                s = jnp.where(mask[m] > 0.0, s, NEG)
                top = jnp.max(s, axis=-1, keepdims=True)
                e = jnp.exp(s - top)
                p = e * (1.0 / jnp.sum(e, axis=-1, keepdims=True))
                ps[m, hh] = p
                qs[r, 576 + a : 576 + a + size] = nn(p.astype(BF), qs[r, 384 + a : 384 + a + size]).astype(BF)
            probs_copy(dd, m, m).start()
        g.step(7 + 2 * dd)
        for m in range(micro):
            r = slice(m * seq, (m + 1) * seq)
            acc[r] += nt(qs[r, 576:768], wbuf[slot, :, 576:768])
        pltpu.make_async_copy(qs, qkv_out.at[dd], q_sem).start()

    loop(4, attention)
    pltpu.make_async_copy(qs, qkv_out.at[0], q_sem).wait()
    for m in range(micro):
        probs_copy(3, m, m).wait()
    mid_copy = pltpu.make_async_copy(acc, middle_out, out_sem.at[1])
    mid_copy.start()
    norm_rows(acc, gain2, n2, tokens)
    n2_copy = pltpu.make_async_copy(n2, n2_out, out_sem.at[2])
    n2_copy.start()
    mid_copy.wait()

    def pre_copy(t, slot):
        return pltpu.make_async_copy(pre.at[slot], pre_out.at[t], pre_sem.at[slot])

    def act_copy(t, slot):
        return pltpu.make_async_copy(act.at[slot], act_out.at[t], act_sem.at[slot])

    def feed(t):
        slot = t % 2

        @pl.when(t % 4 == 0)
        def _():
            g.arrived(1 + t // 4)
            load_w(4 + t, slot).start()

        pl.when(t % 4 < 3)(lambda: load_w(5 + t, 1 - slot).start())
        load_w(4 + t, slot).wait()

        @pl.when(t > 1)
        def _():
            pre_copy(t, slot).wait()
            act_copy(t, slot).wait()

        for m in range(micro):
            r = slice(m * seq, (m + 1) * seq)
            gu = nn(n2[r], wbuf[slot, :, 0 : 2 * CHUNK])
            pre[slot, r] = gu
            ge, _ = gelu_parts(gu[:, 0:CHUNK])
            act[slot, r] = (ge * gu[:, CHUNK:]).astype(BF)
        pre_copy(t, slot).start()
        act_copy(t, slot).start()

        @pl.when(t < 8)
        def _():
            pl.when(t % 2 == 0)(lambda: g.step(14 + t // 2))

        pl.when((t >= 8) & (t < 12))(lambda: g.step(10 + t))
        for m in range(micro):
            r = slice(m * seq, (m + 1) * seq)
            acc[r] += nt(act[slot, r], wbuf[slot, :, 2 * CHUNK :])

    loop(16, feed)
    load_t.wait()
    load_c.wait()
    n1_copy.wait()
    n2_copy.wait()
    for slot in range(2):
        pre_copy(14 + slot, slot).wait()
        act_copy(14 + slot, slot).wait()
    total = tabv[0, 4:5, 0:1]
    for i in range(1, 32):
        total = total + tabv[i, 4:5, 0:1]
    factor = (2.0 * scale / width) / total
    lossv[...] = jnp.zeros_like(lossv)

    def ends(t):
        r = tile_rows(t, 16)
        full = acc[r]
        gap = full - teach[r].astype(F32)
        weighted = valid_col[r] * gap
        grad = scale * cot[r].astype(F32) + factor * weighted
        acc[r] = grad
        x[r] = grad.astype(BF)
        n1[r] = full.astype(BF)
        lossv[...] += weighted * gap

    loop(tokens // 16, ends)
    copies = [
        pltpu.make_async_copy(n1, layer_out, out_sem.at[0]),
        pltpu.make_async_copy(acc, grad_out, out_sem.at[1]),
        pltpu.make_async_copy(x, gffn_out, out_sem.at[2]),
    ]
    for r in copies:
        r.start()
    loss_out[...] = jnp.zeros_like(loss_out) + jnp.sum(lossv[...])
    g.finish()
    for r in copies:
        r.wait()


def forward(own, tile, x, teacher, cotangent, buckets, bias_table, blocks_row, blocks_col, valid_row, valid_col, scale):
    packs = own.shape[1] // LANES
    tokens, width = x.shape
    seq = buckets.shape[0]
    heads = bias_table.shape[1]
    micro = tokens // seq
    any_ = pl.BlockSpec(memory_space=pl.ANY)
    vmem = pl.BlockSpec(memory_space=pltpu.VMEM)
    smem = pl.BlockSpec(memory_space=pltpu.SMEM)
    S = jax.ShapeDtypeStruct
    dma = pltpu.SemaphoreType.DMA
    outs = (
        S((4, 8 * ROWS, own.shape[1]), BF), S((32, 8, 128), F32), S((tokens, width), BF), S((tokens, width), BF),
        S((4, tokens, 768), BF), S((4 * micro, heads // 4, seq, seq), F32), S((16, tokens, 2 * CHUNK), F32),
        S((16, tokens, CHUNK), BF), S((tokens, width), F32), S((tokens, width), BF), S((tokens, width), F32), S((tokens, width), BF), S((8, 128), F32),
    )
    return pl.pallas_call(
        functools.partial(forward_kernel, packs, tokens, width, seq, heads, scale),
        out_shape=outs,
        in_specs=[any_] * 5 + [vmem, smem] + [vmem] * 4,
        out_specs=[any_] * 12 + [vmem],
        scratch_shapes=[
            pltpu.VMEM((tokens, width), BF), pltpu.VMEM((tokens, width), BF), pltpu.VMEM((tokens, width), BF),
            pltpu.VMEM((tokens, width), F32), pltpu.VMEM((heads, seq, seq), F32), pltpu.VMEM((micro, seq, seq), F32),
            pltpu.VMEM((2, 8 * ROWS, LANES), BF), pltpu.VMEM((tokens, 768), BF), pltpu.VMEM((micro, heads // 4, seq, seq), F32),
            pltpu.VMEM((2, tokens, 2 * CHUNK), F32), pltpu.VMEM((2, tokens, CHUNK), BF), pltpu.VMEM((32, 8, 128), F32),
            pltpu.VMEM((1, width), F32), pltpu.VMEM((1, width), F32), pltpu.VMEM((tokens, width), BF),
            pltpu.VMEM((tokens, width), BF), pltpu.VMEM((16, width), F32),
            dma((packs, G_COUNT)), dma((packs, G_COUNT)), dma((packs,)), dma, dma, dma, dma((4,)), dma((2,)), dma((2,)), dma,
            dma((2,)), dma((2,)), dma((3,)),
        ],
        compiler_params=pltpu.CompilerParams(collective_id=1, has_side_effects=True, vmem_limit_bytes=63 * 1024 * 1024),
    )(own, tile, x, teacher, cotangent, buckets, bias_table, blocks_row, blocks_col, valid_row, valid_col)


def prepare(weights, gain_one, gain_two, valid):
    part = weights[4].shape[1]
    pads = [jnp.pad(w, ((0, 0), (0, 4 * CHUNK - part))) for w in weights[4:]]
    pieces = list(weights[:4])
    for j in range(4):
        pieces += [w[:, j * CHUNK : (j + 1) * CHUNK] for w in pads]
    own = jnp.concatenate(pieces, axis=1)
    me = lax.axis_index("fsdp") * 4 + lax.axis_index("dp")
    first = (me * 48) % 128

    def lines(gain):
        return lax.dynamic_update_slice(jnp.zeros((256,), F32), gain.astype(F32), (first,)).reshape(2, 128)

    count = jnp.zeros((4, 128), F32) + jnp.sum(valid.astype(F32))
    return own, jnp.concatenate([lines(gain_one), lines(gain_two), count])


def gelu_slope(u, t):
    root = 0.7978845608028654
    return 0.5 * (1.0 + t) + 0.5 * u * (1.0 - t * t) * root * (1.0 + 3.0 * 0.044715 * (u * u))


def norm_back(src_row, up_row, gain, gain_sum):
    v, u = src_row, up_row
    scale = lax.rsqrt(jnp.mean(v * v, axis=-1, keepdims=True) + EPS)
    scaled = u * gain
    mean = jnp.mean(scaled * v, axis=-1, keepdims=True)
    term = u * v * scale
    total = term[0:8]
    for i in range(1, term.shape[0] // 8):
        total = total + term[8 * i : 8 * i + 8]
    gain_sum[...] += total
    return scale * scaled - v * (scale * scale * scale) * mean


def backward_kernel(
    packs, tokens, width, seq, heads,
    whole, table, x_any, n1_any, n2_any, qkv_any, probs_any, pre_any, act_any, mid_any, gout_any, gffn_any, buckets, loss,
    part, out, hidden_out, tiles_out, sums_out,
    low, src, acc, acc2, wbuf, pre, act, ggu, gst, strm, qs, ps, ga, gqkv, bsum, gain1, gain2, sum1, sum2, tilev, tabv,
    in_sem, w_sem, pre_sem, act_sem, g_sem, s_sem, q_sem, p_sem, out2_sem, tile_send, tile_recv, tile_local, *scatter_refs,
):
    micro = tokens // seq
    per = heads // 4
    size = 192 // per
    me = lax.axis_index("fsdp") * 4 + lax.axis_index("dp")
    start_barrier()
    rs = Scatter(part, out, *scatter_refs, packs)

    def fetch(a, b, sem):
        r = pltpu.make_async_copy(a, b, sem)
        r.start()
        return r

    loads = [fetch(gffn_any, low, in_sem.at[0]), fetch(n2_any, src, in_sem.at[1]), fetch(table, tabv, in_sem.at[2])]

    def load_w(i, slot):
        return pltpu.make_async_copy(whole.at[i % 4, :, lanes_of(i // 4)], wbuf.at[slot], w_sem.at[slot])

    def load_pre(t, slot):
        return pltpu.make_async_copy(pre_any.at[t], pre.at[slot], pre_sem.at[slot])

    def load_act(t, slot):
        return pltpu.make_async_copy(act_any.at[t], act.at[slot], act_sem.at[slot])

    def put_g(dd, lane_pack):
        return pltpu.make_async_copy(gst, part.at[dd, :, lanes_of(lane_pack)], g_sem)

    for r in (load_w(4, 0), load_pre(0, 0), load_act(0, 0)):
        r.start()
    sum1[...] = jnp.zeros_like(sum1)
    sum2[...] = jnp.zeros_like(sum2)

    def clear(t):
        r = tile_rows(t, 32)
        acc[r] = jnp.zeros((32, width), F32)
        acc2[r] = jnp.zeros((32, width), F32)

    loop(tokens // 32, clear)
    for r in loads:
        r.wait()
    gain_rows(tabv, 0, gain1)
    gain_rows(tabv, 2, gain2)
    half = width // 2

    def feed(t):
        slot = t % 2

        @pl.when(t < 15)
        def _():
            load_w(5 + t, 1 - slot).start()
            load_pre(t + 1, 1 - slot).start()
            load_act(t + 1, 1 - slot).start()

        load_w(4 + t, slot).wait()
        load_pre(t, slot).wait()
        load_act(t, slot).wait()
        for m in range(micro):
            r = slice(m * seq, (m + 1) * seq)
            gh = nn(low[r], wbuf[slot, :, 2 * CHUNK :])
            u = pre[slot, r, 0:CHUNK]
            ge, th = gelu_parts(u)
            ggu[r, 0:CHUNK] = (gh * pre[slot, r, CHUNK:] * gelu_slope(u, th)).astype(BF)
            ggu[r, CHUNK:] = (gh * ge).astype(BF)
        pl.when((t > 0) & (t != 4))(lambda: put_g(0, 0).wait())
        for h in range(2):
            c = slice(h * half, (h + 1) * half)
            gst[c, 0 : 2 * CHUNK] = tn(src[:, c], ggu[...]).astype(BF)
            gst[c, 2 * CHUNK :] = tn(low[:, c], act[slot]).astype(BF)
        put_g(t % 4, 1 + t // 4).start()
        for m in range(micro):
            r = slice(m * seq, (m + 1) * seq)
            acc[r] += nt(ggu[r], wbuf[slot, :, 0 : 2 * CHUNK])

        @pl.when(t == 3)
        def _():
            put_g(0, 0).wait()
            rs.launch(0)

        pl.when((t > 3) & (t % 2 == 1))(lambda: rs.step(t // 2 - 2))

    loop(16, feed)
    put_g(0, 0).wait()
    n1_load = fetch(n1_any, src, in_sem.at[1])
    load_w(0, 0).start()

    def strm_load(t, slot):
        r = tile_rows(t, 32)
        return [
            pltpu.make_async_copy(mid_any.at[r], strm.at[slot, 0], s_sem.at[slot, 0]),
            pltpu.make_async_copy(gout_any.at[r], strm.at[slot, 1], s_sem.at[slot, 1]),
        ]

    for r in strm_load(0, 0):
        r.start()

    def norm_two(t):
        slot = t % 2

        @pl.when(t + 1 < tokens // 32)
        def _():
            for r in strm_load(t + 1, 1 - slot):
                r.start()

        for r in strm_load(t, slot):
            r.wait()
        r = tile_rows(t, 32)
        grad = strm[slot, 1] + norm_back(strm[slot, 0], acc[r], gain2[...], sum2)
        acc[r] = grad
        low[r] = grad.astype(BF)

    loop(tokens // 32, norm_two)
    n1_load.wait()

    def probs_load(dd, m):
        return pltpu.make_async_copy(probs_any.at[dd * micro + m], ps.at[m], p_sem.at[m])

    def attention(dd):
        slot = dd % 2
        q_load = pltpu.make_async_copy(qkv_any.at[dd], qs, q_sem)
        q_load.start()
        for m in range(micro):
            probs_load(dd, m).start()
        pl.when(dd < 3)(lambda: load_w(dd + 1, 1 - slot).start())
        load_w(dd, slot).wait()
        ga[...] = nn(low[...], wbuf[slot, :, 576:768]).astype(BF)
        q_load.wait()
        pl.when(dd > 0)(lambda: put_g(0, 0).wait())
        gst[:, 576:768] = tn(low[...], qs[:, 576:768]).astype(BF)
        rs.step(6 + 2 * dd)
        for m in range(micro):
            r = slice(m * seq, (m + 1) * seq)
            probs_load(dd, m).wait()
            for hh in range(per):
                a = hh * size
                p = ps[m, hh]
                go = ga[r, a : a + size]
                gp = nt(go, qs[r, 384 + a : 384 + a + size])
                gs = p * (gp - jnp.sum(p * gp, axis=-1, keepdims=True))
                gs = gs.astype(BF)
                gqkv[r, a : a + size] = nn(gs, qs[r, 192 + a : 192 + a + size]).astype(BF)
                gqkv[r, 192 + a : 192 + a + size] = tn(gs, qs[r, a : a + size]).astype(BF)
                gqkv[r, 384 + a : 384 + a + size] = tn(p.astype(BF), go).astype(BF)
                if m == 0:
                    ps[0, hh] = gs.astype(F32)
                else:
                    ps[0, hh] += gs.astype(F32)
        rs.step(7 + 2 * dd)
        for h in range(2):
            c = slice(h * half, (h + 1) * half)
            gst[c, 0:576] = tn(src[:, c], gqkv[...]).astype(BF)
        put_g(dd, 0).start()
        for m in range(micro):
            r = slice(m * seq, (m + 1) * seq)
            acc2[r] += nt(gqkv[r], wbuf[slot, :, 0:576])

        def by_bucket(i):
            hh, group = i // 4, i % 4

            def some(t, totals):
                r = tile_rows(t, 8)
                b = buckets[r]
                v = ps[0, hh, r]
                return tuple(o + jnp.where(b == group * 8 + j, v, 0.0) for j, o in enumerate(totals))

            totals = lax.fori_loop(0, seq // 8, some, (jnp.zeros((8, seq), F32),) * 8)
            lines = [jnp.sum(o, axis=0, keepdims=True) for o in totals]
            bsum[dd * per + hh, pl.ds(pl.multiple_of(group * 8, 8), 8)] = jnp.concatenate(lines, axis=0)

        loop(4 * per, by_bucket)

    loop(4, attention)
    put_g(0, 0).wait()
    rs.step(14)
    x_load = fetch(x_any, src, in_sem.at[1])
    x_load.wait()

    def norm_one(t):
        r = tile_rows(t, 32)
        term = norm_back(src[r].astype(F32), acc2[r], gain1[...], sum1)
        low[r] = (acc[r] + term).astype(BF)

    loop(tokens // 32, norm_one)
    hidden_copy = fetch(low, hidden_out, out2_sem)
    one = jnp.sum(sum1[...], axis=0, keepdims=True)
    two = jnp.sum(sum2[...], axis=0, keepdims=True)
    biases = lax.dot_general(
        jnp.ones((8, seq), F32), bsum[...].reshape(heads * 32, seq), (((1,), (1,)), ((), ())),
        precision=lax.Precision.HIGHEST, preferred_element_type=F32,
    )
    lines = [biases[0:1, 128 * i : 128 * (i + 1)] for i in range(3)]
    none = jnp.zeros((1, 128), F32)
    for i in range(32):
        first = 128 * ((48 * i) // 128)
        rows = []
        for v in (one, two):
            rows.append(v[:, first : first + 128])
            rows.append(v[:, first + 128 : first + 256] if first + 128 < width else none)
        tilev[i] = jnp.concatenate(rows + [loss[0:1, :]] + lines, axis=0)
    tile_copy = fetch(tilev, tiles_out, in_sem.at[0])
    rs.step(15)
    tile_copy.wait()
    tiles = exchange(lambda other: tiles_out.at[other], sums_out, tile_send, tile_recv)
    tile_keep = fetch(tilev.at[me], sums_out.at[me], tile_local)
    lax.fori_loop(16, 4 * packs + 2, lambda s, carry: (rs.step(s), carry)[1], 0)
    rs.finish()
    hidden_copy.wait()
    tile_keep.wait()
    tiles.wait()


def backward(whole, table, x, n1, n2, qkv, probs, pre, act, mid, gout, gffn, buckets, loss, heads):
    packs = whole.shape[2] // LANES
    tokens, width = x.shape
    seq = buckets.shape[0]
    micro = tokens // seq
    any_ = pl.BlockSpec(memory_space=pl.ANY)
    vmem = pl.BlockSpec(memory_space=pltpu.VMEM)
    S = jax.ShapeDtypeStruct
    V = pltpu.VMEM
    dma = pltpu.SemaphoreType.DMA
    outs = (
        S(whole.shape, BF), S((ROWS, whole.shape[2]), F32), S((tokens, width), BF), S((32, 8, 128), F32), S((32, 8, 128), F32),
    )
    return pl.pallas_call(
        functools.partial(backward_kernel, packs, tokens, width, seq, heads),
        out_shape=outs,
        in_specs=[any_] * 12 + [vmem] * 2,
        out_specs=[any_] * 5,
        scratch_shapes=[
            V((tokens, width), BF), V((tokens, width), BF), V((tokens, width), F32), V((tokens, width), F32),
            V((2, 8 * ROWS, LANES), BF), V((2, tokens, 2 * CHUNK), F32), V((2, tokens, CHUNK), BF), V((tokens, 2 * CHUNK), BF),
            V((8 * ROWS, LANES), BF), V((2, 2, 32, width), F32), V((tokens, 768), BF), V((micro, heads // 4, seq, seq), F32),
            V((tokens, 192), BF), V((tokens, 576), BF), V((heads, 32, seq), F32), V((1, width), F32), V((1, width), F32),
            V((8, width), F32), V((8, width), F32), V((32, 8, 128), F32), V((32, 8, 128), F32),
            dma((3,)), dma((2,)), dma((2,)), dma((2,)), dma, dma((2, 2)), dma, dma((micro,)), dma, dma, dma, dma,
        ] + scatter_scratch(packs),
        compiler_params=pltpu.CompilerParams(collective_id=2, has_side_effects=True, vmem_limit_bytes=67043328),
    )(whole, table, x, n1, n2, qkv, probs, pre, act, mid, gout, gffn, buckets, loss)


def tuned_body(
    hidden, teacher, cotangent, valid_mask, blocks, buckets, first_gain, query_weight, key_weight, value_weight,
    output_weight, second_gain, gate_weight, up_weight, down_weight, bias_table,
):
    micro, _, seq, width = hidden.shape
    tokens = micro * seq
    bucket_count, heads = bias_table.shape
    part = gate_weight.shape[1]
    cols = query_weight.shape[1]
    per = first_gain.shape[0]
    scale = float(tokens * 32 * width)
    valid = valid_mask.reshape(micro, seq)
    block_ids = blocks.reshape(micro, seq)
    weights = (query_weight, key_weight, value_weight, output_weight, gate_weight, up_weight, down_weight)
    own, tile = prepare(weights, first_gain, second_gain, valid)
    x = hidden.reshape(tokens, width)
    whole, table, n1, n2, qkv, probs, pre, act, mid, layer, gout, gffn, loss = forward(
        own, tile, x, teacher.reshape(tokens, width), cotangent.reshape(tokens, width), buckets, bias_table.astype(F32),
        block_ids, block_ids.reshape(tokens, 1), valid, valid.reshape(tokens, 1).astype(F32), scale,
    )
    _, shard, hidden_grad, _, sums = backward(
        whole, table, x, n1, n2, qkv, probs, pre, act, mid, gout, gffn, buckets, loss, heads
    )
    sums = jnp.sum(sums, axis=0)
    me = lax.axis_index("fsdp") * 4 + lax.axis_index("dp")
    first = (me * per) % 128
    gain_one = lax.dynamic_slice(sums[0:2].reshape(256), (first,), (per,))
    gain_two = lax.dynamic_slice(sums[2:4].reshape(256), (first,), (per,))
    valid_total = jnp.sum(table[:, 4, 0])
    ff = [
        jnp.concatenate([shard[:, LANES * (j + 1) + i * CHUNK : LANES * (j + 1) + (i + 1) * CHUNK] for j in range(4)], axis=1)[:, :part]
        for i in range(3)
    ]
    at = [shard[:, i * cols : (i + 1) * cols] for i in range(4)]
    return (
        layer.reshape(hidden.shape),
        sums[4, 0] / (valid_total * width),
        hidden_grad.reshape(hidden.shape),
        gain_one, at[0], at[1], at[2], at[3], gain_two, ff[0], ff[1], ff[2],
        sums[5:8].reshape(heads, bucket_count).T,
    )


def solution(mesh):
    in_specs = (
        P(None, ("fsdp", "dp"), None, None),
        P(None, ("fsdp", "dp"), None, None),
        P(None, ("fsdp", "dp"), None, None),
        P(None, ("fsdp", "dp"), None),
        P(None, ("fsdp", "dp"), None),
        P(),
        P(("fsdp", "dp")),
        P("fsdp", "dp"),
        P("fsdp", "dp"),
        P("fsdp", "dp"),
        P("fsdp", "dp"),
        P(("fsdp", "dp")),
        P("fsdp", "dp"),
        P("fsdp", "dp"),
        P("fsdp", "dp"),
        P(),
    )
    out_specs = (
        P(None, ("fsdp", "dp"), None, None),
        P(),
        P(None, ("fsdp", "dp"), None, None),
        P(("fsdp", "dp")),
        P("fsdp", "dp"),
        P("fsdp", "dp"),
        P("fsdp", "dp"),
        P("fsdp", "dp"),
        P(("fsdp", "dp")),
        P("fsdp", "dp"),
        P("fsdp", "dp"),
        P("fsdp", "dp"),
        P(),
    )
    chosen = tuned_body if dict(mesh.shape) == {"fsdp": 8, "dp": 4} else body
    return jax.shard_map(chosen, mesh=mesh, in_specs=in_specs, out_specs=out_specs, check_vma=False)
```

```python
import functools
import jax
import jax.numpy as jnp
from jax import lax
from jax.experimental import pallas as pl
from jax.experimental.pallas import tpu as pltpu
from jax.sharding import PartitionSpec as P

EPS = 1e-06
NEG = -1000000000.0
HIGH = lax.Precision.HIGHEST


def times_rows(former, latter):
    return jnp.dot(former, latter, preferred_element_type=jnp.float32)


def times_transpose(former, latter):
    return lax.dot_general(
        former, latter, (((1,), (1,)), ((), ())), preferred_element_type=jnp.float32
    )


def over_tokens(former, latter):
    return lax.dot_general(
        former, latter, (((0,), (0,)), ((), ())), preferred_element_type=jnp.float32
    )


def assemble(gathered, fsdp_count, dp_count):
    row_block = gathered.shape[0] // (fsdp_count * dp_count)
    col_block = gathered.shape[1]
    shaped = gathered.reshape(fsdp_count, dp_count, row_block, col_block)
    return jnp.transpose(shaped, (0, 2, 1, 3)).reshape(fsdp_count * row_block, dp_count * col_block)


def disperse(gradient, fsdp_count, dp_count):
    row_block = gradient.shape[0] // fsdp_count
    col_block = gradient.shape[1] // dp_count
    shaped = gradient.reshape(fsdp_count, row_block, dp_count, col_block)
    return jnp.transpose(shaped, (0, 2, 1, 3)).reshape(fsdp_count * dp_count * row_block, col_block)


def norm_forward(inputs, norm_gain):
    row_scale = lax.rsqrt(jnp.mean(inputs * inputs, axis=-1, keepdims=True) + EPS)
    return (inputs * row_scale * norm_gain, row_scale)


def norm_backward(inputs, row_scale, norm_gain, upstream):
    scaled = upstream * norm_gain
    gain_grad = jnp.sum(upstream * inputs * row_scale, axis=0)
    mean_term = jnp.mean(scaled * inputs, axis=-1, keepdims=True)
    return (
        row_scale * scaled - inputs * (row_scale * row_scale * row_scale) * mean_term,
        gain_grad,
    )


def gelu_tanh(values_in):
    return jax.nn.gelu(values_in, approximate=True)


def masked_scores(queries, key_heads, position_bias, allowed):
    products = jnp.einsum("qhd,khd->hqk", queries, key_heads, preferred_element_type=jnp.float32)
    return jnp.where(allowed[None], products + position_bias, NEG)


def body(
    hidden,
    teacher,
    cotangent,
    valid_mask,
    blocks,
    buckets,
    first_gain,
    query_weight,
    key_weight,
    value_weight,
    output_weight,
    second_gain,
    gate_weight,
    up_weight,
    down_weight,
    bias_table,
):
    fsdp_count = lax.axis_size("fsdp")
    dp_count = lax.axis_size("dp")
    micro_count = hidden.shape[0]
    seq_len = hidden.shape[2]
    model_width = hidden.shape[3]
    bucket_count = bias_table.shape[0]
    head_count = bias_table.shape[1]
    scale_factor = jnp.float32(
        float(micro_count * lax.axis_size(("fsdp", "dp")) * hidden.shape[1] * seq_len * model_width)
    )
    valid_float = valid_mask.astype(jnp.float32)
    valid_total = lax.psum(jnp.sum(valid_float), ("fsdp", "dp"))
    places = lax.broadcasted_iota(jnp.int32, (1, 1, bucket_count), 2)
    onehot = (buckets[:, :, None] == places).astype(jnp.float32)
    position_bias = jnp.einsum(
        "qkb,bh->hqk", onehot, bias_table.astype(jnp.float32), precision=HIGH
    )
    onehot_low = onehot.astype(jnp.bfloat16)
    rows_iota = lax.broadcasted_iota(jnp.int32, (seq_len, seq_len), 0)
    cols_iota = lax.broadcasted_iota(jnp.int32, (seq_len, seq_len), 1)
    diagonal = rows_iota == cols_iota

    def rebuild(gathered):
        return (gathered[0],) + tuple(
            (assemble(matrix, fsdp_count, dp_count) for matrix in gathered[1:])
        )

    def spread_out(grads):
        return (
            (grads[0],)
            + tuple((disperse(matrix, fsdp_count, dp_count) for matrix in grads[1:5]))
            + (grads[5],)
            + tuple((disperse(matrix, fsdp_count, dp_count) for matrix in grads[6:]))
        )

    outputs_list = []
    input_grads = []
    squares = jnp.float32(0.0)
    table_grad = jnp.zeros((bucket_count, head_count), jnp.float32)
    totals = None
    for step_index in range(micro_count):
        inputs = hidden[step_index, 0].astype(jnp.float32)
        target = teacher[step_index, 0].astype(jnp.float32)
        upstream = cotangent[step_index, 0].astype(jnp.float32)
        token_valid = valid_float[step_index, 0]
        block_ids = blocks[step_index, 0]
        allowed = (block_ids[None, :] <= block_ids[:, None]) & (
            valid_mask[step_index, 0][None, :] == 1
        ) | diagonal
        first_block = rebuild(
            (
                lax.all_gather(first_gain, ("fsdp", "dp"), axis=0, tiled=True),
                lax.all_gather(query_weight, ("fsdp", "dp"), axis=0, tiled=True),
                lax.all_gather(key_weight, ("fsdp", "dp"), axis=0, tiled=True),
                lax.all_gather(value_weight, ("fsdp", "dp"), axis=0, tiled=True),
                lax.all_gather(output_weight, ("fsdp", "dp"), axis=0, tiled=True),
            )
        )
        gain_one = first_block[0].astype(jnp.float32)
        normed_full, scale_one = norm_forward(inputs, gain_one)
        normed_one = normed_full.astype(jnp.bfloat16)
        head_size = first_block[1].shape[1] // head_count
        head_split = (seq_len, head_count, head_size)
        queries = times_rows(normed_one, first_block[1]).astype(jnp.bfloat16).reshape(head_split)
        key_heads = times_rows(normed_one, first_block[2]).astype(jnp.bfloat16).reshape(head_split)
        value_heads = (
            times_rows(normed_one, first_block[3]).astype(jnp.bfloat16).reshape(head_split)
        )
        scores = masked_scores(queries, key_heads, position_bias, allowed)
        row_max = jnp.max(scores, axis=-1, keepdims=True)
        exponent = jnp.exp(scores - row_max)
        row_total = jnp.sum(exponent, axis=-1, keepdims=True)
        log_total = row_max + jnp.log(row_total)
        softmax_low = (exponent / row_total).astype(jnp.bfloat16)
        attended = jnp.einsum(
            "hqk,khd->qhd", softmax_low, value_heads, preferred_element_type=jnp.float32
        )
        attended = attended.astype(jnp.bfloat16).reshape(seq_len, head_count * head_size)
        middle = inputs + times_transpose(attended, first_block[4])
        second_block = rebuild(
            (
                lax.all_gather(second_gain, ("fsdp", "dp"), axis=0, tiled=True),
                lax.all_gather(gate_weight, ("fsdp", "dp"), axis=0, tiled=True),
                lax.all_gather(up_weight, ("fsdp", "dp"), axis=0, tiled=True),
                lax.all_gather(down_weight, ("fsdp", "dp"), axis=0, tiled=True),
            )
        )
        gain_two = second_block[0].astype(jnp.float32)
        normed_mid, scale_two = norm_forward(middle, gain_two)
        normed_two = normed_mid.astype(jnp.bfloat16)
        gate_pre = times_rows(normed_two, second_block[1])
        up_pre = times_rows(normed_two, second_block[2])
        gate_act, gelu_pullback = jax.vjp(gelu_tanh, gate_pre)
        hidden_act = (gate_act * up_pre).astype(jnp.bfloat16)
        layer_full = middle + times_transpose(hidden_act, second_block[3])
        outputs_list.append(layer_full.astype(jnp.bfloat16))
        residual_gap = layer_full - target
        weighted_gap = token_valid[:, None] * residual_gap
        squares = squares + jnp.sum(weighted_gap * residual_gap)
        grad_out = scale_factor * upstream + scale_factor * (
            2.0 * weighted_gap / (valid_total * model_width)
        )
        back_second = rebuild(
            (
                lax.all_gather(second_gain, ("fsdp", "dp"), axis=0, tiled=True),
                lax.all_gather(gate_weight, ("fsdp", "dp"), axis=0, tiled=True),
                lax.all_gather(up_weight, ("fsdp", "dp"), axis=0, tiled=True),
                lax.all_gather(down_weight, ("fsdp", "dp"), axis=0, tiled=True),
            )
        )
        grad_ffn = grad_out.astype(jnp.bfloat16)
        down_part = over_tokens(grad_ffn, hidden_act)
        grad_hidden_act = times_rows(grad_ffn, back_second[3])
        grad_gate = gelu_pullback(grad_hidden_act * up_pre)[0].astype(jnp.bfloat16)
        grad_up = (grad_hidden_act * gate_act).astype(jnp.bfloat16)
        gate_part = over_tokens(normed_two, grad_gate)
        up_part = over_tokens(normed_two, grad_up)
        grad_normed_two = times_transpose(grad_gate, back_second[1]) + times_transpose(
            grad_up, back_second[2]
        )
        middle_term, gain_two_part = norm_backward(
            middle, scale_two, back_second[0].astype(jnp.float32), grad_normed_two
        )
        grad_middle = grad_out + middle_term
        grad_attn = grad_middle.astype(jnp.bfloat16)
        back_first = rebuild(
            (
                lax.all_gather(first_gain, ("fsdp", "dp"), axis=0, tiled=True),
                lax.all_gather(query_weight, ("fsdp", "dp"), axis=0, tiled=True),
                lax.all_gather(key_weight, ("fsdp", "dp"), axis=0, tiled=True),
                lax.all_gather(value_weight, ("fsdp", "dp"), axis=0, tiled=True),
                lax.all_gather(output_weight, ("fsdp", "dp"), axis=0, tiled=True),
            )
        )
        output_part = over_tokens(grad_attn, attended)
        grad_attended = (
            times_rows(grad_attn, back_first[4]).astype(jnp.bfloat16).reshape(head_split)
        )
        scores_again = masked_scores(queries, key_heads, position_bias, allowed)
        softmax_again = jnp.exp(scores_again - log_total)
        grad_probs = jnp.einsum(
            "qhd,khd->hqk", grad_attended, value_heads, preferred_element_type=jnp.float32
        )
        grad_scores = softmax_again * (
            grad_probs - jnp.sum(softmax_again * grad_probs, axis=-1, keepdims=True)
        )
        grad_scores = grad_scores.astype(jnp.bfloat16)
        table_grad = table_grad + jnp.einsum(
            "hqk,qkb->bh", grad_scores, onehot_low, preferred_element_type=jnp.float32
        )
        flat_width = head_count * head_size
        grad_queries = (
            jnp.einsum("hqk,khd->qhd", grad_scores, key_heads, preferred_element_type=jnp.float32)
            .astype(jnp.bfloat16)
            .reshape(seq_len, flat_width)
        )
        grad_keys = (
            jnp.einsum("hqk,qhd->khd", grad_scores, queries, preferred_element_type=jnp.float32)
            .astype(jnp.bfloat16)
            .reshape(seq_len, flat_width)
        )
        grad_values = (
            jnp.einsum(
                "hqk,qhd->khd",
                softmax_again.astype(jnp.bfloat16),
                grad_attended,
                preferred_element_type=jnp.float32,
            )
            .astype(jnp.bfloat16)
            .reshape(seq_len, flat_width)
        )
        query_part = over_tokens(normed_one, grad_queries)
        key_part = over_tokens(normed_one, grad_keys)
        value_part = over_tokens(normed_one, grad_values)
        grad_normed_one = (
            times_transpose(grad_queries, back_first[1])
            + times_transpose(grad_keys, back_first[2])
            + times_transpose(grad_values, back_first[3])
        )
        input_term, gain_one_part = norm_backward(
            inputs, scale_one, back_first[0].astype(jnp.float32), grad_normed_one
        )
        input_grads.append((grad_middle + input_term).astype(jnp.bfloat16))
        step_set = spread_out(
            (
                gain_one_part,
                query_part,
                key_part,
                value_part,
                output_part,
                gain_two_part,
                gate_part,
                up_part,
                down_part,
            )
        )
        totals = step_set if totals is None else jax.tree.map(jnp.add, totals, step_set)
    shards = (
        lax.psum_scatter(totals[0], ("fsdp", "dp"), scatter_dimension=0, tiled=True),
        lax.psum_scatter(totals[1], ("fsdp", "dp"), scatter_dimension=0, tiled=True),
        lax.psum_scatter(totals[2], ("fsdp", "dp"), scatter_dimension=0, tiled=True),
        lax.psum_scatter(totals[3], ("fsdp", "dp"), scatter_dimension=0, tiled=True),
        lax.psum_scatter(totals[4], ("fsdp", "dp"), scatter_dimension=0, tiled=True),
        lax.psum_scatter(totals[5], ("fsdp", "dp"), scatter_dimension=0, tiled=True),
        lax.psum_scatter(totals[6], ("fsdp", "dp"), scatter_dimension=0, tiled=True),
        lax.psum_scatter(totals[7], ("fsdp", "dp"), scatter_dimension=0, tiled=True),
        lax.psum_scatter(totals[8], ("fsdp", "dp"), scatter_dimension=0, tiled=True),
    )
    total_squares, table_all = lax.psum((squares, table_grad), ("fsdp", "dp"))
    loss_value = total_squares / (valid_total * model_width)
    layer_output = jnp.stack(outputs_list)[:, None]
    hidden_grad = jnp.stack(input_grads)[:, None]
    return (
        layer_output,
        loss_value,
        hidden_grad,
        shards[0],
        shards[1],
        shards[2],
        shards[3],
        shards[4],
        shards[5],
        shards[6],
        shards[7],
        shards[8],
        table_all,
    )


MESH_ID = pl.DeviceIdType.MESH
LANES = 768
ROWS = 192


def place():
    f = lax.axis_index("fsdp")
    d = lax.axis_index("dp")
    return f // 2, f % 2, d // 2, d % 2


def device(z, x, y, c):
    return (z * 2 + x, y * 2 + c)


def tell_all():
    f = lax.axis_index("fsdp")
    d = lax.axis_index("dp")
    barrier = pltpu.get_barrier_semaphore()

    def tell(step, carry):
        other = (f * 4 + d + step) % 32
        pl.semaphore_signal(
            barrier, inc=1, device_id=(other // 4, other % 4), device_id_type=MESH_ID
        )
        return carry

    lax.fori_loop(1, 32, tell, 0)


def hear_all():
    pl.semaphore_wait(pltpu.get_barrier_semaphore(), 31)


def start_barrier():
    tell_all()
    hear_all()


def exchange(tile_of, table, send, recv):
    f = lax.axis_index("fsdp")
    d = lax.axis_index("dp")
    me = f * 4 + d

    def one(step, carry):
        other = (me + step) % 32
        pltpu.make_async_remote_copy(
            tile_of(other), table.at[me], send, recv,
            device_id=(other // 4, other % 4), device_id_type=MESH_ID,
        ).start()
        return carry

    lax.fori_loop(1, 32, one, 0)
    view = table.at[pl.ds(0, 31)]
    return pltpu.make_async_remote_copy(
        view, view, send, recv, device_id=(f, (d + 1) % 4), device_id_type=MESH_ID
    )


def lanes_of(pack):
    return pl.ds(pl.multiple_of(pack * LANES, 128), LANES)


def rows_of(z, x, first, count):
    return pl.ds(pl.multiple_of((z * 2 + x) * ROWS + first, 32), count)


G_Z, G_X0, G_Y0, G_XZ, G_YZ, G_DY, G_DX = 0, 4, 5, 6, 10, 14, 18
G_XA, G_XB, G_YA, G_YB, G_C, G_BACK = 22, 25, 28, 31, 34, 50
G_COUNT = 53


def on_chain(z, k):
    end = (3 - z) // 3 + z // 3
    low = end * k + (1 - end) * (k - (3 - k) // 2)
    high = z // 2
    return high * (3 - low) + (1 - high) * low


class Gather:
    def __init__(self, own, whole, send, recv, packs):
        self.own, self.whole, self.send, self.recv, self.packs = own, whole, send, recv, packs
        self.z, self.x, self.y, self.c = place()

    def put(self, pack, slot, shard, first, count, target, own=False, send=None):
        zz, xx, yy = shard
        there = self.whole.at[yy * 2 + self.c, rows_of(zz, xx, first, count), lanes_of(pack)]
        here = self.own.at[pl.ds(first, count), lanes_of(pack)] if own else there
        pltpu.make_async_remote_copy(
            here, there, self.send.at[pack, slot if send is None else send], self.recv.at[pack, slot],
            device_id=device(*target), device_id_type=MESH_ID,
        ).start()

    def along(self, pack, slot, back, shard, first, count, own=False):
        z, x, y, c = self.z, self.x, self.y, self.c
        pl.when(z < 3)(lambda: self.put(pack, slot + z, shard, first, count, (z + 1, x, y, c), own=own))
        pl.when(z > 0)(lambda: self.put(pack, slot + z, shard, first, count, (z - 1, x, y, c), own=own, send=back))

    def further(self, pack, slot, shard, first, count):
        z, x, y, c = self.z, self.x, self.y, self.c
        zz = shard[0]
        pl.when((zz < z) & (z < 3))(lambda: self.put(pack, slot + zz, shard, first, count, (z + 1, x, y, c)))
        pl.when((zz > z) & (z > 0))(lambda: self.put(pack, slot + zz, shard, first, count, (z - 1, x, y, c)))

    def some(self, pack, slot, count):
        view = self.whole.at[0, pl.ds(0, count), lanes_of(pack)]
        return pltpu.make_async_remote_copy(
            view, view, self.send.at[pack, slot], self.recv.at[pack, slot],
            device_id=device(self.z, self.x, self.y, 1 - self.c), device_id_type=MESH_ID,
        )

    def got(self, pack, slot, count):
        self.some(pack, slot, count).wait_recv()

    def launch(self, pack):
        self.along(pack, G_Z, G_BACK, (self.z, self.x, self.y), 0, 192, own=True)

    def first(self, pack, k):
        z, x, y, c = self.z, self.x, self.y, self.c
        xn, yn, cn = (z, 1 - x, y, c), (z, x, 1 - y, c), (z, x, y, 1 - c)

        @pl.when(k == 0)
        def _():
            self.put(pack, G_X0, (z, x, y), 0, 192, xn, own=True)
            self.put(pack, G_Y0, (z, x, y), 0, 192, yn, own=True)
            self.put(pack, G_C, (z, x, y), 0, 192, cn, own=True)

        @pl.when(k > 0)
        def _():
            zz = on_chain(z, k)
            mine = (zz, x, y)
            self.got(pack, G_Z + zz, 192)
            self.further(pack, G_Z, mine, 0, 192)
            self.put(pack, G_XA + k - 1, mine, 0, 32, xn)
            self.put(pack, G_YA + k - 1, mine, 160, 32, yn)
            self.put(pack, G_XB + k - 1, mine, 96, 96, xn)
            self.put(pack, G_YB + k - 1, mine, 0, 96, yn)
            self.put(pack, G_C + 4 * k, mine, 0, 192, cn)

    def second(self, pack, k):
        z, x, y, c = self.z, self.x, self.y, self.c
        xn, yn, cn = (z, 1 - x, y, c), (z, x, 1 - y, c), (z, x, y, 1 - c)

        @pl.when(k == 0)
        def _():
            self.got(pack, G_X0, 192)
            self.along(pack, G_XZ, G_BACK + 1, (z, 1 - x, y), 32, 64)
            self.put(pack, G_DY, (z, 1 - x, y), 0, 96, yn)
            self.put(pack, G_C + 1, (z, 1 - x, y), 0, 192, cn)
            self.got(pack, G_Y0, 192)
            self.along(pack, G_YZ, G_BACK + 2, (z, x, 1 - y), 96, 64)
            self.put(pack, G_DX, (z, x, 1 - y), 96, 96, xn)
            self.put(pack, G_C + 2, (z, x, 1 - y), 0, 192, cn)

        @pl.when(k > 0)
        def _():
            zz = on_chain(z, k)
            across_x, across_y = (zz, 1 - x, y), (zz, x, 1 - y)
            self.got(pack, G_XZ + zz, 64)
            self.further(pack, G_XZ, across_x, 32, 64)
            self.got(pack, G_YZ + zz, 64)
            self.further(pack, G_YZ, across_y, 96, 64)
            self.got(pack, G_XA + k - 1, 32)
            self.put(pack, G_DY + k, across_x, 0, 96, yn)
            self.got(pack, G_YA + k - 1, 32)
            self.put(pack, G_DX + k, across_y, 96, 96, xn)
            self.got(pack, G_XB + k - 1, 96)
            self.put(pack, G_C + 4 * k + 1, across_x, 0, 192, cn)
            self.got(pack, G_YB + k - 1, 96)
            self.put(pack, G_C + 4 * k + 2, across_y, 0, 192, cn)

    def third(self, pack, k):
        z, x, y, c = self.z, self.x, self.y, self.c
        self.got(pack, G_DY + k, 96)
        self.got(pack, G_DX + k, 96)

        def on(zz):
            self.put(pack, G_C + 4 * k + 3, (zz, 1 - x, 1 - y), 0, 192, (z, x, y, 1 - c))

        pl.when(k == 0)(lambda: on(z))
        pl.when(k > 0)(lambda: on(on_chain(z, k)))

    def step(self, s):
        total = 4 * self.packs

        @pl.when(s < total)
        def _():
            self.first(s // 4, s % 4)
            pl.when((s % 4 == 3) & (s + 1 < total))(lambda: self.launch(s // 4 + 1))

        pl.when((s >= 2) & (s <= total + 1))(lambda: self.second((s + 2) // 4 - 1, (s + 2) % 4))
        pl.when((s >= 4) & (s <= total + 3))(lambda: self.third(s // 4 - 1, s % 4))

    def arrived(self, pack):
        for slot in range(G_C, G_C + 16):
            self.got(pack, slot, 192)

    def finish(self):
        z = self.z

        def sent(pack, slot, count):
            self.some(pack, slot, count).wait_send()

        def one(pack, carry):
            for slot, count in ((G_X0, 192), (G_Y0, 192)):
                sent(pack, slot, count)
            for base, n, count in (
                (G_DY, 4, 96), (G_DX, 4, 96), (G_XA, 3, 32), (G_XB, 3, 96), (G_YA, 3, 32), (G_YB, 3, 96), (G_C, 16, 192),
            ):
                for i in range(n):
                    sent(pack, base + i, count)
            for i, (base, count) in enumerate(((G_Z, 192), (G_XZ, 64), (G_YZ, 64))):
                pl.when(z > 0)(lambda: sent(pack, G_BACK + i, count))
                for zz in range(4):
                    pl.when((zz <= z) & (z < 3))(lambda: sent(pack, base + zz, count))
                    pl.when((zz > z) & (z > 0))(lambda: sent(pack, base + zz, count))
            return carry

        lax.fori_loop(0, self.packs, one, 0)


R_C, R_V, R_U, R_ZC, R_Z, R_F = 0, 16, 32, 38, 44, 47
R_COUNT = 49
R_ROWS = [192] * 16 + [96] * 16 + [64] * 6 + [32] * 6 + [192] * 3 + [96] * 2
ORDER = (1, 2, 3, 0)
TILE = 32


def add_rows(into, what, count):
    size = 96 if count % 96 == 0 else count

    def one(t, carry):
        r = pl.ds(pl.multiple_of(t * size, 32), size)
        into[r] = into[r] + what[r]
        return carry

    if count == size:
        into[...] = into[...] + what[...]
    else:
        lax.fori_loop(0, count // size, one, 0)


class Scatter:
    def __init__(self, part, out, mine, buf_c, buf_v, buf_u, buf_zc, buf_z, buf_f, send, recv, load, credit, stage, out_sem, packs):
        self.stage, self.out_sem = stage, out_sem
        self.part, self.out, self.mine = part, out, mine
        self.buf_c, self.buf_v, self.buf_u, self.buf_zc, self.buf_z, self.buf_f = buf_c, buf_v, buf_u, buf_zc, buf_z, buf_f
        self.send, self.recv, self.load_sem, self.credit, self.packs = send, recv, load, credit, packs
        self.z, self.x, self.y, self.c = place()
        z, x, y, c = place()
        self.xn, self.yn, self.cn = (z, 1 - x, y, c), (z, x, 1 - y, c), (z, x, y, 1 - c)

    def at(self, par, shard, first, count):
        zz, xx, yy = shard
        return self.mine.at[par, yy, rows_of(zz, xx, first, count)]

    def put(self, par, slot, here, there, target):
        pltpu.make_async_remote_copy(
            here, there, self.send.at[par, slot], self.recv.at[par, slot],
            device_id=device(*target), device_id_type=MESH_ID,
        ).start()

    def some(self, par, slot, count):
        view = self.mine.at[par, 0, pl.ds(0, count)]
        return pltpu.make_async_remote_copy(
            view, view, self.send.at[par, slot], self.recv.at[par, slot],
            device_id=device(*self.cn), device_id_type=MESH_ID,
        )

    def got(self, par, slot, count):
        self.some(par, slot, count).wait_recv()

    def lane_pack(self, pack):
        return (pack + 1) % self.packs

    def shards(self, k):
        zz = (self.z + k) % 4
        return ((zz, 1 - self.x, 1 - self.y), (zz, self.x, 1 - self.y), (zz, 1 - self.x, self.y), (zz, self.x, self.y))

    def loads(self, pack):
        par = pack % 2
        return [
            pltpu.make_async_copy(
                self.part.at[yy * 2 + self.c, :, lanes_of(self.lane_pack(pack))], self.mine.at[par, yy], self.load_sem.at[yy]
            )
            for yy in range(2)
        ]

    def ahead(self, s):
        pack = s // 4
        k = (s % 4 + 1) % 4
        par = pack % 2
        if not isinstance(s, int):
            pl.when((pack >= 2) & (s % 4 == 0))(lambda: pl.semaphore_wait(self.credit.at[pack - 2, 0], 1))
        for i, (zz, xx, yy) in enumerate(self.shards(k)):
            rows = rows_of(zz, xx, 0, 192)
            slot = R_C + 4 * k + i
            if not isinstance(s, int):
                pl.when(pack >= 2)(lambda: self.some(par, slot, 192).wait_send())
            self.put(
                par, slot,
                self.part.at[yy * 2 + 1 - self.c, rows, lanes_of(self.lane_pack(pack))],
                self.buf_c.at[par, yy, rows], self.cn,
            )

    def launch(self):
        self.ahead(0)
        self.ahead(1)
        self.load(0)

    def load(self, pack):
        for r in self.loads(pack):
            r.start()

    def sent(self, pack, first, last):
        for slot in range(first, last):
            self.some(pack % 2, slot, R_ROWS[slot]).wait_send()

    def core(self, pack, k):
        par = pack % 2
        sh = self.shards(k)

        @pl.when(k == ORDER[0])
        def _():
            for r in self.loads(pack):
                r.wait()
            pl.when(pack >= 2)(lambda: pl.semaphore_wait(self.credit.at[pack - 2, 1], 5))

        for i, (zz, xx, yy) in enumerate(sh):
            self.got(par, R_C + 4 * k + i, 192)
            add_rows(self.at(par, sh[i], 0, 192), self.buf_c.at[par, yy, rows_of(zz, xx, 0, 192)], 192)
        pl.when((k == ORDER[3]) & (pack + 2 < self.packs))(lambda: self.free(pack, 0, self.cn))
        v = self.buf_v
        self.put(par, R_V + 4 * k, self.at(par, sh[0], 0, 96), v.at[par, k, 0], self.yn)
        self.put(par, R_V + 4 * k + 1, self.at(par, sh[0], 96, 96), v.at[par, k, 1], self.xn)
        self.put(par, R_V + 4 * k + 2, self.at(par, sh[1], 0, 96), v.at[par, k, 2], self.yn)
        self.put(par, R_V + 4 * k + 3, self.at(par, sh[2], 96, 96), v.at[par, k, 3], self.xn)

    def free(self, pack, kind, target):
        pl.semaphore_signal(
            self.credit.at[pack, kind], inc=1, device_id=device(*target), device_id_type=MESH_ID
        )

    def vees(self, pack, k):
        par = pack % 2
        sh = self.shards(k)
        peer = ((self.z + k) % 4, self.x, self.y, self.c)
        v = self.buf_v
        self.got(par, R_V + 4 * k, 96)
        add_rows(self.at(par, sh[2], 0, 96), v.at[par, k, 0], 96)

        @pl.when(k > 0)
        def _():
            self.put(par, R_U + 2 * (k - 1), self.at(par, sh[2], 0, 64), self.buf_u.at[par, k - 1, 0], self.xn)
            self.put(par, R_ZC + 2 * (k - 1), self.at(par, sh[2], 64, 32), self.buf_zc.at[par, k - 1, 0], peer)

        self.got(par, R_V + 4 * k + 1, 96)
        add_rows(self.at(par, sh[1], 96, 96), v.at[par, k, 1], 96)

        @pl.when(k > 0)
        def _():
            self.put(par, R_U + 2 * (k - 1) + 1, self.at(par, sh[1], 128, 64), self.buf_u.at[par, k - 1, 1], self.yn)
            self.put(par, R_ZC + 2 * (k - 1) + 1, self.at(par, sh[1], 96, 32), self.buf_zc.at[par, k - 1, 1], peer)
            self.got(par, R_V + 4 * k + 2, 96)
            add_rows(self.at(par, sh[3], 0, 96), v.at[par, k, 2], 96)
            self.got(par, R_V + 4 * k + 3, 96)
            add_rows(self.at(par, sh[3], 96, 96), v.at[par, k, 3], 96)

    def yous(self, pack, k):
        par = pack % 2
        sh = self.shards(k)
        peer = ((self.z + k) % 4, self.x, self.y, self.c)
        self.got(par, R_U + 2 * (k - 1), 64)
        add_rows(self.at(par, sh[3], 0, 64), self.buf_u.at[par, k - 1, 0], 64)
        self.got(par, R_U + 2 * (k - 1) + 1, 64)
        add_rows(self.at(par, sh[3], 128, 64), self.buf_u.at[par, k - 1, 1], 64)
        self.put(par, R_Z + k - 1, self.at(par, sh[3], 0, 192), self.buf_z.at[par, k - 1], peer)

    def near(self, pack):
        par = pack % 2
        sh = self.shards(0)
        for j, (shard, first, whole, nb) in enumerate(((sh[2], 64, 0, self.xn), (sh[1], 96, 96, self.yn))):
            for k in range(3):
                self.got(par, R_ZC + 2 * k + j, 32)
            into = self.at(par, shard, first, 32)
            b = self.buf_zc
            into[...] = (
                into[...].astype(jnp.float32)
                + b[par, 0, j].astype(jnp.float32)
                + b[par, 1, j].astype(jnp.float32)
                + b[par, 2, j].astype(jnp.float32)
            ).astype(into.dtype)
            self.put(par, R_F + j, self.at(par, shard, whole, 96), self.buf_f.at[par, j], nb)

    def out_copy(self, pack):
        return pltpu.make_async_copy(self.stage, self.out.at[:, lanes_of(self.lane_pack(pack))], self.out_sem)

    def final(self, pack):
        par = pack % 2
        own = self.at(par, self.shards(0)[3], 0, 192)
        self.got(par, R_V + 2, 96)
        self.got(par, R_V + 3, 96)
        for k in range(3):
            self.got(par, R_Z + k, 192)
        for j in range(2):
            self.got(par, R_F + j, 96)
        pl.when(pack > 0)(lambda: self.out_copy(pack).wait())
        for j in range(2):
            def one(t, carry, j=j):
                r = pl.ds(pl.multiple_of(t * TILE, TILE), TILE)
                rr = pl.ds(pl.multiple_of(j * 96 + t * TILE, TILE), TILE)
                total = own[rr].astype(jnp.float32) + self.buf_v[par, 0, 2 + j, r].astype(jnp.float32)
                total = total + self.buf_f[par, j, r].astype(jnp.float32)
                for k in range(3):
                    total = total + self.buf_z[par, k, rr].astype(jnp.float32)
                self.stage[rr] = total
                return carry
            lax.fori_loop(0, 96 // TILE, one, 0)
        self.out_copy(pack).start()
        self.sent(pack, R_V, R_COUNT)

        @pl.when(pack + 2 < self.packs)
        def _():
            z, x, y, c = self.z, self.x, self.y, self.c
            for t in (self.xn, self.yn) + tuple(((z + k) % 4, x, y, c) for k in (1, 2, 3)):
                self.free(pack, 1, t)

    def step(self, s):
        total = 4 * self.packs
        pl.when(s < total)(lambda: self.core(s // 4, (s % 4 + 1) % 4))

        @pl.when((s >= 2) & (s <= total + 1))
        def _():
            before = (s + 2) // 4 - 1
            k = (s + 3) % 4
            self.vees(before, k)
            pl.when(k == 0)(lambda: self.near(before))

        @pl.when((s >= 4) & (s <= total + 3))
        def _():
            before = s // 4 - 1
            k = (s % 4 + 1) % 4
            pl.when(k > 0)(lambda: self.yous(before, k))
            pl.when(k == 0)(lambda: self.final(before))

        more = s + 2
        if not isinstance(s, int):
            pl.when(more < total)(lambda: self.ahead(more))
        elif more < total:
            self.ahead(jnp.int32(more))
        later = s // 4 + 1
        pl.when((s % 4 == 3) & (later < self.packs))(lambda: self.load(later))

    def finish(self):
        self.out_copy(self.packs - 1).wait()
        for pack in (self.packs - 2, self.packs - 1):
            self.sent(pack, R_C, R_V)


def scatter_scratch(packs):
    bf = jnp.bfloat16
    return [
        pltpu.VMEM((2, 2, 8 * ROWS, LANES), bf),
        pltpu.VMEM((2, 2, 8 * ROWS, LANES), bf),
        pltpu.VMEM((2, 4, 4, 96, LANES), bf),
        pltpu.VMEM((2, 3, 2, 64, LANES), bf),
        pltpu.VMEM((2, 3, 2, 32, LANES), bf),
        pltpu.VMEM((2, 3, 192, LANES), bf),
        pltpu.VMEM((2, 2, 96, LANES), bf),
        pltpu.SemaphoreType.DMA((2, R_COUNT)),
        pltpu.SemaphoreType.DMA((2, R_COUNT)),
        pltpu.SemaphoreType.DMA((2,)),
        pltpu.SemaphoreType.REGULAR((packs, 2)),
        pltpu.VMEM((ROWS, LANES), jnp.float32),
        pltpu.SemaphoreType.DMA,
    ]


BF = jnp.bfloat16
F32 = jnp.float32
CHUNK = 256


def gain_rows(table, line, into):
    lines = [None] * 13
    for i in range(32):
        first = (48 * i) // 128
        for j in range(2):
            got = table[i, line + j : line + j + 1, :]
            lines[first + j] = got if lines[first + j] is None else lines[first + j] + got
    for r in range(12):
        into[:, 128 * r : 128 * (r + 1)] = lines[r]


def loop(count, body):
    def one(t, carry):
        body(t)
        return carry

    lax.fori_loop(0, count, one, 0)


def tile_rows(t, size):
    return pl.ds(pl.multiple_of(t * size, size), size)


def norm_rows(src, gain, into, tokens):
    def one(t):
        r = tile_rows(t, 32)
        v = src[r].astype(F32)
        scale = lax.rsqrt(jnp.mean(v * v, axis=-1, keepdims=True) + EPS)
        into[r] = (v * scale * gain[...]).astype(BF)

    loop(tokens // 32, one)


def turn(src, into, tokens):
    def one(t):
        r = tile_rows(t, 128)
        into[:, r] = jnp.transpose(src[r])

    loop(tokens // 128, one)


def gelu_parts(u):
    root = 0.7978845608028654
    t = jnp.tanh(root * (u + 0.044715 * (u * u * u)))
    return 0.5 * u * (1.0 + t), t


def nt(a, b):
    return lax.dot_general(a, b, (((1,), (1,)), ((), ())), preferred_element_type=F32)


def tn(a, b):
    return lax.dot_general(a, b, (((0,), (0,)), ((), ())), preferred_element_type=F32)


def nn(a, b):
    return jnp.dot(a, b, preferred_element_type=F32)


def forward_kernel(
    packs, tokens, width, seq, heads, scale,
    own, tile, x_any, teacher_any, cotangent_any, buckets, bias_smem, blocks_row, blocks_col, valid_row, valid_col,
    whole, table, n1_out, n2_out, qkv_out, probs_out, pre_out, act_out, middle_out, layer_out, grad_out, gffn_out, loss_out,
    x, n1, n2, turned, acc, bias, mask, wbuf, qs, ps, pre, act, tabv, gain1, gain2, teach, cot, lossv,
    send, recv, local, tile_send, tile_recv, tile_local, in_sem, w_sem, p_sem, q_sem, pre_sem, act_sem, out_sem,
):
    f = lax.axis_index("fsdp")
    d = lax.axis_index("dp")
    micro = tokens // seq
    per = heads // 4
    size = 192 // per
    start_barrier()
    g = Gather(own, whole, send, recv, packs)
    g.launch(0)
    tiles = exchange(lambda other: tile, table, tile_send, tile_recv)
    tile_keep = pltpu.make_async_copy(tile, table.at[f * 4 + d], tile_local)
    tile_keep.start()
    bounce = [
        pltpu.make_async_copy(own.at[:, pl.ds(p * LANES, LANES)], wbuf.at[1, pl.ds(p * ROWS, ROWS)], local.at[p])
        for p in range(packs)
    ]
    keep = [
        pltpu.make_async_copy(
            wbuf.at[1, pl.ds(p * ROWS, ROWS)],
            whole.at[d, pl.ds(pl.multiple_of(f * ROWS, ROWS), ROWS), pl.ds(p * LANES, LANES)],
            local.at[p],
        )
        for p in range(packs)
    ]
    for r in bounce:
        r.start()
    load_x = pltpu.make_async_copy(x_any, x, in_sem.at[0])
    load_x.start()
    g.step(0)
    for a, b in zip(bounce, keep):
        a.wait()
        b.start()
    rows_i = lax.broadcasted_iota(jnp.int32, (seq, seq), 0)
    cols_i = lax.broadcasted_iota(jnp.int32, (seq, seq), 1)
    for m in range(micro):
        ok = (blocks_row[m : m + 1, :] <= blocks_col[m * seq : (m + 1) * seq, :]) & (valid_row[m : m + 1, :] == 1)
        mask[m] = jnp.where(ok | (rows_i == cols_i), 1.0, 0.0)

    def bias_tile(t):
        r = tile_rows(t, 8)
        b = buckets[r]
        totals = [jnp.zeros((8, seq), F32)] * heads
        for k in range(32):
            here = b == k
            totals = [jnp.where(here, bias_smem[k, h], v) for h, v in enumerate(totals)]
        for h in range(heads):
            bias[h, r] = totals[h]

    step_tiles = -(-(seq // 8) // 7)

    def early(s):
        def some(i):
            t = s * step_tiles + i
            pl.when(t < seq // 8)(lambda: bias_tile(t))

        loop(step_tiles, some)
        g.step(s + 1)

    loop(7, early)
    tile_keep.wait()
    tiles.wait()
    load_table = pltpu.make_async_copy(table, tabv, in_sem.at[1])
    load_table.start()
    load_x.wait()
    load_table.wait()
    gain_rows(tabv, 0, gain1)
    gain_rows(tabv, 2, gain2)
    load_t = pltpu.make_async_copy(teacher_any, teach, in_sem.at[2])
    load_t.start()
    load_c = pltpu.make_async_copy(cotangent_any, cot, in_sem.at[3])
    load_c.start()
    norm_rows(x, gain1, n1, tokens)

    def copy_x(t):
        r = tile_rows(t, 32)
        acc[r] = x[r].astype(F32)

    loop(tokens // 32, copy_x)
    turn(n1, turned, tokens)
    n1_copy = pltpu.make_async_copy(turned, n1_out, out_sem.at[0])
    n1_copy.start()
    for r in keep:
        r.wait()
    g.arrived(0)

    def load_w(i, slot):
        return pltpu.make_async_copy(
            whole.at[i % 4, :, lanes_of(i // 4)], wbuf.at[slot], w_sem.at[slot]
        )

    load_w(0, 0).start()

    def probs_copy(dd, m, slot):
        return pltpu.make_async_copy(ps.at[slot], probs_out.at[dd * micro + m], p_sem.at[slot])

    def attention(dd):
        slot = dd % 2
        pl.when(dd < 3)(lambda: load_w(dd + 1, 1 - slot).start())
        load_w(dd, slot).wait()
        pl.when(dd > 0)(lambda: pltpu.make_async_copy(qs, qkv_out.at[dd], q_sem).wait())
        qs[:, 0:576] = nn(n1[...], wbuf[slot, :, 0:576]).astype(BF)
        g.step(8 + 2 * dd)
        for m in range(micro):
            r = slice(m * seq, (m + 1) * seq)
            pl.when(dd > 0)(lambda: probs_copy(dd, m, m).wait())
            for hh in range(per):
                a = hh * size
                s = nt(qs[r, a : a + size], qs[r, 192 + a : 192 + a + size]) + bias[dd * per + hh]
                s = jnp.where(mask[m] > 0.0, s, NEG)
                top = jnp.max(s, axis=-1, keepdims=True)
                e = jnp.exp(s - top)
                p = e * (1.0 / jnp.sum(e, axis=-1, keepdims=True))
                ps[m, hh] = p
                qs[r, 576 + a : 576 + a + size] = nn(p.astype(BF), qs[r, 384 + a : 384 + a + size]).astype(BF)
            probs_copy(dd, m, m).start()
        g.step(9 + 2 * dd)
        for m in range(micro):
            r = slice(m * seq, (m + 1) * seq)
            acc[r] += nt(qs[r, 576:768], wbuf[slot, :, 576:768])
        pltpu.make_async_copy(qs, qkv_out.at[dd], q_sem).start()

    loop(4, attention)
    pltpu.make_async_copy(qs, qkv_out.at[0], q_sem).wait()
    for m in range(micro):
        probs_copy(3, m, m).wait()
    mid_copy = pltpu.make_async_copy(acc, middle_out, out_sem.at[1])
    mid_copy.start()
    norm_rows(acc, gain2, n2, tokens)
    n1_copy.wait()
    turn(n2, turned, tokens)
    n2_copy = pltpu.make_async_copy(turned, n2_out, out_sem.at[2])
    n2_copy.start()
    mid_copy.wait()

    def pre_copy(t, slot):
        return pltpu.make_async_copy(pre.at[slot], pre_out.at[t], pre_sem.at[slot])

    def act_copy(t, slot):
        return pltpu.make_async_copy(act.at[slot], act_out.at[t], act_sem.at[slot])

    def feed(t):
        slot = t % 2

        @pl.when(t % 4 == 0)
        def _():
            g.arrived(1 + t // 4)
            load_w(4 + t, slot).start()

        pl.when(t % 4 < 3)(lambda: load_w(5 + t, 1 - slot).start())
        load_w(4 + t, slot).wait()

        @pl.when(t > 1)
        def _():
            pre_copy(t, slot).wait()
            act_copy(t, slot).wait()

        for m in range(micro):
            r = slice(m * seq, (m + 1) * seq)
            gu = nn(n2[r], wbuf[slot, :, 0 : 2 * CHUNK])
            pre[slot, r] = gu
            ge, _ = gelu_parts(gu[:, 0:CHUNK])
            act[slot, r] = (ge * gu[:, CHUNK:]).astype(BF)
        pre_copy(t, slot).start()
        act_copy(t, slot).start()

        @pl.when(t < 8)
        def _():
            pl.when(t % 2 == 1)(lambda: g.step(16 + t // 2))

        pl.when((t >= 8) & (t < 12))(lambda: g.step(12 + t))
        for m in range(micro):
            r = slice(m * seq, (m + 1) * seq)
            acc[r] += nt(act[slot, r], wbuf[slot, :, 2 * CHUNK :])

    loop(16, feed)
    load_t.wait()
    load_c.wait()
    n2_copy.wait()
    for slot in range(2):
        pre_copy(14 + slot, slot).wait()
        act_copy(14 + slot, slot).wait()
    total = tabv[0, 4:5, 0:1]
    for i in range(1, 32):
        total = total + tabv[i, 4:5, 0:1]
    factor = (2.0 * scale / width) / total
    lossv[...] = jnp.zeros_like(lossv)

    def ends(t):
        r = tile_rows(t, 16)
        full = acc[r]
        gap = full - teach[r].astype(F32)
        weighted = valid_col[r] * gap
        grad = scale * cot[r].astype(F32) + factor * weighted
        acc[r] = grad
        x[r] = grad.astype(BF)
        n1[r] = full.astype(BF)
        lossv[...] += weighted * gap

    loop(tokens // 16, ends)
    copies = [
        pltpu.make_async_copy(n1, layer_out, out_sem.at[0]),
        pltpu.make_async_copy(acc, grad_out, out_sem.at[1]),
        pltpu.make_async_copy(x, gffn_out, out_sem.at[2]),
    ]
    for r in copies:
        r.start()
    loss_out[...] = jnp.zeros_like(loss_out) + jnp.sum(lossv[...])
    g.finish()
    for r in copies:
        r.wait()


def forward(own, tile, x, teacher, cotangent, buckets, bias_table, blocks_row, blocks_col, valid_row, valid_col, scale):
    packs = own.shape[1] // LANES
    tokens, width = x.shape
    seq = buckets.shape[0]
    heads = bias_table.shape[1]
    micro = tokens // seq
    any_ = pl.BlockSpec(memory_space=pl.ANY)
    vmem = pl.BlockSpec(memory_space=pltpu.VMEM)
    smem = pl.BlockSpec(memory_space=pltpu.SMEM)
    S = jax.ShapeDtypeStruct
    dma = pltpu.SemaphoreType.DMA
    outs = (
        S((4, 8 * ROWS, own.shape[1]), BF), S((32, 8, 128), F32), S((width, tokens), BF), S((width, tokens), BF),
        S((4, tokens, 768), BF), S((4 * micro, heads // 4, seq, seq), F32), S((16, tokens, 2 * CHUNK), F32),
        S((16, tokens, CHUNK), BF), S((tokens, width), F32), S((tokens, width), BF), S((tokens, width), F32), S((tokens, width), BF), S((8, 128), F32),
    )
    return pl.pallas_call(
        functools.partial(forward_kernel, packs, tokens, width, seq, heads, scale),
        out_shape=outs,
        in_specs=[any_] * 5 + [vmem, smem] + [vmem] * 4,
        out_specs=[any_] * 12 + [vmem],
        scratch_shapes=[
            pltpu.VMEM((tokens, width), BF), pltpu.VMEM((tokens, width), BF), pltpu.VMEM((tokens, width), BF),
            pltpu.VMEM((width, tokens), BF), pltpu.VMEM((tokens, width), F32), pltpu.VMEM((heads, seq, seq), F32), pltpu.VMEM((micro, seq, seq), F32),
            pltpu.VMEM((2, 8 * ROWS, LANES), BF), pltpu.VMEM((tokens, 768), BF), pltpu.VMEM((micro, heads // 4, seq, seq), F32),
            pltpu.VMEM((2, tokens, 2 * CHUNK), F32), pltpu.VMEM((2, tokens, CHUNK), BF), pltpu.VMEM((32, 8, 128), F32),
            pltpu.VMEM((1, width), F32), pltpu.VMEM((1, width), F32), pltpu.VMEM((tokens, width), BF),
            pltpu.VMEM((tokens, width), BF), pltpu.VMEM((16, width), F32),
            dma((packs, G_COUNT)), dma((packs, G_COUNT)), dma((packs,)), dma, dma, dma, dma((4,)), dma((2,)), dma((2,)), dma,
            dma((2,)), dma((2,)), dma((3,)),
        ],
        compiler_params=pltpu.CompilerParams(collective_id=1, has_side_effects=True, vmem_limit_bytes=63 * 1024 * 1024),
    )(own, tile, x, teacher, cotangent, buckets, bias_table, blocks_row, blocks_col, valid_row, valid_col)


def prepare(weights, gain_one, gain_two, valid):
    part = weights[4].shape[1]
    pads = [jnp.pad(w, ((0, 0), (0, 4 * CHUNK - part))) for w in weights[4:]]
    pieces = list(weights[:4])
    for j in range(4):
        pieces += [w[:, j * CHUNK : (j + 1) * CHUNK] for w in pads]
    own = jnp.concatenate(pieces, axis=1)
    me = lax.axis_index("fsdp") * 4 + lax.axis_index("dp")
    first = (me * 48) % 128

    def lines(gain):
        return lax.dynamic_update_slice(jnp.zeros((256,), F32), gain.astype(F32), (first,)).reshape(2, 128)

    count = jnp.zeros((4, 128), F32) + jnp.sum(valid.astype(F32))
    return own, jnp.concatenate([lines(gain_one), lines(gain_two), count])


def gelu_slope(u, t):
    root = 0.7978845608028654
    return 0.5 * (1.0 + t) + 0.5 * u * (1.0 - t * t) * root * (1.0 + 3.0 * 0.044715 * (u * u))


def norm_back(src_row, up_row, gain, gain_sum):
    v, u = src_row, up_row
    scale = lax.rsqrt(jnp.mean(v * v, axis=-1, keepdims=True) + EPS)
    scaled = u * gain
    mean = jnp.mean(scaled * v, axis=-1, keepdims=True)
    term = u * v * scale
    total = term[0:8]
    for i in range(1, term.shape[0] // 8):
        total = total + term[8 * i : 8 * i + 8]
    gain_sum[...] += total
    return scale * scaled - v * (scale * scale * scale) * mean


def backward_kernel(
    packs, tokens, width, seq, heads,
    whole, table, x_any, n1_any, n2_any, qkv_any, probs_any, pre_any, act_any, mid_any, gout_any, gffn_any, buckets, loss,
    part, out, hidden_out, tiles_out, sums_out, gs_out,
    low, src, acc, acc2, wbuf, pre, act, ggu, gst, strm, qs, ps, ga, gqkv, bsum, gain1, gain2, sum1, sum2, tilev, tabv,
    in_sem, w_sem, pre_sem, act_sem, g_sem, s_sem, q_sem, p_sem, out2_sem, gs_sem, tile_send, tile_recv, tile_local, *scatter_refs,
):
    micro = tokens // seq
    per = heads // 4
    size = 192 // per
    me = lax.axis_index("fsdp") * 4 + lax.axis_index("dp")
    tell_all()
    rs = Scatter(part, out, *scatter_refs, packs)

    def fetch(a, b, sem):
        r = pltpu.make_async_copy(a, b, sem)
        r.start()
        return r

    mid_load = fetch(mid_any, acc2, in_sem.at[3])
    loads = [fetch(gffn_any, low, in_sem.at[0]), fetch(n2_any, src, in_sem.at[1]), fetch(table, tabv, in_sem.at[2])]

    def load_w(i, slot):
        return pltpu.make_async_copy(whole.at[i % 4, :, lanes_of(i // 4)], wbuf.at[slot], w_sem.at[slot])

    def load_pre(t, slot):
        return pltpu.make_async_copy(pre_any.at[t], pre.at[slot], pre_sem.at[slot])

    def load_act(t, slot):
        return pltpu.make_async_copy(act_any.at[t], act.at[slot], act_sem.at[slot])

    def put_g(dd, lane_pack):
        return pltpu.make_async_copy(gst, part.at[dd, :, lanes_of(lane_pack)], g_sem)

    for r in (load_w(4, 0), load_pre(0, 0), load_act(0, 0)):
        r.start()
    sum1[...] = jnp.zeros_like(sum1)
    sum2[...] = jnp.zeros_like(sum2)

    def clear(t):
        r = tile_rows(t, 32)
        acc[r] = jnp.zeros((32, width), F32)

    loop(tokens // 32, clear)
    for r in loads:
        r.wait()
    gain_rows(tabv, 0, gain1)
    gain_rows(tabv, 2, gain2)
    half = width // 2

    def feed(t):
        slot = t % 2

        @pl.when(t < 15)
        def _():
            load_w(5 + t, 1 - slot).start()
            load_pre(t + 1, 1 - slot).start()
            load_act(t + 1, 1 - slot).start()

        load_w(4 + t, slot).wait()
        load_pre(t, slot).wait()
        load_act(t, slot).wait()
        for m in range(micro):
            r = slice(m * seq, (m + 1) * seq)
            gh = nn(low[r], wbuf[slot, :, 2 * CHUNK :])
            u = pre[slot, r, 0:CHUNK]
            ge, th = gelu_parts(u)
            ggu[r, 0:CHUNK] = (gh * pre[slot, r, CHUNK:] * gelu_slope(u, th)).astype(BF)
            ggu[r, CHUNK:] = (gh * ge).astype(BF)
        pl.when((t > 0) & (t != 4))(lambda: put_g(0, 0).wait())
        for h in range(2):
            c = slice(h * half, (h + 1) * half)
            gst[c, 0 : 2 * CHUNK] = nn(src[c], ggu[...]).astype(BF)
            gst[c, 2 * CHUNK :] = tn(low[:, c], act[slot]).astype(BF)
        put_g(t % 4, 1 + t // 4).start()
        for m in range(micro):
            r = slice(m * seq, (m + 1) * seq)
            acc[r] += nt(ggu[r], wbuf[slot, :, 0 : 2 * CHUNK])

        @pl.when(t == 3)
        def _():
            put_g(0, 0).wait()
            hear_all()
            rs.launch()

        pl.when((t == 4) | (t == 6))(lambda: rs.step(t // 2 - 2))
        pl.when(t >= 8)(lambda: rs.step(t - 6))

    loop(16, feed)
    put_g(0, 0).wait()
    n1_load = fetch(n1_any, src, in_sem.at[1])
    load_w(0, 0).start()

    def strm_load(t, slot):
        return pltpu.make_async_copy(gout_any.at[tile_rows(t, 128)], strm.at[slot], s_sem.at[slot])

    def probs_load(dd, m):
        return pltpu.make_async_copy(probs_any.at[dd * micro + m], ps.at[m], p_sem.at[m])

    def q_load(dd):
        return pltpu.make_async_copy(qkv_any.at[dd], qs, q_sem)

    strm_load(0, 0).start()
    q_load(0).start()
    for m in range(micro):
        probs_load(0, m).start()
    mid_load.wait()

    def norm_two(block):
        slot = block % 2
        pl.when(block + 1 < tokens // 128)(lambda: strm_load(block + 1, 1 - slot).start())
        strm_load(block, slot).wait()

        def some(t):
            r = tile_rows(block * 4 + t, 32)
            grad = strm[slot, tile_rows(t, 32)] + norm_back(acc2[r], acc[r], gain2[...], sum2)
            acc[r] = grad
            acc2[r] = jnp.zeros((32, width), F32)
            low[r] = grad.astype(BF)

        loop(4, some)

    loop(tokens // 128, norm_two)
    n1_load.wait()
    rs.step(10)

    def gs_copy(dd):
        return pltpu.make_async_copy(ps.at[micro - 1], gs_out.at[dd], gs_sem.at[0])

    def gs_load(dd):
        return pltpu.make_async_copy(gs_out.at[dd], ps.at[dd % 2], gs_sem.at[dd % 2])

    def attention(dd):
        slot = dd % 2
        pl.when(dd < 3)(lambda: load_w(dd + 1, 1 - slot).start())
        load_w(dd, slot).wait()
        ga[...] = nn(low[...], wbuf[slot, :, 576:768]).astype(BF)
        q_load(dd).wait()

        @pl.when(dd > 0)
        def _():
            gs_copy(dd).wait()
            probs_load(dd, micro - 1).start()
            put_g(0, 0).wait()

        gst[:, 576:768] = tn(low[...], qs[:, 576:768]).astype(BF)
        for m in range(micro):
            r = slice(m * seq, (m + 1) * seq)
            probs_load(dd, m).wait()
            for hh in range(per):
                a = hh * size
                p = ps[m, hh]
                go = ga[r, a : a + size]
                gp = nt(go, qs[r, 384 + a : 384 + a + size])
                gs = p * (gp - jnp.sum(p * gp, axis=-1, keepdims=True))
                gs = gs.astype(BF)
                gqkv[r, a : a + size] = nn(gs, qs[r, 192 + a : 192 + a + size]).astype(BF)
                gqkv[r, 192 + a : 192 + a + size] = tn(gs, qs[r, a : a + size]).astype(BF)
                gqkv[r, 384 + a : 384 + a + size] = tn(p.astype(BF), go).astype(BF)
                ps[m, hh] = gs.astype(F32) if m == 0 else ps[m - 1, hh] + gs.astype(F32)
        gs_copy(dd).start()

        @pl.when(dd < 3)
        def _():
            q_load(dd + 1).start()
            probs_load(dd + 1, 0).start()

        pl.when(dd < 3)(lambda: rs.step(11 + dd))
        for h in range(2):
            c = slice(h * half, (h + 1) * half)
            gst[c, 0:576] = nn(src[c], gqkv[...]).astype(BF)
        put_g(dd, 0).start()
        for m in range(micro):
            r = slice(m * seq, (m + 1) * seq)
            acc2[r] += nt(gqkv[r], wbuf[slot, :, 0:576])


    loop(4, attention)
    put_g(0, 0).wait()
    gs_copy(0).wait()
    rs.step(14)
    gs_load(0).start()
    x_load = fetch(x_any, low, in_sem.at[1])
    x_load.wait()

    def norm_one(t):
        r = tile_rows(t, 32)
        term = norm_back(low[r].astype(F32), acc2[r], gain1[...], sum1)
        low[r] = (acc[r] + term).astype(BF)

    loop(tokens // 32, norm_one)
    hidden_copy = fetch(low, hidden_out, out2_sem)
    rs.step(15)

    def buckets_of(dd):
        gs_load(dd).wait()
        pl.when(dd < 3)(lambda: gs_load(dd + 1).start())

        def by_bucket(group):
            def some(t, totals):
                r = tile_rows(t, 8)
                b = buckets[r]
                v = [ps[dd % 2, hh, r] for hh in range(per)]
                new = []
                for j in range(4):
                    here = b == group * 4 + j
                    new += [totals[j * per + hh] + jnp.where(here, v[hh], 0.0) for hh in range(per)]
                return tuple(new)

            totals = lax.fori_loop(0, seq // 8, some, (jnp.zeros((8, seq), F32),) * (4 * per))
            for j in range(4):
                for hh in range(per):
                    bsum[dd * per + hh, pl.ds(group * 4 + j, 1)] = jnp.sum(totals[j * per + hh], axis=0, keepdims=True)

        loop(8, by_bucket)
        rs.step(16 + dd)

    loop(4, buckets_of)
    one = jnp.sum(sum1[...], axis=0, keepdims=True)
    two = jnp.sum(sum2[...], axis=0, keepdims=True)
    biases = lax.dot_general(
        jnp.ones((8, seq), F32), bsum[...].reshape(heads * 32, seq), (((1,), (1,)), ((), ())),
        precision=lax.Precision.HIGHEST, preferred_element_type=F32,
    )
    lines = [biases[0:1, 128 * i : 128 * (i + 1)] for i in range(3)]
    none = jnp.zeros((1, 128), F32)
    for i in range(32):
        first = 128 * ((48 * i) // 128)
        rows = []
        for v in (one, two):
            rows.append(v[:, first : first + 128])
            rows.append(v[:, first + 128 : first + 256] if first + 128 < width else none)
        tilev[i] = jnp.concatenate(rows + [loss[0:1, :]] + lines, axis=0)
    tile_copy = fetch(tilev, tiles_out, in_sem.at[0])
    tile_copy.wait()
    tiles = exchange(lambda other: tiles_out.at[other], sums_out, tile_send, tile_recv)
    tile_keep = fetch(tilev.at[me], sums_out.at[me], tile_local)
    lax.fori_loop(20, 4 * packs + 4, lambda s, carry: (rs.step(s), carry)[1], 0)
    rs.finish()
    hidden_copy.wait()
    tile_keep.wait()
    tiles.wait()


def backward(whole, table, x, n1, n2, qkv, probs, pre, act, mid, gout, gffn, buckets, loss, heads):
    packs = whole.shape[2] // LANES
    tokens, width = x.shape
    seq = buckets.shape[0]
    micro = tokens // seq
    any_ = pl.BlockSpec(memory_space=pl.ANY)
    vmem = pl.BlockSpec(memory_space=pltpu.VMEM)
    S = jax.ShapeDtypeStruct
    V = pltpu.VMEM
    dma = pltpu.SemaphoreType.DMA
    outs = (
        S(whole.shape, BF), S((ROWS, whole.shape[2]), F32), S((tokens, width), BF), S((32, 8, 128), F32), S((32, 8, 128), F32),
        S((4, heads // 4, seq, seq), F32),
    )
    return pl.pallas_call(
        functools.partial(backward_kernel, packs, tokens, width, seq, heads),
        out_shape=outs,
        in_specs=[any_] * 12 + [vmem] * 2,
        out_specs=[any_] * 6,
        scratch_shapes=[
            V((tokens, width), BF), V((width, tokens), BF), V((tokens, width), F32), V((tokens, width), F32),
            V((2, 8 * ROWS, LANES), BF), V((2, tokens, 2 * CHUNK), F32), V((2, tokens, CHUNK), BF), V((tokens, 2 * CHUNK), BF),
            V((8 * ROWS, LANES), BF), V((2, 128, width), F32), V((tokens, 768), BF), V((micro, heads // 4, seq, seq), F32),
            V((tokens, 192), BF), V((tokens, 576), BF), V((heads, 32, seq), F32), V((1, width), F32), V((1, width), F32),
            V((8, width), F32), V((8, width), F32), V((32, 8, 128), F32), V((32, 8, 128), F32),
            dma((4,)), dma((2,)), dma((2,)), dma((2,)), dma, dma((2,)), dma, dma((micro,)), dma, dma((2,)), dma, dma, dma,
        ] + scatter_scratch(packs),
        compiler_params=pltpu.CompilerParams(collective_id=2, has_side_effects=True, vmem_limit_bytes=67043328),
    )(whole, table, x, n1, n2, qkv, probs, pre, act, mid, gout, gffn, buckets, loss)


def tuned_body(
    hidden, teacher, cotangent, valid_mask, blocks, buckets, first_gain, query_weight, key_weight, value_weight,
    output_weight, second_gain, gate_weight, up_weight, down_weight, bias_table,
):
    micro, _, seq, width = hidden.shape
    tokens = micro * seq
    bucket_count, heads = bias_table.shape
    part = gate_weight.shape[1]
    cols = query_weight.shape[1]
    per = first_gain.shape[0]
    scale = float(tokens * 32 * width)
    valid = valid_mask.reshape(micro, seq)
    block_ids = blocks.reshape(micro, seq)
    weights = (query_weight, key_weight, value_weight, output_weight, gate_weight, up_weight, down_weight)
    own, tile = prepare(weights, first_gain, second_gain, valid)
    x = hidden.reshape(tokens, width)
    whole, table, n1, n2, qkv, probs, pre, act, mid, layer, gout, gffn, loss = forward(
        own, tile, x, teacher.reshape(tokens, width), cotangent.reshape(tokens, width), buckets, bias_table.astype(F32),
        block_ids, block_ids.reshape(tokens, 1), valid, valid.reshape(tokens, 1).astype(F32), scale,
    )
    _, shard, hidden_grad, _, sums, _ = backward(
        whole, table, x, n1, n2, qkv, probs, pre, act, mid, gout, gffn, buckets, loss, heads
    )
    sums = jnp.sum(sums, axis=0)
    me = lax.axis_index("fsdp") * 4 + lax.axis_index("dp")
    first = (me * per) % 128
    gain_one = lax.dynamic_slice(sums[0:2].reshape(256), (first,), (per,))
    gain_two = lax.dynamic_slice(sums[2:4].reshape(256), (first,), (per,))
    valid_total = jnp.sum(table[:, 4, 0])
    ff = [
        jnp.concatenate([shard[:, LANES * (j + 1) + i * CHUNK : LANES * (j + 1) + (i + 1) * CHUNK] for j in range(4)], axis=1)[:, :part]
        for i in range(3)
    ]
    at = [shard[:, i * cols : (i + 1) * cols] for i in range(4)]
    return (
        layer.reshape(hidden.shape),
        sums[4, 0] / (valid_total * width),
        hidden_grad.reshape(hidden.shape),
        gain_one, at[0], at[1], at[2], at[3], gain_two, ff[0], ff[1], ff[2],
        sums[5:8].reshape(heads, bucket_count).T,
    )


def solution(mesh):
    in_specs = (
        P(None, ("fsdp", "dp"), None, None),
        P(None, ("fsdp", "dp"), None, None),
        P(None, ("fsdp", "dp"), None, None),
        P(None, ("fsdp", "dp"), None),
        P(None, ("fsdp", "dp"), None),
        P(),
        P(("fsdp", "dp")),
        P("fsdp", "dp"),
        P("fsdp", "dp"),
        P("fsdp", "dp"),
        P("fsdp", "dp"),
        P(("fsdp", "dp")),
        P("fsdp", "dp"),
        P("fsdp", "dp"),
        P("fsdp", "dp"),
        P(),
    )
    out_specs = (
        P(None, ("fsdp", "dp"), None, None),
        P(),
        P(None, ("fsdp", "dp"), None, None),
        P(("fsdp", "dp")),
        P("fsdp", "dp"),
        P("fsdp", "dp"),
        P("fsdp", "dp"),
        P("fsdp", "dp"),
        P(("fsdp", "dp")),
        P("fsdp", "dp"),
        P("fsdp", "dp"),
        P("fsdp", "dp"),
        P(),
    )
    chosen = tuned_body if dict(mesh.shape) == {"fsdp": 8, "dp": 4} else body
    return jax.shard_map(chosen, mesh=mesh, in_specs=in_specs, out_specs=out_specs, check_vma=False)
```

```python
import functools
import jax
import jax.numpy as jnp
from jax import lax
from jax.experimental import pallas as pl
from jax.experimental.pallas import tpu as pltpu
from jax.sharding import PartitionSpec as P

EPS = 1e-06
NEG = -1000000000.0
HIGH = lax.Precision.HIGHEST


def times_rows(former, latter):
    return jnp.dot(former, latter, preferred_element_type=jnp.float32)


def times_transpose(former, latter):
    return lax.dot_general(
        former, latter, (((1,), (1,)), ((), ())), preferred_element_type=jnp.float32
    )


def over_tokens(former, latter):
    return lax.dot_general(
        former, latter, (((0,), (0,)), ((), ())), preferred_element_type=jnp.float32
    )


def assemble(gathered, fsdp_count, dp_count):
    row_block = gathered.shape[0] // (fsdp_count * dp_count)
    col_block = gathered.shape[1]
    shaped = gathered.reshape(fsdp_count, dp_count, row_block, col_block)
    return jnp.transpose(shaped, (0, 2, 1, 3)).reshape(fsdp_count * row_block, dp_count * col_block)


def disperse(gradient, fsdp_count, dp_count):
    row_block = gradient.shape[0] // fsdp_count
    col_block = gradient.shape[1] // dp_count
    shaped = gradient.reshape(fsdp_count, row_block, dp_count, col_block)
    return jnp.transpose(shaped, (0, 2, 1, 3)).reshape(fsdp_count * dp_count * row_block, col_block)


def norm_forward(inputs, norm_gain):
    row_scale = lax.rsqrt(jnp.mean(inputs * inputs, axis=-1, keepdims=True) + EPS)
    return (inputs * row_scale * norm_gain, row_scale)


def norm_backward(inputs, row_scale, norm_gain, upstream):
    scaled = upstream * norm_gain
    gain_grad = jnp.sum(upstream * inputs * row_scale, axis=0)
    mean_term = jnp.mean(scaled * inputs, axis=-1, keepdims=True)
    return (
        row_scale * scaled - inputs * (row_scale * row_scale * row_scale) * mean_term,
        gain_grad,
    )


def gelu_tanh(values_in):
    return jax.nn.gelu(values_in, approximate=True)


def masked_scores(queries, key_heads, position_bias, allowed):
    products = jnp.einsum("qhd,khd->hqk", queries, key_heads, preferred_element_type=jnp.float32)
    return jnp.where(allowed[None], products + position_bias, NEG)


def body(
    hidden,
    teacher,
    cotangent,
    valid_mask,
    blocks,
    buckets,
    first_gain,
    query_weight,
    key_weight,
    value_weight,
    output_weight,
    second_gain,
    gate_weight,
    up_weight,
    down_weight,
    bias_table,
):
    fsdp_count = lax.axis_size("fsdp")
    dp_count = lax.axis_size("dp")
    micro_count = hidden.shape[0]
    seq_len = hidden.shape[2]
    model_width = hidden.shape[3]
    bucket_count = bias_table.shape[0]
    head_count = bias_table.shape[1]
    scale_factor = jnp.float32(
        float(micro_count * lax.axis_size(("fsdp", "dp")) * hidden.shape[1] * seq_len * model_width)
    )
    valid_float = valid_mask.astype(jnp.float32)
    valid_total = lax.psum(jnp.sum(valid_float), ("fsdp", "dp"))
    places = lax.broadcasted_iota(jnp.int32, (1, 1, bucket_count), 2)
    onehot = (buckets[:, :, None] == places).astype(jnp.float32)
    position_bias = jnp.einsum(
        "qkb,bh->hqk", onehot, bias_table.astype(jnp.float32), precision=HIGH
    )
    onehot_low = onehot.astype(jnp.bfloat16)
    rows_iota = lax.broadcasted_iota(jnp.int32, (seq_len, seq_len), 0)
    cols_iota = lax.broadcasted_iota(jnp.int32, (seq_len, seq_len), 1)
    diagonal = rows_iota == cols_iota

    def rebuild(gathered):
        return (gathered[0],) + tuple(
            (assemble(matrix, fsdp_count, dp_count) for matrix in gathered[1:])
        )

    def spread_out(grads):
        return (
            (grads[0],)
            + tuple((disperse(matrix, fsdp_count, dp_count) for matrix in grads[1:5]))
            + (grads[5],)
            + tuple((disperse(matrix, fsdp_count, dp_count) for matrix in grads[6:]))
        )

    outputs_list = []
    input_grads = []
    squares = jnp.float32(0.0)
    table_grad = jnp.zeros((bucket_count, head_count), jnp.float32)
    totals = None
    for step_index in range(micro_count):
        inputs = hidden[step_index, 0].astype(jnp.float32)
        target = teacher[step_index, 0].astype(jnp.float32)
        upstream = cotangent[step_index, 0].astype(jnp.float32)
        token_valid = valid_float[step_index, 0]
        block_ids = blocks[step_index, 0]
        allowed = (block_ids[None, :] <= block_ids[:, None]) & (
            valid_mask[step_index, 0][None, :] == 1
        ) | diagonal
        first_block = rebuild(
            (
                lax.all_gather(first_gain, ("fsdp", "dp"), axis=0, tiled=True),
                lax.all_gather(query_weight, ("fsdp", "dp"), axis=0, tiled=True),
                lax.all_gather(key_weight, ("fsdp", "dp"), axis=0, tiled=True),
                lax.all_gather(value_weight, ("fsdp", "dp"), axis=0, tiled=True),
                lax.all_gather(output_weight, ("fsdp", "dp"), axis=0, tiled=True),
            )
        )
        gain_one = first_block[0].astype(jnp.float32)
        normed_full, scale_one = norm_forward(inputs, gain_one)
        normed_one = normed_full.astype(jnp.bfloat16)
        head_size = first_block[1].shape[1] // head_count
        head_split = (seq_len, head_count, head_size)
        queries = times_rows(normed_one, first_block[1]).astype(jnp.bfloat16).reshape(head_split)
        key_heads = times_rows(normed_one, first_block[2]).astype(jnp.bfloat16).reshape(head_split)
        value_heads = (
            times_rows(normed_one, first_block[3]).astype(jnp.bfloat16).reshape(head_split)
        )
        scores = masked_scores(queries, key_heads, position_bias, allowed)
        row_max = jnp.max(scores, axis=-1, keepdims=True)
        exponent = jnp.exp(scores - row_max)
        row_total = jnp.sum(exponent, axis=-1, keepdims=True)
        log_total = row_max + jnp.log(row_total)
        softmax_low = (exponent / row_total).astype(jnp.bfloat16)
        attended = jnp.einsum(
            "hqk,khd->qhd", softmax_low, value_heads, preferred_element_type=jnp.float32
        )
        attended = attended.astype(jnp.bfloat16).reshape(seq_len, head_count * head_size)
        middle = inputs + times_transpose(attended, first_block[4])
        second_block = rebuild(
            (
                lax.all_gather(second_gain, ("fsdp", "dp"), axis=0, tiled=True),
                lax.all_gather(gate_weight, ("fsdp", "dp"), axis=0, tiled=True),
                lax.all_gather(up_weight, ("fsdp", "dp"), axis=0, tiled=True),
                lax.all_gather(down_weight, ("fsdp", "dp"), axis=0, tiled=True),
            )
        )
        gain_two = second_block[0].astype(jnp.float32)
        normed_mid, scale_two = norm_forward(middle, gain_two)
        normed_two = normed_mid.astype(jnp.bfloat16)
        gate_pre = times_rows(normed_two, second_block[1])
        up_pre = times_rows(normed_two, second_block[2])
        gate_act, gelu_pullback = jax.vjp(gelu_tanh, gate_pre)
        hidden_act = (gate_act * up_pre).astype(jnp.bfloat16)
        layer_full = middle + times_transpose(hidden_act, second_block[3])
        outputs_list.append(layer_full.astype(jnp.bfloat16))
        residual_gap = layer_full - target
        weighted_gap = token_valid[:, None] * residual_gap
        squares = squares + jnp.sum(weighted_gap * residual_gap)
        grad_out = scale_factor * upstream + scale_factor * (
            2.0 * weighted_gap / (valid_total * model_width)
        )
        back_second = rebuild(
            (
                lax.all_gather(second_gain, ("fsdp", "dp"), axis=0, tiled=True),
                lax.all_gather(gate_weight, ("fsdp", "dp"), axis=0, tiled=True),
                lax.all_gather(up_weight, ("fsdp", "dp"), axis=0, tiled=True),
                lax.all_gather(down_weight, ("fsdp", "dp"), axis=0, tiled=True),
            )
        )
        grad_ffn = grad_out.astype(jnp.bfloat16)
        down_part = over_tokens(grad_ffn, hidden_act)
        grad_hidden_act = times_rows(grad_ffn, back_second[3])
        grad_gate = gelu_pullback(grad_hidden_act * up_pre)[0].astype(jnp.bfloat16)
        grad_up = (grad_hidden_act * gate_act).astype(jnp.bfloat16)
        gate_part = over_tokens(normed_two, grad_gate)
        up_part = over_tokens(normed_two, grad_up)
        grad_normed_two = times_transpose(grad_gate, back_second[1]) + times_transpose(
            grad_up, back_second[2]
        )
        middle_term, gain_two_part = norm_backward(
            middle, scale_two, back_second[0].astype(jnp.float32), grad_normed_two
        )
        grad_middle = grad_out + middle_term
        grad_attn = grad_middle.astype(jnp.bfloat16)
        back_first = rebuild(
            (
                lax.all_gather(first_gain, ("fsdp", "dp"), axis=0, tiled=True),
                lax.all_gather(query_weight, ("fsdp", "dp"), axis=0, tiled=True),
                lax.all_gather(key_weight, ("fsdp", "dp"), axis=0, tiled=True),
                lax.all_gather(value_weight, ("fsdp", "dp"), axis=0, tiled=True),
                lax.all_gather(output_weight, ("fsdp", "dp"), axis=0, tiled=True),
            )
        )
        output_part = over_tokens(grad_attn, attended)
        grad_attended = (
            times_rows(grad_attn, back_first[4]).astype(jnp.bfloat16).reshape(head_split)
        )
        scores_again = masked_scores(queries, key_heads, position_bias, allowed)
        softmax_again = jnp.exp(scores_again - log_total)
        grad_probs = jnp.einsum(
            "qhd,khd->hqk", grad_attended, value_heads, preferred_element_type=jnp.float32
        )
        grad_scores = softmax_again * (
            grad_probs - jnp.sum(softmax_again * grad_probs, axis=-1, keepdims=True)
        )
        grad_scores = grad_scores.astype(jnp.bfloat16)
        table_grad = table_grad + jnp.einsum(
            "hqk,qkb->bh", grad_scores, onehot_low, preferred_element_type=jnp.float32
        )
        flat_width = head_count * head_size
        grad_queries = (
            jnp.einsum("hqk,khd->qhd", grad_scores, key_heads, preferred_element_type=jnp.float32)
            .astype(jnp.bfloat16)
            .reshape(seq_len, flat_width)
        )
        grad_keys = (
            jnp.einsum("hqk,qhd->khd", grad_scores, queries, preferred_element_type=jnp.float32)
            .astype(jnp.bfloat16)
            .reshape(seq_len, flat_width)
        )
        grad_values = (
            jnp.einsum(
                "hqk,qhd->khd",
                softmax_again.astype(jnp.bfloat16),
                grad_attended,
                preferred_element_type=jnp.float32,
            )
            .astype(jnp.bfloat16)
            .reshape(seq_len, flat_width)
        )
        query_part = over_tokens(normed_one, grad_queries)
        key_part = over_tokens(normed_one, grad_keys)
        value_part = over_tokens(normed_one, grad_values)
        grad_normed_one = (
            times_transpose(grad_queries, back_first[1])
            + times_transpose(grad_keys, back_first[2])
            + times_transpose(grad_values, back_first[3])
        )
        input_term, gain_one_part = norm_backward(
            inputs, scale_one, back_first[0].astype(jnp.float32), grad_normed_one
        )
        input_grads.append((grad_middle + input_term).astype(jnp.bfloat16))
        step_set = spread_out(
            (
                gain_one_part,
                query_part,
                key_part,
                value_part,
                output_part,
                gain_two_part,
                gate_part,
                up_part,
                down_part,
            )
        )
        totals = step_set if totals is None else jax.tree.map(jnp.add, totals, step_set)
    shards = (
        lax.psum_scatter(totals[0], ("fsdp", "dp"), scatter_dimension=0, tiled=True),
        lax.psum_scatter(totals[1], ("fsdp", "dp"), scatter_dimension=0, tiled=True),
        lax.psum_scatter(totals[2], ("fsdp", "dp"), scatter_dimension=0, tiled=True),
        lax.psum_scatter(totals[3], ("fsdp", "dp"), scatter_dimension=0, tiled=True),
        lax.psum_scatter(totals[4], ("fsdp", "dp"), scatter_dimension=0, tiled=True),
        lax.psum_scatter(totals[5], ("fsdp", "dp"), scatter_dimension=0, tiled=True),
        lax.psum_scatter(totals[6], ("fsdp", "dp"), scatter_dimension=0, tiled=True),
        lax.psum_scatter(totals[7], ("fsdp", "dp"), scatter_dimension=0, tiled=True),
        lax.psum_scatter(totals[8], ("fsdp", "dp"), scatter_dimension=0, tiled=True),
    )
    total_squares, table_all = lax.psum((squares, table_grad), ("fsdp", "dp"))
    loss_value = total_squares / (valid_total * model_width)
    layer_output = jnp.stack(outputs_list)[:, None]
    hidden_grad = jnp.stack(input_grads)[:, None]
    return (
        layer_output,
        loss_value,
        hidden_grad,
        shards[0],
        shards[1],
        shards[2],
        shards[3],
        shards[4],
        shards[5],
        shards[6],
        shards[7],
        shards[8],
        table_all,
    )


MESH_ID = pl.DeviceIdType.MESH
LANES = 768
ROWS = 192


def place():
    f = lax.axis_index("fsdp")
    d = lax.axis_index("dp")
    return f // 2, f % 2, d // 2, d % 2


def device(z, x, y, c):
    return (z * 2 + x, y * 2 + c)


def tell_all():
    f = lax.axis_index("fsdp")
    d = lax.axis_index("dp")
    barrier = pltpu.get_barrier_semaphore()

    def tell(step, carry):
        other = (f * 4 + d + step) % 32
        pl.semaphore_signal(
            barrier, inc=1, device_id=(other // 4, other % 4), device_id_type=MESH_ID
        )
        return carry

    lax.fori_loop(1, 32, tell, 0)


def hear_all():
    pl.semaphore_wait(pltpu.get_barrier_semaphore(), 31)


def start_barrier():
    tell_all()
    hear_all()


def exchange(tile_of, table, send, recv):
    f = lax.axis_index("fsdp")
    d = lax.axis_index("dp")
    me = f * 4 + d

    def one(step, carry):
        other = (me + step) % 32
        pltpu.make_async_remote_copy(
            tile_of(other), table.at[me], send, recv,
            device_id=(other // 4, other % 4), device_id_type=MESH_ID,
        ).start()
        return carry

    lax.fori_loop(1, 32, one, 0)
    view = table.at[pl.ds(0, 31)]
    return pltpu.make_async_remote_copy(
        view, view, send, recv, device_id=(f, (d + 1) % 4), device_id_type=MESH_ID
    )


def lanes_of(pack):
    return pl.ds(pl.multiple_of(pack * LANES, 128), LANES)


def rows_of(z, x, first, count):
    return pl.ds(pl.multiple_of((z * 2 + x) * ROWS + first, 32), count)


G_Z, G_X0, G_Y0, G_XZ, G_YZ, G_DY, G_DX = 0, 4, 5, 6, 10, 14, 18
G_XA, G_XB, G_YA, G_YB, G_C, G_BACK = 22, 25, 28, 31, 34, 50
G_COUNT = 53


def on_chain(z, k):
    end = (3 - z) // 3 + z // 3
    low = end * k + (1 - end) * (k - (3 - k) // 2)
    high = z // 2
    return high * (3 - low) + (1 - high) * low


class Gather:
    def __init__(self, own, whole, send, recv, packs):
        self.own, self.whole, self.send, self.recv, self.packs = own, whole, send, recv, packs
        self.z, self.x, self.y, self.c = place()

    def put(self, pack, slot, shard, first, count, target, own=False, send=None):
        zz, xx, yy = shard
        there = self.whole.at[yy * 2 + self.c, rows_of(zz, xx, first, count), lanes_of(pack)]
        here = self.own.at[pl.ds(first, count), lanes_of(pack)] if own else there
        pltpu.make_async_remote_copy(
            here, there, self.send.at[pack, slot if send is None else send], self.recv.at[pack, slot],
            device_id=device(*target), device_id_type=MESH_ID,
        ).start()

    def along(self, pack, slot, back, shard, first, count, own=False):
        z, x, y, c = self.z, self.x, self.y, self.c
        pl.when(z < 3)(lambda: self.put(pack, slot + z, shard, first, count, (z + 1, x, y, c), own=own))
        pl.when(z > 0)(lambda: self.put(pack, slot + z, shard, first, count, (z - 1, x, y, c), own=own, send=back))

    def further(self, pack, slot, shard, first, count):
        z, x, y, c = self.z, self.x, self.y, self.c
        zz = shard[0]
        pl.when((zz < z) & (z < 3))(lambda: self.put(pack, slot + zz, shard, first, count, (z + 1, x, y, c)))
        pl.when((zz > z) & (z > 0))(lambda: self.put(pack, slot + zz, shard, first, count, (z - 1, x, y, c)))

    def some(self, pack, slot, count):
        view = self.whole.at[0, pl.ds(0, count), lanes_of(pack)]
        return pltpu.make_async_remote_copy(
            view, view, self.send.at[pack, slot], self.recv.at[pack, slot],
            device_id=device(self.z, self.x, self.y, 1 - self.c), device_id_type=MESH_ID,
        )

    def got(self, pack, slot, count):
        self.some(pack, slot, count).wait_recv()

    def launch(self, pack):
        self.along(pack, G_Z, G_BACK, (self.z, self.x, self.y), 0, 192, own=True)

    def first(self, pack, k):
        z, x, y, c = self.z, self.x, self.y, self.c
        xn, yn, cn = (z, 1 - x, y, c), (z, x, 1 - y, c), (z, x, y, 1 - c)

        @pl.when(k == 0)
        def _():
            self.put(pack, G_X0, (z, x, y), 0, 192, xn, own=True)
            self.put(pack, G_Y0, (z, x, y), 0, 192, yn, own=True)
            self.put(pack, G_C, (z, x, y), 0, 192, cn, own=True)

        @pl.when(k > 0)
        def _():
            zz = on_chain(z, k)
            mine = (zz, x, y)
            self.got(pack, G_Z + zz, 192)
            self.further(pack, G_Z, mine, 0, 192)
            self.put(pack, G_XA + k - 1, mine, 0, 32, xn)
            self.put(pack, G_YA + k - 1, mine, 160, 32, yn)
            self.put(pack, G_XB + k - 1, mine, 96, 96, xn)
            self.put(pack, G_YB + k - 1, mine, 0, 96, yn)
            self.put(pack, G_C + 4 * k, mine, 0, 192, cn)

    def second(self, pack, k):
        z, x, y, c = self.z, self.x, self.y, self.c
        xn, yn, cn = (z, 1 - x, y, c), (z, x, 1 - y, c), (z, x, y, 1 - c)

        @pl.when(k == 0)
        def _():
            self.got(pack, G_X0, 192)
            self.along(pack, G_XZ, G_BACK + 1, (z, 1 - x, y), 32, 64)
            self.put(pack, G_DY, (z, 1 - x, y), 0, 96, yn)
            self.put(pack, G_C + 1, (z, 1 - x, y), 0, 192, cn)
            self.got(pack, G_Y0, 192)
            self.along(pack, G_YZ, G_BACK + 2, (z, x, 1 - y), 96, 64)
            self.put(pack, G_DX, (z, x, 1 - y), 96, 96, xn)
            self.put(pack, G_C + 2, (z, x, 1 - y), 0, 192, cn)

        @pl.when(k > 0)
        def _():
            zz = on_chain(z, k)
            across_x, across_y = (zz, 1 - x, y), (zz, x, 1 - y)
            self.got(pack, G_XZ + zz, 64)
            self.further(pack, G_XZ, across_x, 32, 64)
            self.got(pack, G_YZ + zz, 64)
            self.further(pack, G_YZ, across_y, 96, 64)
            self.got(pack, G_XA + k - 1, 32)
            self.put(pack, G_DY + k, across_x, 0, 96, yn)
            self.got(pack, G_YA + k - 1, 32)
            self.put(pack, G_DX + k, across_y, 96, 96, xn)
            self.got(pack, G_XB + k - 1, 96)
            self.put(pack, G_C + 4 * k + 1, across_x, 0, 192, cn)
            self.got(pack, G_YB + k - 1, 96)
            self.put(pack, G_C + 4 * k + 2, across_y, 0, 192, cn)

    def third(self, pack, k):
        z, x, y, c = self.z, self.x, self.y, self.c
        self.got(pack, G_DY + k, 96)
        self.got(pack, G_DX + k, 96)

        def on(zz):
            self.put(pack, G_C + 4 * k + 3, (zz, 1 - x, 1 - y), 0, 192, (z, x, y, 1 - c))

        pl.when(k == 0)(lambda: on(z))
        pl.when(k > 0)(lambda: on(on_chain(z, k)))

    def step(self, s):
        total = 4 * self.packs

        @pl.when(s < total)
        def _():
            self.first(s // 4, s % 4)
            pl.when((s % 4 == 3) & (s + 1 < total))(lambda: self.launch(s // 4 + 1))

        pl.when((s >= 2) & (s <= total + 1))(lambda: self.second((s + 2) // 4 - 1, (s + 2) % 4))
        pl.when((s >= 4) & (s <= total + 3))(lambda: self.third(s // 4 - 1, s % 4))

    def arrived(self, pack):
        for slot in range(G_C, G_C + 16):
            self.got(pack, slot, 192)

    def finish(self):
        z = self.z

        def sent(pack, slot, count):
            self.some(pack, slot, count).wait_send()

        def one(pack, carry):
            for slot, count in ((G_X0, 192), (G_Y0, 192)):
                sent(pack, slot, count)
            for base, n, count in (
                (G_DY, 4, 96), (G_DX, 4, 96), (G_XA, 3, 32), (G_XB, 3, 96), (G_YA, 3, 32), (G_YB, 3, 96), (G_C, 16, 192),
            ):
                for i in range(n):
                    sent(pack, base + i, count)
            for i, (base, count) in enumerate(((G_Z, 192), (G_XZ, 64), (G_YZ, 64))):
                pl.when(z > 0)(lambda: sent(pack, G_BACK + i, count))
                for zz in range(4):
                    pl.when((zz <= z) & (z < 3))(lambda: sent(pack, base + zz, count))
                    pl.when((zz > z) & (z > 0))(lambda: sent(pack, base + zz, count))
            return carry

        lax.fori_loop(0, self.packs, one, 0)


R_C, R_V, R_U, R_ZC, R_Z, R_F = 0, 16, 32, 38, 48, 53
R_COUNT = 55
R_ROWS = [192] * 16 + [96] * 16 + [32] * 6 + [64] * 10 + [192] * 5 + [96] * 2
ORDER = (3, 2, 1, 0)
TILE = 32


def add_rows(into, what, count):
    size = 96 if count % 96 == 0 else count

    def one(t, carry):
        r = pl.ds(pl.multiple_of(t * size, 32), size)
        into[r] = into[r] + what[r]
        return carry

    if count == size:
        into[...] = into[...] + what[...]
    else:
        lax.fori_loop(0, count // size, one, 0)


class Scatter:
    def __init__(self, part, out, mine, buf_c, buf_v, buf_u, buf_zc, buf_z, buf_f, send, recv, load, credit, stage, out_sem, packs):
        self.stage, self.out_sem = stage, out_sem
        self.part, self.out, self.mine = part, out, mine
        self.buf_c, self.buf_v, self.buf_u, self.buf_zc, self.buf_z, self.buf_f = buf_c, buf_v, buf_u, buf_zc, buf_z, buf_f
        self.send, self.recv, self.load_sem, self.credit, self.packs = send, recv, load, credit, packs
        self.z, self.x, self.y, self.c = place()
        z, x, y, c = place()
        self.xn, self.yn, self.cn = (z, 1 - x, y, c), (z, x, 1 - y, c), (z, x, y, 1 - c)

    def at(self, par, shard, first, count):
        zz, xx, yy = shard
        return self.mine.at[par, yy, rows_of(zz, xx, first, count)]

    def put(self, par, slot, here, there, target):
        pltpu.make_async_remote_copy(
            here, there, self.send.at[par, slot], self.recv.at[par, slot],
            device_id=device(*target), device_id_type=MESH_ID,
        ).start()

    def some(self, par, slot, count):
        view = self.mine.at[par, 0, pl.ds(0, count)]
        return pltpu.make_async_remote_copy(
            view, view, self.send.at[par, slot], self.recv.at[par, slot],
            device_id=device(*self.cn), device_id_type=MESH_ID,
        )

    def got(self, par, slot, count):
        self.some(par, slot, count).wait_recv()

    def lane_pack(self, pack):
        return (pack + 1) % self.packs

    def dest(self, k):
        if isinstance(k, int):
            return self.z if k == 0 else on_chain(self.z, k)
        none = (3 - k) // 3
        return none * self.z + (1 - none) * on_chain(self.z, k)

    def slot_to(self, zz):
        apart = zz - self.z + 4
        home = (apart // 3) * (1 - apart // 4)
        return zz * (1 - home) + 4 * home

    def onward(self, par, base, buf, j, zz, here):
        z, x, y, c = self.z, self.x, self.y, self.c
        slot = self.slot_to(zz)
        there = buf.at[par, slot] if j is None else buf.at[par, slot, j]
        number = base + (slot if j is None else 2 * slot + j)
        pl.when(zz > z)(lambda: self.put(par, number, here, there, (z + 1, x, y, c)))
        pl.when(zz < z)(lambda: self.put(par, number, here, there, (z - 1, x, y, c)))

    def shards(self, k):
        zz = self.dest(k)
        return ((zz, 1 - self.x, 1 - self.y), (zz, self.x, 1 - self.y), (zz, 1 - self.x, self.y), (zz, self.x, self.y))

    def loads(self, pack):
        par = pack % 2
        return [
            pltpu.make_async_copy(
                self.part.at[yy * 2 + self.c, :, lanes_of(self.lane_pack(pack))], self.mine.at[par, yy], self.load_sem.at[yy]
            )
            for yy in range(2)
        ]

    def ahead(self, s):
        pack = s // 4
        k = 3 - s % 4
        par = pack % 2
        if not isinstance(s, int):
            pl.when((pack >= 2) & (s % 4 == 0))(lambda: pl.semaphore_wait(self.credit.at[pack - 2, 0], 1))
        for i, (zz, xx, yy) in enumerate(self.shards(k)):
            rows = rows_of(zz, xx, 0, 192)
            slot = R_C + 4 * k + i
            if not isinstance(s, int):
                pl.when(pack >= 2)(lambda: self.some(par, slot, 192).wait_send())
            self.put(
                par, slot,
                self.part.at[yy * 2 + 1 - self.c, rows, lanes_of(self.lane_pack(pack))],
                self.buf_c.at[par, yy, rows], self.cn,
            )

    def launch(self):
        self.ahead(0)
        self.ahead(1)
        self.load(0)

    def load(self, pack):
        for r in self.loads(pack):
            r.start()

    def sent(self, pack, first, last):
        for slot in range(first, last):
            self.some(pack % 2, slot, R_ROWS[slot]).wait_send()

    def core(self, pack, k):
        par = pack % 2
        sh = self.shards(k)

        @pl.when(k == ORDER[0])
        def _():
            for r in self.loads(pack):
                r.wait()
            pl.when(pack >= 2)(lambda: pl.semaphore_wait(self.credit.at[pack - 2, 1], 5))

        for i, (zz, xx, yy) in enumerate(sh):
            self.got(par, R_C + 4 * k + i, 192)
            add_rows(self.at(par, sh[i], 0, 192), self.buf_c.at[par, yy, rows_of(zz, xx, 0, 192)], 192)
        pl.when((k == ORDER[3]) & (pack + 2 < self.packs))(lambda: self.free(pack, 0, self.cn))
        v = self.buf_v
        self.put(par, R_V + 4 * k, self.at(par, sh[0], 0, 96), v.at[par, k, 0], self.yn)
        self.put(par, R_V + 4 * k + 1, self.at(par, sh[0], 96, 96), v.at[par, k, 1], self.xn)
        self.put(par, R_V + 4 * k + 2, self.at(par, sh[1], 0, 96), v.at[par, k, 2], self.yn)
        self.put(par, R_V + 4 * k + 3, self.at(par, sh[2], 96, 96), v.at[par, k, 3], self.xn)

    def free(self, pack, kind, target):
        pl.semaphore_signal(
            self.credit.at[pack, kind], inc=1, device_id=device(*target), device_id_type=MESH_ID
        )

    def vees(self, pack, k):
        par = pack % 2
        sh = self.shards(k)
        zz = self.dest(k)
        end = (self.z == 0) | (self.z == 3)
        v = self.buf_v
        self.got(par, R_V + 4 * k, 96)
        add_rows(self.at(par, sh[2], 0, 96), v.at[par, k, 0], 96)

        @pl.when(k > 0)
        def _():
            self.put(par, R_U + 2 * (k - 1), self.at(par, sh[2], 0, 32), self.buf_u.at[par, k - 1, 0], self.xn)
            pl.when(end)(lambda: self.onward(par, R_ZC, self.buf_zc, 0, zz, self.at(par, sh[2], 32, 64)))

        self.got(par, R_V + 4 * k + 1, 96)
        add_rows(self.at(par, sh[1], 96, 96), v.at[par, k, 1], 96)

        @pl.when(k > 0)
        def _():
            self.put(par, R_U + 2 * (k - 1) + 1, self.at(par, sh[1], 160, 32), self.buf_u.at[par, k - 1, 1], self.yn)
            pl.when(end)(lambda: self.onward(par, R_ZC, self.buf_zc, 1, zz, self.at(par, sh[1], 96, 64)))
            self.got(par, R_V + 4 * k + 2, 96)
            add_rows(self.at(par, sh[3], 0, 96), v.at[par, k, 2], 96)
            self.got(par, R_V + 4 * k + 3, 96)
            add_rows(self.at(par, sh[3], 96, 96), v.at[par, k, 3], 96)

    def yous(self, pack, k):
        par = pack % 2
        sh = self.shards(k)
        zz = self.dest(k)
        end = (self.z == 0) | (self.z == 3)

        @pl.when((self.z > 0) & (self.z < 3))
        def _():
            for j, (shard, first) in enumerate(((sh[2], 32), (sh[1], 96))):
                self.got(par, R_ZC + 2 * zz + j, 64)
                add_rows(self.at(par, shard, first, 64), self.buf_zc.at[par, zz, j], 64)
                self.onward(par, R_ZC, self.buf_zc, j, zz, self.at(par, shard, first, 64))

        self.got(par, R_U + 2 * (k - 1), 32)
        add_rows(self.at(par, sh[3], 0, 32), self.buf_u.at[par, k - 1, 0], 32)
        self.got(par, R_U + 2 * (k - 1) + 1, 32)
        add_rows(self.at(par, sh[3], 160, 32), self.buf_u.at[par, k - 1, 1], 32)
        pl.when(end)(lambda: self.onward(par, R_Z, self.buf_z, None, zz, self.at(par, sh[3], 0, 192)))

    def chain(self, pack, k):
        par = pack % 2
        sh = self.shards(k)
        zz = self.dest(k)

        @pl.when((self.z > 0) & (self.z < 3))
        def _():
            self.got(par, R_Z + zz, 192)
            add_rows(self.at(par, sh[3], 0, 192), self.buf_z.at[par, zz], 192)
            self.onward(par, R_Z, self.buf_z, None, zz, self.at(par, sh[3], 0, 192))

    def near(self, pack):
        par = pack % 2
        sh = self.shards(0)
        z = self.z
        for j, (shard, first, whole, nb) in enumerate(((sh[2], 32, 0, self.xn), (sh[1], 96, 96, self.yn))):
            into = self.at(par, shard, first, 64)

            @pl.when(z > 0)
            def _(j=j, into=into):
                self.got(par, R_ZC + 2 * z + j, 64)
                add_rows(into, self.buf_zc.at[par, z, j], 64)

            @pl.when(z < 3)
            def _(j=j, into=into):
                self.got(par, R_ZC + 8 + j, 64)
                add_rows(into, self.buf_zc.at[par, 4, j], 64)

            self.put(par, R_F + j, self.at(par, shard, whole, 96), self.buf_f.at[par, j], nb)

    def out_copy(self, pack):
        return pltpu.make_async_copy(self.stage, self.out.at[:, lanes_of(self.lane_pack(pack))], self.out_sem)

    def final(self, pack):
        par = pack % 2
        own = self.at(par, self.shards(0)[3], 0, 192)
        self.got(par, R_V + 2, 96)
        self.got(par, R_V + 3, 96)
        for j in range(2):
            self.got(par, R_F + j, 96)

        pl.when(pack > 0)(lambda: self.out_copy(pack).wait())
        for j in range(2):
            def one(t, carry, j=j):
                r = pl.ds(pl.multiple_of(t * TILE, TILE), TILE)
                rr = pl.ds(pl.multiple_of(j * 96 + t * TILE, TILE), TILE)
                total = own[rr].astype(jnp.float32) + self.buf_v[par, 0, 2 + j, r].astype(jnp.float32)
                total = total + self.buf_f[par, j, r].astype(jnp.float32)
                self.stage[rr] = total
                return carry
            lax.fori_loop(0, 96 // TILE, one, 0)
        def more(slot):
            self.got(par, R_Z + slot, 192)

            def one(t, carry):
                rr = pl.ds(pl.multiple_of(t * TILE, TILE), TILE)
                self.stage[rr] += self.buf_z[par, slot, rr].astype(jnp.float32)
                return carry

            lax.fori_loop(0, ROWS // TILE, one, 0)

        pl.when(self.z > 0)(lambda: more(self.z))
        pl.when(self.z < 3)(lambda: more(4))
        self.out_copy(pack).start()
        self.sent(pack, R_V, R_ZC)
        self.sent(pack, R_F, R_COUNT)
        for k in (1, 2, 3):
            slot = self.slot_to(self.dest(k))
            self.some(par, R_Z + slot, 192).wait_send()
            for j in range(2):
                self.some(par, R_ZC + 2 * slot + j, 64).wait_send()

        @pl.when(pack + 2 < self.packs)
        def _():
            z, x, y, c = self.z, self.x, self.y, self.c
            for t in (self.xn, self.yn) + tuple(((z + k) % 4, x, y, c) for k in (1, 2, 3)):
                self.free(pack, 1, t)

    def step(self, s):
        total = 4 * self.packs
        pl.when(s < total)(lambda: self.core(s // 4, 3 - s % 4))
        pl.when((s >= 1) & (s <= total))(lambda: self.vees((s + 3) // 4 - 1, 3 - (s + 3) % 4))

        @pl.when((s >= 2) & (s <= total + 1))
        def _():
            before = (s + 2) // 4 - 1
            k = 3 - (s + 2) % 4
            pl.when(k > 0)(lambda: self.yous(before, k))
            pl.when(k == 0)(lambda: self.near(before))

        @pl.when((s >= 3) & (s <= total + 2))
        def _():
            before = (s + 1) // 4 - 1
            k = 3 - (s + 1) % 4
            pl.when(k > 0)(lambda: self.chain(before, k))
            pl.when(k == 0)(lambda: self.final(before))

        more = s + 2
        due = (more < total - 4) | ((more >= total - 2) & (more < total))
        if not isinstance(s, int):
            pl.when(due)(lambda: self.ahead(more))
        elif due:
            self.ahead(jnp.int32(more))
        later = s // 4 + 1
        pl.when((s % 4 == 3) & (later < self.packs))(lambda: self.load(later))

    def finish(self):
        self.out_copy(self.packs - 1).wait()
        for pack in (self.packs - 2, self.packs - 1):
            self.sent(pack, R_C, R_V)


def scatter_scratch(packs):
    bf = jnp.bfloat16
    return [
        pltpu.VMEM((2, 2, 8 * ROWS, LANES), bf),
        pltpu.VMEM((2, 2, 8 * ROWS, LANES), bf),
        pltpu.VMEM((2, 4, 4, 96, LANES), bf),
        pltpu.VMEM((2, 3, 2, 32, LANES), bf),
        pltpu.VMEM((2, 5, 2, 64, LANES), bf),
        pltpu.VMEM((2, 5, 192, LANES), bf),
        pltpu.VMEM((2, 2, 96, LANES), bf),
        pltpu.SemaphoreType.DMA((2, R_COUNT)),
        pltpu.SemaphoreType.DMA((2, R_COUNT)),
        pltpu.SemaphoreType.DMA((2,)),
        pltpu.SemaphoreType.REGULAR((packs, 2)),
        pltpu.VMEM((ROWS, LANES), jnp.float32),
        pltpu.SemaphoreType.DMA,
    ]


BF = jnp.bfloat16
F32 = jnp.float32
CHUNK = 256


def gain_rows(table, line, into):
    lines = [None] * 13
    for i in range(32):
        first = (48 * i) // 128
        for j in range(2):
            got = table[i, line + j : line + j + 1, :]
            lines[first + j] = got if lines[first + j] is None else lines[first + j] + got
    for r in range(12):
        into[:, 128 * r : 128 * (r + 1)] = lines[r]


def loop(count, body):
    def one(t, carry):
        body(t)
        return carry

    lax.fori_loop(0, count, one, 0)


def tile_rows(t, size):
    return pl.ds(pl.multiple_of(t * size, size), size)


def norm_rows(src, gain, into, tokens):
    def one(t):
        r = tile_rows(t, 32)
        v = src[r].astype(F32)
        scale = lax.rsqrt(jnp.mean(v * v, axis=-1, keepdims=True) + EPS)
        into[r] = (v * scale * gain[...]).astype(BF)

    loop(tokens // 32, one)


def turn(src, into, tokens):
    def one(t):
        r = tile_rows(t, 128)
        into[:, r] = jnp.transpose(src[r])

    loop(tokens // 128, one)


def gelu_parts(u):
    root = 0.7978845608028654
    t = jnp.tanh(root * (u + 0.044715 * (u * u * u)))
    return 0.5 * u * (1.0 + t), t


def nt(a, b):
    return lax.dot_general(a, b, (((1,), (1,)), ((), ())), preferred_element_type=F32)


def tn(a, b):
    return lax.dot_general(a, b, (((0,), (0,)), ((), ())), preferred_element_type=F32)


def nn(a, b):
    return jnp.dot(a, b, preferred_element_type=F32)


def forward_kernel(
    packs, tokens, width, seq, heads, scale,
    own, tile, x_any, teacher_any, cotangent_any, buckets, bias_smem, blocks_row, blocks_col, valid_row, valid_col,
    whole, table, n1_out, n2_out, qkv_out, probs_out, pre_out, act_out, middle_out, layer_out, grad_out, gffn_out, loss_out,
    x, n1, n2, turned, acc, bias, mask, wbuf, qs, ps, pre, act, tabv, gain1, gain2, teach, cot, lossv,
    send, recv, local, tile_send, tile_recv, tile_local, in_sem, w_sem, p_sem, q_sem, pre_sem, act_sem, out_sem,
):
    f = lax.axis_index("fsdp")
    d = lax.axis_index("dp")
    micro = tokens // seq
    per = heads // 4
    size = 192 // per
    start_barrier()
    g = Gather(own, whole, send, recv, packs)
    g.launch(0)
    tiles = exchange(lambda other: tile, table, tile_send, tile_recv)
    tile_keep = pltpu.make_async_copy(tile, table.at[f * 4 + d], tile_local)
    tile_keep.start()
    bounce = [
        pltpu.make_async_copy(own.at[:, pl.ds(p * LANES, LANES)], wbuf.at[1, pl.ds(p * ROWS, ROWS)], local.at[p])
        for p in range(packs)
    ]
    keep = [
        pltpu.make_async_copy(
            wbuf.at[1, pl.ds(p * ROWS, ROWS)],
            whole.at[d, pl.ds(pl.multiple_of(f * ROWS, ROWS), ROWS), pl.ds(p * LANES, LANES)],
            local.at[p],
        )
        for p in range(packs)
    ]
    for r in bounce:
        r.start()
    load_x = pltpu.make_async_copy(x_any, x, in_sem.at[0])
    load_x.start()
    g.step(0)
    for a, b in zip(bounce, keep):
        a.wait()
        b.start()
    rows_i = lax.broadcasted_iota(jnp.int32, (seq, seq), 0)
    cols_i = lax.broadcasted_iota(jnp.int32, (seq, seq), 1)
    for m in range(micro):
        ok = (blocks_row[m : m + 1, :] <= blocks_col[m * seq : (m + 1) * seq, :]) & (valid_row[m : m + 1, :] == 1)
        mask[m] = jnp.where(ok | (rows_i == cols_i), 1.0, 0.0)

    def bias_tile(t):
        r = tile_rows(t, 8)
        b = buckets[r]
        totals = [jnp.zeros((8, seq), F32)] * heads
        for k in range(32):
            here = b == k
            totals = [jnp.where(here, bias_smem[k, h], v) for h, v in enumerate(totals)]
        for h in range(heads):
            bias[h, r] = totals[h]

    step_tiles = -(-(seq // 8) // 7)

    def early(s):
        def some(i):
            t = s * step_tiles + i
            pl.when(t < seq // 8)(lambda: bias_tile(t))

        loop(step_tiles, some)
        g.step(s + 1)

    loop(7, early)
    tile_keep.wait()
    tiles.wait()
    load_table = pltpu.make_async_copy(table, tabv, in_sem.at[1])
    load_table.start()
    load_x.wait()
    load_table.wait()
    gain_rows(tabv, 0, gain1)
    gain_rows(tabv, 2, gain2)
    load_t = pltpu.make_async_copy(teacher_any, teach, in_sem.at[2])
    load_t.start()
    load_c = pltpu.make_async_copy(cotangent_any, cot, in_sem.at[3])
    load_c.start()
    norm_rows(x, gain1, n1, tokens)

    def copy_x(t):
        r = tile_rows(t, 32)
        acc[r] = x[r].astype(F32)

    loop(tokens // 32, copy_x)
    turn(n1, turned, tokens)
    n1_copy = pltpu.make_async_copy(turned, n1_out, out_sem.at[0])
    n1_copy.start()
    for r in keep:
        r.wait()
    g.arrived(0)

    def load_w(i, slot):
        return pltpu.make_async_copy(
            whole.at[i % 4, :, lanes_of(i // 4)], wbuf.at[slot], w_sem.at[slot]
        )

    load_w(0, 0).start()

    def probs_copy(dd, m, slot):
        return pltpu.make_async_copy(ps.at[slot], probs_out.at[dd * micro + m], p_sem.at[slot])

    def attention(dd):
        slot = dd % 2
        pl.when(dd < 3)(lambda: load_w(dd + 1, 1 - slot).start())
        load_w(dd, slot).wait()
        pl.when(dd > 0)(lambda: pltpu.make_async_copy(qs, qkv_out.at[dd], q_sem).wait())
        qs[:, 0:576] = nn(n1[...], wbuf[slot, :, 0:576]).astype(BF)
        g.step(8 + 2 * dd)
        for m in range(micro):
            r = slice(m * seq, (m + 1) * seq)
            pl.when(dd > 0)(lambda: probs_copy(dd, m, m).wait())
            for hh in range(per):
                a = hh * size
                s = nt(qs[r, a : a + size], qs[r, 192 + a : 192 + a + size]) + bias[dd * per + hh]
                s = jnp.where(mask[m] > 0.0, s, NEG)
                top = jnp.max(s, axis=-1, keepdims=True)
                e = jnp.exp(s - top)
                p = e * (1.0 / jnp.sum(e, axis=-1, keepdims=True))
                ps[m, hh] = p
                qs[r, 576 + a : 576 + a + size] = nn(p.astype(BF), qs[r, 384 + a : 384 + a + size]).astype(BF)
            probs_copy(dd, m, m).start()
        g.step(9 + 2 * dd)
        for m in range(micro):
            r = slice(m * seq, (m + 1) * seq)
            acc[r] += nt(qs[r, 576:768], wbuf[slot, :, 576:768])
        pltpu.make_async_copy(qs, qkv_out.at[dd], q_sem).start()

    loop(4, attention)
    pltpu.make_async_copy(qs, qkv_out.at[0], q_sem).wait()
    for m in range(micro):
        probs_copy(3, m, m).wait()
    mid_copy = pltpu.make_async_copy(acc, middle_out, out_sem.at[1])
    mid_copy.start()
    norm_rows(acc, gain2, n2, tokens)
    n1_copy.wait()
    turn(n2, turned, tokens)
    n2_copy = pltpu.make_async_copy(turned, n2_out, out_sem.at[2])
    n2_copy.start()
    mid_copy.wait()

    def pre_copy(t, slot):
        return pltpu.make_async_copy(pre.at[slot], pre_out.at[t], pre_sem.at[slot])

    def act_copy(t, slot):
        return pltpu.make_async_copy(act.at[slot], act_out.at[t], act_sem.at[slot])

    def feed(t):
        slot = t % 2

        @pl.when(t % 4 == 0)
        def _():
            g.arrived(1 + t // 4)
            load_w(4 + t, slot).start()

        pl.when(t % 4 < 3)(lambda: load_w(5 + t, 1 - slot).start())
        load_w(4 + t, slot).wait()

        @pl.when(t > 1)
        def _():
            pre_copy(t, slot).wait()
            act_copy(t, slot).wait()

        for m in range(micro):
            r = slice(m * seq, (m + 1) * seq)
            gu = nn(n2[r], wbuf[slot, :, 0 : 2 * CHUNK])
            pre[slot, r] = gu
            ge, _ = gelu_parts(gu[:, 0:CHUNK])
            act[slot, r] = (ge * gu[:, CHUNK:]).astype(BF)
        pre_copy(t, slot).start()
        act_copy(t, slot).start()

        @pl.when(t < 8)
        def _():
            pl.when(t % 2 == 1)(lambda: g.step(16 + t // 2))

        pl.when((t >= 8) & (t < 12))(lambda: g.step(12 + t))
        for m in range(micro):
            r = slice(m * seq, (m + 1) * seq)
            acc[r] += nt(act[slot, r], wbuf[slot, :, 2 * CHUNK :])

    loop(16, feed)
    load_t.wait()
    load_c.wait()
    n2_copy.wait()
    for slot in range(2):
        pre_copy(14 + slot, slot).wait()
        act_copy(14 + slot, slot).wait()
    total = tabv[0, 4:5, 0:1]
    for i in range(1, 32):
        total = total + tabv[i, 4:5, 0:1]
    factor = (2.0 * scale / width) / total
    lossv[...] = jnp.zeros_like(lossv)

    def ends(t):
        r = tile_rows(t, 16)
        full = acc[r]
        gap = full - teach[r].astype(F32)
        weighted = valid_col[r] * gap
        grad = scale * cot[r].astype(F32) + factor * weighted
        acc[r] = grad
        x[r] = grad.astype(BF)
        n1[r] = full.astype(BF)
        lossv[...] += weighted * gap

    loop(tokens // 16, ends)
    copies = [
        pltpu.make_async_copy(n1, layer_out, out_sem.at[0]),
        pltpu.make_async_copy(acc, grad_out, out_sem.at[1]),
        pltpu.make_async_copy(x, gffn_out, out_sem.at[2]),
    ]
    for r in copies:
        r.start()
    loss_out[...] = jnp.zeros_like(loss_out) + jnp.sum(lossv[...])
    g.finish()
    for r in copies:
        r.wait()


def forward(own, tile, x, teacher, cotangent, buckets, bias_table, blocks_row, blocks_col, valid_row, valid_col, scale):
    packs = own.shape[1] // LANES
    tokens, width = x.shape
    seq = buckets.shape[0]
    heads = bias_table.shape[1]
    micro = tokens // seq
    any_ = pl.BlockSpec(memory_space=pl.ANY)
    vmem = pl.BlockSpec(memory_space=pltpu.VMEM)
    smem = pl.BlockSpec(memory_space=pltpu.SMEM)
    S = jax.ShapeDtypeStruct
    dma = pltpu.SemaphoreType.DMA
    outs = (
        S((4, 8 * ROWS, own.shape[1]), BF), S((32, 8, 128), F32), S((width, tokens), BF), S((width, tokens), BF),
        S((4, tokens, 768), BF), S((4 * micro, heads // 4, seq, seq), F32), S((16, tokens, 2 * CHUNK), F32),
        S((16, tokens, CHUNK), BF), S((tokens, width), F32), S((tokens, width), BF), S((tokens, width), F32), S((tokens, width), BF), S((8, 128), F32),
    )
    return pl.pallas_call(
        functools.partial(forward_kernel, packs, tokens, width, seq, heads, scale),
        out_shape=outs,
        in_specs=[any_] * 5 + [vmem, smem] + [vmem] * 4,
        out_specs=[any_] * 12 + [vmem],
        scratch_shapes=[
            pltpu.VMEM((tokens, width), BF), pltpu.VMEM((tokens, width), BF), pltpu.VMEM((tokens, width), BF),
            pltpu.VMEM((width, tokens), BF), pltpu.VMEM((tokens, width), F32), pltpu.VMEM((heads, seq, seq), F32), pltpu.VMEM((micro, seq, seq), F32),
            pltpu.VMEM((2, 8 * ROWS, LANES), BF), pltpu.VMEM((tokens, 768), BF), pltpu.VMEM((micro, heads // 4, seq, seq), F32),
            pltpu.VMEM((2, tokens, 2 * CHUNK), F32), pltpu.VMEM((2, tokens, CHUNK), BF), pltpu.VMEM((32, 8, 128), F32),
            pltpu.VMEM((1, width), F32), pltpu.VMEM((1, width), F32), pltpu.VMEM((tokens, width), BF),
            pltpu.VMEM((tokens, width), BF), pltpu.VMEM((16, width), F32),
            dma((packs, G_COUNT)), dma((packs, G_COUNT)), dma((packs,)), dma, dma, dma, dma((4,)), dma((2,)), dma((2,)), dma,
            dma((2,)), dma((2,)), dma((3,)),
        ],
        compiler_params=pltpu.CompilerParams(collective_id=1, has_side_effects=True, vmem_limit_bytes=63 * 1024 * 1024),
    )(own, tile, x, teacher, cotangent, buckets, bias_table, blocks_row, blocks_col, valid_row, valid_col)


def prepare(weights, gain_one, gain_two, valid):
    part = weights[4].shape[1]
    pads = [jnp.pad(w, ((0, 0), (0, 4 * CHUNK - part))) for w in weights[4:]]
    pieces = list(weights[:4])
    for j in range(4):
        pieces += [w[:, j * CHUNK : (j + 1) * CHUNK] for w in pads]
    own = jnp.concatenate(pieces, axis=1)
    me = lax.axis_index("fsdp") * 4 + lax.axis_index("dp")
    first = (me * 48) % 128

    def lines(gain):
        return lax.dynamic_update_slice(jnp.zeros((256,), F32), gain.astype(F32), (first,)).reshape(2, 128)

    count = jnp.zeros((4, 128), F32) + jnp.sum(valid.astype(F32))
    return own, jnp.concatenate([lines(gain_one), lines(gain_two), count])


def gelu_slope(u, t):
    root = 0.7978845608028654
    return 0.5 * (1.0 + t) + 0.5 * u * (1.0 - t * t) * root * (1.0 + 3.0 * 0.044715 * (u * u))


def norm_back(src_row, up_row, gain, gain_sum):
    v, u = src_row, up_row
    scale = lax.rsqrt(jnp.mean(v * v, axis=-1, keepdims=True) + EPS)
    scaled = u * gain
    mean = jnp.mean(scaled * v, axis=-1, keepdims=True)
    term = u * v * scale
    total = term[0:8]
    for i in range(1, term.shape[0] // 8):
        total = total + term[8 * i : 8 * i + 8]
    gain_sum[...] += total
    return scale * scaled - v * (scale * scale * scale) * mean


def backward_kernel(
    packs, tokens, width, seq, heads,
    whole, table, x_any, n1_any, n2_any, qkv_any, probs_any, pre_any, act_any, mid_any, gout_any, gffn_any, buckets, loss,
    part, out, hidden_out, tiles_out, sums_out, gs_out,
    low, src, acc, acc2, wbuf, pre, act, ggu, gst, qs, ps, gqkv, bsum, gain1, gain2, sum1, sum2, tilev,
    in_sem, w_sem, pre_sem, act_sem, g_sem, s_sem, q_sem, p_sem, out2_sem, gs_sem, tile_send, tile_recv, tile_local, *scatter_refs,
):
    micro = tokens // seq
    per = heads // 4
    size = 192 // per
    me = lax.axis_index("fsdp") * 4 + lax.axis_index("dp")
    tell_all()
    rs = Scatter(part, out, *scatter_refs, packs)

    def fetch(a, b, sem):
        r = pltpu.make_async_copy(a, b, sem)
        r.start()
        return r

    loads = [fetch(gffn_any, low, in_sem.at[0]), fetch(n2_any, src, in_sem.at[1]), fetch(table, tilev, in_sem.at[2])]

    def load_w(i, slot):
        return pltpu.make_async_copy(whole.at[i % 4, :, lanes_of(i // 4)], wbuf.at[slot], w_sem.at[slot])

    def load_pre(t, slot):
        return pltpu.make_async_copy(pre_any.at[t], pre.at[slot], pre_sem.at[slot])

    def load_act(t, slot):
        return pltpu.make_async_copy(act_any.at[t], act.at[slot], act_sem.at[slot])

    def put_g(dd, lane_pack):
        return pltpu.make_async_copy(gst, part.at[dd, :, lanes_of(lane_pack)], g_sem)

    for r in (load_w(4, 0), load_pre(0, 0), load_act(0, 0)):
        r.start()
    mid_load = fetch(mid_any, acc2, in_sem.at[3])
    wide = 2 * CHUNK
    gout_loads = [
        pltpu.make_async_copy(gout_any.at[:, pl.ds(i * wide, wide)], pre.at[i], s_sem.at[i]) for i in range(2)
    ]
    for m in range(micro):
        rows = pl.ds(m * seq, seq)
        gout_loads.append(pltpu.make_async_copy(gout_any.at[rows, pl.ds(2 * wide, seq)], ps.at[m, 0], s_sem.at[2 + 2 * m]))
        gout_loads.append(
            pltpu.make_async_copy(
                gout_any.at[rows, pl.ds(2 * wide + seq, 128)], ps.at[m, 1, :, pl.ds(0, 128)], s_sem.at[3 + 2 * m]
            )
        )
    for r in gout_loads[2:]:
        r.start()
    sum1[...] = jnp.zeros_like(sum1)
    sum2[...] = jnp.zeros_like(sum2)

    def clear(t):
        r = tile_rows(t, 32)
        acc[r] = jnp.zeros((32, width), F32)

    loop(tokens // 32, clear)
    for r in loads:
        r.wait()
    gain_rows(tilev, 0, gain1)
    gain_rows(tilev, 2, gain2)
    half = width // 2

    def feed(t):
        slot = t % 2

        @pl.when(t < 15)
        def _():
            load_w(5 + t, 1 - slot).start()
            load_pre(t + 1, 1 - slot).start()
            load_act(t + 1, 1 - slot).start()

        load_w(4 + t, slot).wait()
        load_pre(t, slot).wait()
        load_act(t, slot).wait()
        for m in range(micro):
            r = slice(m * seq, (m + 1) * seq)
            gh = nn(low[r], wbuf[slot, :, 2 * CHUNK :])
            u = pre[slot, r, 0:CHUNK]
            ge, th = gelu_parts(u)
            ggu[r, 0:CHUNK] = (gh * pre[slot, r, CHUNK:] * gelu_slope(u, th)).astype(BF)
            ggu[r, CHUNK:] = (gh * ge).astype(BF)
        pl.when((t > 0) & (t != 4))(lambda: put_g(0, 0).wait())
        for h in range(2):
            c = slice(h * half, (h + 1) * half)
            gst[c, 0 : 2 * CHUNK] = nn(src[c], ggu[...]).astype(BF)
            gst[c, 2 * CHUNK :] = tn(low[:, c], act[slot]).astype(BF)
        put_g(t % 4, 1 + t // 4).start()
        for m in range(micro):
            r = slice(m * seq, (m + 1) * seq)
            acc[r] += nt(ggu[r], wbuf[slot, :, 0 : 2 * CHUNK])

        @pl.when(t == 3)
        def _():
            put_g(0, 0).wait()
            hear_all()
            rs.launch()

        pl.when((t == 4) | (t == 6))(lambda: rs.step(t // 2 - 2))
        pl.when(t >= 8)(lambda: rs.step(t - 6))

    loop(16, feed)
    put_g(0, 0).wait()
    n1_load = fetch(n1_any, src, in_sem.at[1])
    load_w(0, 0).start()

    def probs_load(dd, m):
        return pltpu.make_async_copy(probs_any.at[dd * micro + m], ps.at[m], p_sem.at[m])

    def q_load(dd):
        return pltpu.make_async_copy(qkv_any.at[dd], qs, q_sem)

    for r in gout_loads[:2]:
        r.start()
    q_load(0).start()
    mid_load.wait()
    for r in gout_loads:
        r.wait()
    for m in range(micro):

        def norm_two(t, m=m):
            r = tile_rows(m * (seq // 32) + t, 32)
            h = tile_rows(t, 32)
            gout = jnp.concatenate([pre[0, r], pre[1, r], ps[m, 0, h], ps[m, 1, h, 0:128]], axis=1)
            grad = gout + norm_back(acc2[r], acc[r], gain2[...], sum2)
            acc[r] = grad
            acc2[r] = jnp.zeros((32, width), F32)
            low[r] = grad.astype(BF)

        loop(seq // 32, norm_two)
        probs_load(0, m).start()
    n1_load.wait()
    rs.step(10)

    def gs_copy(dd):
        return pltpu.make_async_copy(ps.at[micro - 1], gs_out.at[dd], gs_sem.at[0])

    def gs_load(dd):
        return pltpu.make_async_copy(gs_out.at[dd], ps.at[dd % 2], gs_sem.at[dd % 2])

    def attention(dd):
        slot = dd % 2
        pl.when(dd < 3)(lambda: load_w(dd + 1, 1 - slot).start())
        load_w(dd, slot).wait()
        gqkv[:, 576:768] = nn(low[...], wbuf[slot, :, 576:768]).astype(BF)
        q_load(dd).wait()

        @pl.when(dd > 0)
        def _():
            gs_copy(dd).wait()
            probs_load(dd, micro - 1).start()
            put_g(0, 0).wait()

        gst[:, 576:768] = tn(low[...], qs[:, 576:768]).astype(BF)
        for m in range(micro):
            r = slice(m * seq, (m + 1) * seq)
            probs_load(dd, m).wait()
            for hh in range(per):
                a = hh * size
                p = ps[m, hh]
                go = gqkv[r, 576 + a : 576 + a + size]
                gp = nt(go, qs[r, 384 + a : 384 + a + size])
                gs = p * (gp - jnp.sum(p * gp, axis=-1, keepdims=True))
                gs = gs.astype(BF)
                gqkv[r, a : a + size] = nn(gs, qs[r, 192 + a : 192 + a + size]).astype(BF)
                gqkv[r, 192 + a : 192 + a + size] = tn(gs, qs[r, a : a + size]).astype(BF)
                gqkv[r, 384 + a : 384 + a + size] = tn(p.astype(BF), go).astype(BF)
                ps[m, hh] = gs.astype(F32) if m == 0 else ps[m - 1, hh] + gs.astype(F32)
        gs_copy(dd).start()

        @pl.when(dd < 3)
        def _():
            q_load(dd + 1).start()
            probs_load(dd + 1, 0).start()

        rs.step(11 + dd)
        for h in range(2):
            c = slice(h * half, (h + 1) * half)
            gst[c, 0:576] = nn(src[c], gqkv[:, 0:576]).astype(BF)
        put_g(dd, 0).start()
        for m in range(micro):
            r = slice(m * seq, (m + 1) * seq)
            acc2[r] += nt(gqkv[r, 0:576], wbuf[slot, :, 0:576])


    loop(4, attention)
    put_g(0, 0).wait()
    gs_copy(0).wait()
    rs.ahead(jnp.int32(4 * packs - 4))
    rs.ahead(jnp.int32(4 * packs - 3))
    gs_load(0).start()
    rs.step(15)
    x_load = fetch(x_any, low, in_sem.at[1])
    x_load.wait()

    def norm_one(t):
        r = tile_rows(t, 32)
        term = norm_back(low[r].astype(F32), acc2[r], gain1[...], sum1)
        low[r] = (acc[r] + term).astype(BF)

    loop(tokens // 32, norm_one)
    hidden_copy = fetch(low, hidden_out, out2_sem)
    rs.step(16)

    def buckets_of(dd):
        gs_load(dd).wait()
        pl.when(dd < 3)(lambda: gs_load(dd + 1).start())

        def by_bucket(group):
            def some(t, totals):
                r = tile_rows(t, 8)
                b = buckets[r]
                v = [ps[dd % 2, hh, r] for hh in range(per)]
                new = []
                for j in range(4):
                    here = b == group * 4 + j
                    new += [totals[j * per + hh] + jnp.where(here, v[hh], 0.0) for hh in range(per)]
                return tuple(new)

            totals = lax.fori_loop(0, seq // 8, some, (jnp.zeros((8, seq), F32),) * (4 * per))
            for j in range(4):
                for hh in range(per):
                    bsum[dd * per + hh, pl.ds(group * 4 + j, 1)] = jnp.sum(totals[j * per + hh], axis=0, keepdims=True)

        loop(8, by_bucket)
        rs.step(17 + dd)

    loop(4, buckets_of)
    one = jnp.sum(sum1[...], axis=0, keepdims=True)
    two = jnp.sum(sum2[...], axis=0, keepdims=True)
    biases = lax.dot_general(
        jnp.ones((8, seq), F32), bsum[...].reshape(heads * 32, seq), (((1,), (1,)), ((), ())),
        precision=lax.Precision.HIGHEST, preferred_element_type=F32,
    )
    lines = [biases[0:1, 128 * i : 128 * (i + 1)] for i in range(3)]
    none = jnp.zeros((1, 128), F32)
    for i in range(32):
        first = 128 * ((48 * i) // 128)
        rows = []
        for v in (one, two):
            rows.append(v[:, first : first + 128])
            rows.append(v[:, first + 128 : first + 256] if first + 128 < width else none)
        tilev[i] = jnp.concatenate(rows + [loss[0:1, :]] + lines, axis=0)
    tile_copy = fetch(tilev, tiles_out, in_sem.at[0])
    tile_copy.wait()
    tiles = exchange(lambda other: tiles_out.at[other], sums_out, tile_send, tile_recv)
    tile_keep = fetch(tilev.at[me], sums_out.at[me], tile_local)
    lax.fori_loop(21, 4 * packs + 4, lambda s, carry: (rs.step(s), carry)[1], 0)
    rs.finish()
    hidden_copy.wait()
    tile_keep.wait()
    tiles.wait()


def backward(whole, table, x, n1, n2, qkv, probs, pre, act, mid, gout, gffn, buckets, loss, heads):
    packs = whole.shape[2] // LANES
    tokens, width = x.shape
    seq = buckets.shape[0]
    micro = tokens // seq
    any_ = pl.BlockSpec(memory_space=pl.ANY)
    vmem = pl.BlockSpec(memory_space=pltpu.VMEM)
    S = jax.ShapeDtypeStruct
    V = pltpu.VMEM
    dma = pltpu.SemaphoreType.DMA
    outs = (
        S(whole.shape, BF), S((ROWS, whole.shape[2]), F32), S((tokens, width), BF), S((32, 8, 128), F32), S((32, 8, 128), F32),
        S((4, heads // 4, seq, seq), F32),
    )
    return pl.pallas_call(
        functools.partial(backward_kernel, packs, tokens, width, seq, heads),
        out_shape=outs,
        in_specs=[any_] * 12 + [vmem] * 2,
        out_specs=[any_] * 6,
        scratch_shapes=[
            V((tokens, width), BF), V((width, tokens), BF), V((tokens, width), F32), V((tokens, width), F32),
            V((2, 8 * ROWS, LANES), BF), V((2, tokens, 2 * CHUNK), F32), V((2, tokens, CHUNK), BF), V((tokens, 2 * CHUNK), BF),
            V((8 * ROWS, LANES), BF), V((tokens, 768), BF), V((micro, heads // 4, seq, seq), F32),
            V((tokens, 768), BF), V((heads, 32, seq), F32), V((1, width), F32), V((1, width), F32),
            V((8, width), F32), V((8, width), F32), V((32, 8, 128), F32),
            dma((4,)), dma((2,)), dma((2,)), dma((2,)), dma, dma((6,)), dma, dma((micro,)), dma, dma((2,)), dma, dma, dma,
        ] + scatter_scratch(packs),
        compiler_params=pltpu.CompilerParams(collective_id=2, has_side_effects=True, vmem_limit_bytes=67043328),
    )(whole, table, x, n1, n2, qkv, probs, pre, act, mid, gout, gffn, buckets, loss)


def tuned_body(
    hidden, teacher, cotangent, valid_mask, blocks, buckets, first_gain, query_weight, key_weight, value_weight,
    output_weight, second_gain, gate_weight, up_weight, down_weight, bias_table,
):
    micro, _, seq, width = hidden.shape
    tokens = micro * seq
    bucket_count, heads = bias_table.shape
    part = gate_weight.shape[1]
    cols = query_weight.shape[1]
    per = first_gain.shape[0]
    scale = float(tokens * 32 * width)
    valid = valid_mask.reshape(micro, seq)
    block_ids = blocks.reshape(micro, seq)
    weights = (query_weight, key_weight, value_weight, output_weight, gate_weight, up_weight, down_weight)
    own, tile = prepare(weights, first_gain, second_gain, valid)
    x = hidden.reshape(tokens, width)
    whole, table, n1, n2, qkv, probs, pre, act, mid, layer, gout, gffn, loss = forward(
        own, tile, x, teacher.reshape(tokens, width), cotangent.reshape(tokens, width), buckets, bias_table.astype(F32),
        block_ids, block_ids.reshape(tokens, 1), valid, valid.reshape(tokens, 1).astype(F32), scale,
    )
    _, shard, hidden_grad, _, sums, _ = backward(
        whole, table, x, n1, n2, qkv, probs, pre, act, mid, gout, gffn, buckets, loss, heads
    )
    sums = jnp.sum(sums, axis=0)
    me = lax.axis_index("fsdp") * 4 + lax.axis_index("dp")
    first = (me * per) % 128
    gain_one = lax.dynamic_slice(sums[0:2].reshape(256), (first,), (per,))
    gain_two = lax.dynamic_slice(sums[2:4].reshape(256), (first,), (per,))
    valid_total = jnp.sum(table[:, 4, 0])
    ff = [
        jnp.concatenate([shard[:, LANES * (j + 1) + i * CHUNK : LANES * (j + 1) + (i + 1) * CHUNK] for j in range(4)], axis=1)[:, :part]
        for i in range(3)
    ]
    at = [shard[:, i * cols : (i + 1) * cols] for i in range(4)]
    return (
        layer.reshape(hidden.shape),
        sums[4, 0] / (valid_total * width),
        hidden_grad.reshape(hidden.shape),
        gain_one, at[0], at[1], at[2], at[3], gain_two, ff[0], ff[1], ff[2],
        sums[5:8].reshape(heads, bucket_count).T,
    )


def solution(mesh):
    in_specs = (
        P(None, ("fsdp", "dp"), None, None),
        P(None, ("fsdp", "dp"), None, None),
        P(None, ("fsdp", "dp"), None, None),
        P(None, ("fsdp", "dp"), None),
        P(None, ("fsdp", "dp"), None),
        P(),
        P(("fsdp", "dp")),
        P("fsdp", "dp"),
        P("fsdp", "dp"),
        P("fsdp", "dp"),
        P("fsdp", "dp"),
        P(("fsdp", "dp")),
        P("fsdp", "dp"),
        P("fsdp", "dp"),
        P("fsdp", "dp"),
        P(),
    )
    out_specs = (
        P(None, ("fsdp", "dp"), None, None),
        P(),
        P(None, ("fsdp", "dp"), None, None),
        P(("fsdp", "dp")),
        P("fsdp", "dp"),
        P("fsdp", "dp"),
        P("fsdp", "dp"),
        P("fsdp", "dp"),
        P(("fsdp", "dp")),
        P("fsdp", "dp"),
        P("fsdp", "dp"),
        P("fsdp", "dp"),
        P(),
    )
    chosen = tuned_body if dict(mesh.shape) == {"fsdp": 8, "dp": 4} else body
    return jax.shard_map(chosen, mesh=mesh, in_specs=in_specs, out_specs=out_specs, check_vma=False)
```

```python
import functools
import jax
import jax.numpy as jnp
from jax import lax
from jax.experimental import pallas as pl
from jax.experimental.pallas import tpu as pltpu
from jax.sharding import PartitionSpec as P

EPS = 1e-06
NEG = -1000000000.0
HIGH = lax.Precision.HIGHEST


def times_rows(former, latter):
    return jnp.dot(former, latter, preferred_element_type=jnp.float32)


def times_transpose(former, latter):
    return lax.dot_general(
        former, latter, (((1,), (1,)), ((), ())), preferred_element_type=jnp.float32
    )


def over_tokens(former, latter):
    return lax.dot_general(
        former, latter, (((0,), (0,)), ((), ())), preferred_element_type=jnp.float32
    )


def assemble(gathered, fsdp_count, dp_count):
    row_block = gathered.shape[0] // (fsdp_count * dp_count)
    col_block = gathered.shape[1]
    shaped = gathered.reshape(fsdp_count, dp_count, row_block, col_block)
    return jnp.transpose(shaped, (0, 2, 1, 3)).reshape(fsdp_count * row_block, dp_count * col_block)


def disperse(gradient, fsdp_count, dp_count):
    row_block = gradient.shape[0] // fsdp_count
    col_block = gradient.shape[1] // dp_count
    shaped = gradient.reshape(fsdp_count, row_block, dp_count, col_block)
    return jnp.transpose(shaped, (0, 2, 1, 3)).reshape(fsdp_count * dp_count * row_block, col_block)


def norm_forward(inputs, norm_gain):
    row_scale = lax.rsqrt(jnp.mean(inputs * inputs, axis=-1, keepdims=True) + EPS)
    return (inputs * row_scale * norm_gain, row_scale)


def norm_backward(inputs, row_scale, norm_gain, upstream):
    scaled = upstream * norm_gain
    gain_grad = jnp.sum(upstream * inputs * row_scale, axis=0)
    mean_term = jnp.mean(scaled * inputs, axis=-1, keepdims=True)
    return (
        row_scale * scaled - inputs * (row_scale * row_scale * row_scale) * mean_term,
        gain_grad,
    )


def gelu_tanh(values_in):
    return jax.nn.gelu(values_in, approximate=True)


def masked_scores(queries, key_heads, position_bias, allowed):
    products = jnp.einsum("qhd,khd->hqk", queries, key_heads, preferred_element_type=jnp.float32)
    return jnp.where(allowed[None], products + position_bias, NEG)


def body(
    hidden,
    teacher,
    cotangent,
    valid_mask,
    blocks,
    buckets,
    first_gain,
    query_weight,
    key_weight,
    value_weight,
    output_weight,
    second_gain,
    gate_weight,
    up_weight,
    down_weight,
    bias_table,
):
    fsdp_count = lax.axis_size("fsdp")
    dp_count = lax.axis_size("dp")
    micro_count = hidden.shape[0]
    seq_len = hidden.shape[2]
    model_width = hidden.shape[3]
    bucket_count = bias_table.shape[0]
    head_count = bias_table.shape[1]
    scale_factor = jnp.float32(
        float(micro_count * lax.axis_size(("fsdp", "dp")) * hidden.shape[1] * seq_len * model_width)
    )
    valid_float = valid_mask.astype(jnp.float32)
    valid_total = lax.psum(jnp.sum(valid_float), ("fsdp", "dp"))
    places = lax.broadcasted_iota(jnp.int32, (1, 1, bucket_count), 2)
    onehot = (buckets[:, :, None] == places).astype(jnp.float32)
    position_bias = jnp.einsum(
        "qkb,bh->hqk", onehot, bias_table.astype(jnp.float32), precision=HIGH
    )
    onehot_low = onehot.astype(jnp.bfloat16)
    rows_iota = lax.broadcasted_iota(jnp.int32, (seq_len, seq_len), 0)
    cols_iota = lax.broadcasted_iota(jnp.int32, (seq_len, seq_len), 1)
    diagonal = rows_iota == cols_iota

    def rebuild(gathered):
        return (gathered[0],) + tuple(
            (assemble(matrix, fsdp_count, dp_count) for matrix in gathered[1:])
        )

    def spread_out(grads):
        return (
            (grads[0],)
            + tuple((disperse(matrix, fsdp_count, dp_count) for matrix in grads[1:5]))
            + (grads[5],)
            + tuple((disperse(matrix, fsdp_count, dp_count) for matrix in grads[6:]))
        )

    outputs_list = []
    input_grads = []
    squares = jnp.float32(0.0)
    table_grad = jnp.zeros((bucket_count, head_count), jnp.float32)
    totals = None
    for step_index in range(micro_count):
        inputs = hidden[step_index, 0].astype(jnp.float32)
        target = teacher[step_index, 0].astype(jnp.float32)
        upstream = cotangent[step_index, 0].astype(jnp.float32)
        token_valid = valid_float[step_index, 0]
        block_ids = blocks[step_index, 0]
        allowed = (block_ids[None, :] <= block_ids[:, None]) & (
            valid_mask[step_index, 0][None, :] == 1
        ) | diagonal
        first_block = rebuild(
            (
                lax.all_gather(first_gain, ("fsdp", "dp"), axis=0, tiled=True),
                lax.all_gather(query_weight, ("fsdp", "dp"), axis=0, tiled=True),
                lax.all_gather(key_weight, ("fsdp", "dp"), axis=0, tiled=True),
                lax.all_gather(value_weight, ("fsdp", "dp"), axis=0, tiled=True),
                lax.all_gather(output_weight, ("fsdp", "dp"), axis=0, tiled=True),
            )
        )
        gain_one = first_block[0].astype(jnp.float32)
        normed_full, scale_one = norm_forward(inputs, gain_one)
        normed_one = normed_full.astype(jnp.bfloat16)
        head_size = first_block[1].shape[1] // head_count
        head_split = (seq_len, head_count, head_size)
        queries = times_rows(normed_one, first_block[1]).astype(jnp.bfloat16).reshape(head_split)
        key_heads = times_rows(normed_one, first_block[2]).astype(jnp.bfloat16).reshape(head_split)
        value_heads = (
            times_rows(normed_one, first_block[3]).astype(jnp.bfloat16).reshape(head_split)
        )
        scores = masked_scores(queries, key_heads, position_bias, allowed)
        row_max = jnp.max(scores, axis=-1, keepdims=True)
        exponent = jnp.exp(scores - row_max)
        row_total = jnp.sum(exponent, axis=-1, keepdims=True)
        log_total = row_max + jnp.log(row_total)
        softmax_low = (exponent / row_total).astype(jnp.bfloat16)
        attended = jnp.einsum(
            "hqk,khd->qhd", softmax_low, value_heads, preferred_element_type=jnp.float32
        )
        attended = attended.astype(jnp.bfloat16).reshape(seq_len, head_count * head_size)
        middle = inputs + times_transpose(attended, first_block[4])
        second_block = rebuild(
            (
                lax.all_gather(second_gain, ("fsdp", "dp"), axis=0, tiled=True),
                lax.all_gather(gate_weight, ("fsdp", "dp"), axis=0, tiled=True),
                lax.all_gather(up_weight, ("fsdp", "dp"), axis=0, tiled=True),
                lax.all_gather(down_weight, ("fsdp", "dp"), axis=0, tiled=True),
            )
        )
        gain_two = second_block[0].astype(jnp.float32)
        normed_mid, scale_two = norm_forward(middle, gain_two)
        normed_two = normed_mid.astype(jnp.bfloat16)
        gate_pre = times_rows(normed_two, second_block[1])
        up_pre = times_rows(normed_two, second_block[2])
        gate_act, gelu_pullback = jax.vjp(gelu_tanh, gate_pre)
        hidden_act = (gate_act * up_pre).astype(jnp.bfloat16)
        layer_full = middle + times_transpose(hidden_act, second_block[3])
        outputs_list.append(layer_full.astype(jnp.bfloat16))
        residual_gap = layer_full - target
        weighted_gap = token_valid[:, None] * residual_gap
        squares = squares + jnp.sum(weighted_gap * residual_gap)
        grad_out = scale_factor * upstream + scale_factor * (
            2.0 * weighted_gap / (valid_total * model_width)
        )
        back_second = rebuild(
            (
                lax.all_gather(second_gain, ("fsdp", "dp"), axis=0, tiled=True),
                lax.all_gather(gate_weight, ("fsdp", "dp"), axis=0, tiled=True),
                lax.all_gather(up_weight, ("fsdp", "dp"), axis=0, tiled=True),
                lax.all_gather(down_weight, ("fsdp", "dp"), axis=0, tiled=True),
            )
        )
        grad_ffn = grad_out.astype(jnp.bfloat16)
        down_part = over_tokens(grad_ffn, hidden_act)
        grad_hidden_act = times_rows(grad_ffn, back_second[3])
        grad_gate = gelu_pullback(grad_hidden_act * up_pre)[0].astype(jnp.bfloat16)
        grad_up = (grad_hidden_act * gate_act).astype(jnp.bfloat16)
        gate_part = over_tokens(normed_two, grad_gate)
        up_part = over_tokens(normed_two, grad_up)
        grad_normed_two = times_transpose(grad_gate, back_second[1]) + times_transpose(
            grad_up, back_second[2]
        )
        middle_term, gain_two_part = norm_backward(
            middle, scale_two, back_second[0].astype(jnp.float32), grad_normed_two
        )
        grad_middle = grad_out + middle_term
        grad_attn = grad_middle.astype(jnp.bfloat16)
        back_first = rebuild(
            (
                lax.all_gather(first_gain, ("fsdp", "dp"), axis=0, tiled=True),
                lax.all_gather(query_weight, ("fsdp", "dp"), axis=0, tiled=True),
                lax.all_gather(key_weight, ("fsdp", "dp"), axis=0, tiled=True),
                lax.all_gather(value_weight, ("fsdp", "dp"), axis=0, tiled=True),
                lax.all_gather(output_weight, ("fsdp", "dp"), axis=0, tiled=True),
            )
        )
        output_part = over_tokens(grad_attn, attended)
        grad_attended = (
            times_rows(grad_attn, back_first[4]).astype(jnp.bfloat16).reshape(head_split)
        )
        scores_again = masked_scores(queries, key_heads, position_bias, allowed)
        softmax_again = jnp.exp(scores_again - log_total)
        grad_probs = jnp.einsum(
            "qhd,khd->hqk", grad_attended, value_heads, preferred_element_type=jnp.float32
        )
        grad_scores = softmax_again * (
            grad_probs - jnp.sum(softmax_again * grad_probs, axis=-1, keepdims=True)
        )
        grad_scores = grad_scores.astype(jnp.bfloat16)
        table_grad = table_grad + jnp.einsum(
            "hqk,qkb->bh", grad_scores, onehot_low, preferred_element_type=jnp.float32
        )
        flat_width = head_count * head_size
        grad_queries = (
            jnp.einsum("hqk,khd->qhd", grad_scores, key_heads, preferred_element_type=jnp.float32)
            .astype(jnp.bfloat16)
            .reshape(seq_len, flat_width)
        )
        grad_keys = (
            jnp.einsum("hqk,qhd->khd", grad_scores, queries, preferred_element_type=jnp.float32)
            .astype(jnp.bfloat16)
            .reshape(seq_len, flat_width)
        )
        grad_values = (
            jnp.einsum(
                "hqk,qhd->khd",
                softmax_again.astype(jnp.bfloat16),
                grad_attended,
                preferred_element_type=jnp.float32,
            )
            .astype(jnp.bfloat16)
            .reshape(seq_len, flat_width)
        )
        query_part = over_tokens(normed_one, grad_queries)
        key_part = over_tokens(normed_one, grad_keys)
        value_part = over_tokens(normed_one, grad_values)
        grad_normed_one = (
            times_transpose(grad_queries, back_first[1])
            + times_transpose(grad_keys, back_first[2])
            + times_transpose(grad_values, back_first[3])
        )
        input_term, gain_one_part = norm_backward(
            inputs, scale_one, back_first[0].astype(jnp.float32), grad_normed_one
        )
        input_grads.append((grad_middle + input_term).astype(jnp.bfloat16))
        step_set = spread_out(
            (
                gain_one_part,
                query_part,
                key_part,
                value_part,
                output_part,
                gain_two_part,
                gate_part,
                up_part,
                down_part,
            )
        )
        totals = step_set if totals is None else jax.tree.map(jnp.add, totals, step_set)
    shards = (
        lax.psum_scatter(totals[0], ("fsdp", "dp"), scatter_dimension=0, tiled=True),
        lax.psum_scatter(totals[1], ("fsdp", "dp"), scatter_dimension=0, tiled=True),
        lax.psum_scatter(totals[2], ("fsdp", "dp"), scatter_dimension=0, tiled=True),
        lax.psum_scatter(totals[3], ("fsdp", "dp"), scatter_dimension=0, tiled=True),
        lax.psum_scatter(totals[4], ("fsdp", "dp"), scatter_dimension=0, tiled=True),
        lax.psum_scatter(totals[5], ("fsdp", "dp"), scatter_dimension=0, tiled=True),
        lax.psum_scatter(totals[6], ("fsdp", "dp"), scatter_dimension=0, tiled=True),
        lax.psum_scatter(totals[7], ("fsdp", "dp"), scatter_dimension=0, tiled=True),
        lax.psum_scatter(totals[8], ("fsdp", "dp"), scatter_dimension=0, tiled=True),
    )
    total_squares, table_all = lax.psum((squares, table_grad), ("fsdp", "dp"))
    loss_value = total_squares / (valid_total * model_width)
    layer_output = jnp.stack(outputs_list)[:, None]
    hidden_grad = jnp.stack(input_grads)[:, None]
    return (
        layer_output,
        loss_value,
        hidden_grad,
        shards[0],
        shards[1],
        shards[2],
        shards[3],
        shards[4],
        shards[5],
        shards[6],
        shards[7],
        shards[8],
        table_all,
    )


MESH_ID = pl.DeviceIdType.MESH
LANES = 768
ROWS = 192


def place():
    f = lax.axis_index("fsdp")
    d = lax.axis_index("dp")
    return f // 2, f % 2, d // 2, d % 2


def device(z, x, y, c):
    return (z * 2 + x, y * 2 + c)


def tell_all():
    f = lax.axis_index("fsdp")
    d = lax.axis_index("dp")
    barrier = pltpu.get_barrier_semaphore()

    def tell(step, carry):
        other = (f * 4 + d + step) % 32
        pl.semaphore_signal(
            barrier, inc=1, device_id=(other // 4, other % 4), device_id_type=MESH_ID
        )
        return carry

    lax.fori_loop(1, 32, tell, 0)


def hear_all():
    pl.semaphore_wait(pltpu.get_barrier_semaphore(), 31)


def start_barrier():
    tell_all()
    hear_all()


def exchange(tile_of, table, send, recv):
    f = lax.axis_index("fsdp")
    d = lax.axis_index("dp")
    me = f * 4 + d

    def one(step, carry):
        other = (me + step) % 32
        pltpu.make_async_remote_copy(
            tile_of(other), table.at[me], send, recv,
            device_id=(other // 4, other % 4), device_id_type=MESH_ID,
        ).start()
        return carry

    lax.fori_loop(1, 32, one, 0)
    view = table.at[pl.ds(0, 31)]
    return pltpu.make_async_remote_copy(
        view, view, send, recv, device_id=(f, (d + 1) % 4), device_id_type=MESH_ID
    )


def lanes_of(pack):
    return pl.ds(pl.multiple_of(pack * LANES, 128), LANES)


def rows_of(z, x, first, count):
    return pl.ds(pl.multiple_of((z * 2 + x) * ROWS + first, 32), count)


G_Z, G_X0, G_Y0, G_XZ, G_YZ, G_DY, G_DX = 0, 4, 5, 6, 10, 14, 18
G_XA, G_XB, G_YA, G_YB, G_C, G_BACK = 22, 25, 28, 31, 34, 50
G_COUNT = 53


def on_chain(z, k):
    end = (3 - z) // 3 + z // 3
    low = end * k + (1 - end) * (k - (3 - k) // 2)
    high = z // 2
    return high * (3 - low) + (1 - high) * low


class Gather:
    def __init__(self, own, whole, send, recv, packs):
        self.own, self.whole, self.send, self.recv, self.packs = own, whole, send, recv, packs
        self.z, self.x, self.y, self.c = place()

    def put(self, pack, slot, shard, first, count, target, own=False, send=None):
        zz, xx, yy = shard
        there = self.whole.at[yy * 2 + self.c, rows_of(zz, xx, first, count), lanes_of(pack)]
        here = self.own.at[pl.ds(first, count), lanes_of(pack)] if own else there
        pltpu.make_async_remote_copy(
            here, there, self.send.at[pack, slot if send is None else send], self.recv.at[pack, slot],
            device_id=device(*target), device_id_type=MESH_ID,
        ).start()

    def along(self, pack, slot, back, shard, first, count, own=False):
        z, x, y, c = self.z, self.x, self.y, self.c
        pl.when(z < 3)(lambda: self.put(pack, slot + z, shard, first, count, (z + 1, x, y, c), own=own))
        pl.when(z > 0)(lambda: self.put(pack, slot + z, shard, first, count, (z - 1, x, y, c), own=own, send=back))

    def further(self, pack, slot, shard, first, count):
        z, x, y, c = self.z, self.x, self.y, self.c
        zz = shard[0]
        pl.when((zz < z) & (z < 3))(lambda: self.put(pack, slot + zz, shard, first, count, (z + 1, x, y, c)))
        pl.when((zz > z) & (z > 0))(lambda: self.put(pack, slot + zz, shard, first, count, (z - 1, x, y, c)))

    def some(self, pack, slot, count):
        view = self.whole.at[0, pl.ds(0, count), lanes_of(pack)]
        return pltpu.make_async_remote_copy(
            view, view, self.send.at[pack, slot], self.recv.at[pack, slot],
            device_id=device(self.z, self.x, self.y, 1 - self.c), device_id_type=MESH_ID,
        )

    def got(self, pack, slot, count):
        self.some(pack, slot, count).wait_recv()

    def launch(self, pack):
        self.along(pack, G_Z, G_BACK, (self.z, self.x, self.y), 0, 192, own=True)

    def first(self, pack, k):
        z, x, y, c = self.z, self.x, self.y, self.c
        xn, yn, cn = (z, 1 - x, y, c), (z, x, 1 - y, c), (z, x, y, 1 - c)

        @pl.when(k == 0)
        def _():
            self.put(pack, G_X0, (z, x, y), 0, 192, xn, own=True)
            self.put(pack, G_Y0, (z, x, y), 0, 192, yn, own=True)
            self.put(pack, G_C, (z, x, y), 0, 192, cn, own=True)

        @pl.when(k > 0)
        def _():
            zz = on_chain(z, k)
            mine = (zz, x, y)
            self.got(pack, G_Z + zz, 192)
            self.further(pack, G_Z, mine, 0, 192)
            self.put(pack, G_XA + k - 1, mine, 0, 32, xn)
            self.put(pack, G_YA + k - 1, mine, 160, 32, yn)
            self.put(pack, G_XB + k - 1, mine, 96, 96, xn)
            self.put(pack, G_YB + k - 1, mine, 0, 96, yn)
            self.put(pack, G_C + 4 * k, mine, 0, 192, cn)

    def second(self, pack, k):
        z, x, y, c = self.z, self.x, self.y, self.c
        xn, yn, cn = (z, 1 - x, y, c), (z, x, 1 - y, c), (z, x, y, 1 - c)

        @pl.when(k == 0)
        def _():
            self.got(pack, G_X0, 192)
            self.along(pack, G_XZ, G_BACK + 1, (z, 1 - x, y), 32, 64)
            self.put(pack, G_DY, (z, 1 - x, y), 0, 96, yn)
            self.put(pack, G_C + 1, (z, 1 - x, y), 0, 192, cn)
            self.got(pack, G_Y0, 192)
            self.along(pack, G_YZ, G_BACK + 2, (z, x, 1 - y), 96, 64)
            self.put(pack, G_DX, (z, x, 1 - y), 96, 96, xn)
            self.put(pack, G_C + 2, (z, x, 1 - y), 0, 192, cn)

        @pl.when(k > 0)
        def _():
            zz = on_chain(z, k)
            across_x, across_y = (zz, 1 - x, y), (zz, x, 1 - y)
            self.got(pack, G_XZ + zz, 64)
            self.further(pack, G_XZ, across_x, 32, 64)
            self.got(pack, G_YZ + zz, 64)
            self.further(pack, G_YZ, across_y, 96, 64)
            self.got(pack, G_XA + k - 1, 32)
            self.put(pack, G_DY + k, across_x, 0, 96, yn)
            self.got(pack, G_YA + k - 1, 32)
            self.put(pack, G_DX + k, across_y, 96, 96, xn)
            self.got(pack, G_XB + k - 1, 96)
            self.put(pack, G_C + 4 * k + 1, across_x, 0, 192, cn)
            self.got(pack, G_YB + k - 1, 96)
            self.put(pack, G_C + 4 * k + 2, across_y, 0, 192, cn)

    def third(self, pack, k):
        z, x, y, c = self.z, self.x, self.y, self.c
        self.got(pack, G_DY + k, 96)
        self.got(pack, G_DX + k, 96)

        def on(zz):
            self.put(pack, G_C + 4 * k + 3, (zz, 1 - x, 1 - y), 0, 192, (z, x, y, 1 - c))

        pl.when(k == 0)(lambda: on(z))
        pl.when(k > 0)(lambda: on(on_chain(z, k)))

    def step(self, s):
        total = 4 * self.packs

        @pl.when(s < total)
        def _():
            self.first(s // 4, s % 4)
            pl.when((s % 4 == 3) & (s + 1 < total))(lambda: self.launch(s // 4 + 1))

        pl.when((s >= 2) & (s <= total + 1))(lambda: self.second((s + 2) // 4 - 1, (s + 2) % 4))
        pl.when((s >= 4) & (s <= total + 3))(lambda: self.third(s // 4 - 1, s % 4))

    def arrived(self, pack):
        for slot in range(G_C, G_C + 16):
            self.got(pack, slot, 192)

    def finish(self):
        z = self.z

        def sent(pack, slot, count):
            self.some(pack, slot, count).wait_send()

        def one(pack, carry):
            for slot, count in ((G_X0, 192), (G_Y0, 192)):
                sent(pack, slot, count)
            for base, n, count in (
                (G_DY, 4, 96), (G_DX, 4, 96), (G_XA, 3, 32), (G_XB, 3, 96), (G_YA, 3, 32), (G_YB, 3, 96), (G_C, 16, 192),
            ):
                for i in range(n):
                    sent(pack, base + i, count)
            for i, (base, count) in enumerate(((G_Z, 192), (G_XZ, 64), (G_YZ, 64))):
                pl.when(z > 0)(lambda: sent(pack, G_BACK + i, count))
                for zz in range(4):
                    pl.when((zz <= z) & (z < 3))(lambda: sent(pack, base + zz, count))
                    pl.when((zz > z) & (z > 0))(lambda: sent(pack, base + zz, count))
            return carry

        lax.fori_loop(0, self.packs, one, 0)


R_C, R_V, R_U, R_ZC, R_Z, R_F = 0, 16, 32, 38, 48, 53
R_COUNT = 55
R_ROWS = [192] * 16 + [96] * 16 + [32] * 6 + [64] * 10 + [192] * 5 + [96] * 2
ORDER = (3, 2, 1, 0)
TILE = 32


def add_rows(into, what, count):
    size = 96 if count % 96 == 0 else count

    def one(t, carry):
        r = pl.ds(pl.multiple_of(t * size, 32), size)
        into[r] = into[r] + what[r]
        return carry

    if count == size:
        into[...] = into[...] + what[...]
    else:
        lax.fori_loop(0, count // size, one, 0)


class Scatter:
    def __init__(self, part, out, mine, buf_c, buf_v, buf_u, buf_zc, buf_z, buf_f, send, recv, load, credit, stage, out_sem, packs):
        self.stage, self.out_sem = stage, out_sem
        self.part, self.out, self.mine = part, out, mine
        self.buf_c, self.buf_v, self.buf_u, self.buf_zc, self.buf_z, self.buf_f = buf_c, buf_v, buf_u, buf_zc, buf_z, buf_f
        self.send, self.recv, self.load_sem, self.credit, self.packs = send, recv, load, credit, packs
        self.z, self.x, self.y, self.c = place()
        z, x, y, c = place()
        self.xn, self.yn, self.cn = (z, 1 - x, y, c), (z, x, 1 - y, c), (z, x, y, 1 - c)

    def at(self, par, shard, first, count):
        zz, xx, yy = shard
        return self.mine.at[par, yy, rows_of(zz, xx, first, count)]

    def put(self, par, slot, here, there, target):
        pltpu.make_async_remote_copy(
            here, there, self.send.at[par, slot], self.recv.at[par, slot],
            device_id=device(*target), device_id_type=MESH_ID,
        ).start()

    def some(self, par, slot, count):
        view = self.mine.at[par, 0, pl.ds(0, count)]
        return pltpu.make_async_remote_copy(
            view, view, self.send.at[par, slot], self.recv.at[par, slot],
            device_id=device(*self.cn), device_id_type=MESH_ID,
        )

    def got(self, par, slot, count):
        self.some(par, slot, count).wait_recv()

    def lane_pack(self, pack):
        return (pack + 1) % self.packs

    def dest(self, k):
        if isinstance(k, int):
            return self.z if k == 0 else on_chain(self.z, k)
        none = (3 - k) // 3
        return none * self.z + (1 - none) * on_chain(self.z, k)

    def slot_to(self, zz):
        apart = zz - self.z + 4
        home = (apart // 3) * (1 - apart // 4)
        return zz * (1 - home) + 4 * home

    def onward(self, par, base, buf, j, zz, here):
        z, x, y, c = self.z, self.x, self.y, self.c
        slot = self.slot_to(zz)
        there = buf.at[par, slot] if j is None else buf.at[par, slot, j]
        number = base + (slot if j is None else 2 * slot + j)
        pl.when(zz > z)(lambda: self.put(par, number, here, there, (z + 1, x, y, c)))
        pl.when(zz < z)(lambda: self.put(par, number, here, there, (z - 1, x, y, c)))

    def shards(self, k):
        zz = self.dest(k)
        return ((zz, 1 - self.x, 1 - self.y), (zz, self.x, 1 - self.y), (zz, 1 - self.x, self.y), (zz, self.x, self.y))

    def loads(self, pack):
        par = pack % 2
        return [
            pltpu.make_async_copy(
                self.part.at[yy * 2 + self.c, :, lanes_of(self.lane_pack(pack))], self.mine.at[par, yy], self.load_sem.at[yy]
            )
            for yy in range(2)
        ]

    def ahead(self, s):
        pack = s // 4
        k = 3 - s % 4
        par = pack % 2
        if not isinstance(s, int):
            pl.when((pack >= 2) & (s % 4 == 0))(lambda: pl.semaphore_wait(self.credit.at[pack - 2, 0], 1))
        for i, (zz, xx, yy) in enumerate(self.shards(k)):
            rows = rows_of(zz, xx, 0, 192)
            slot = R_C + 4 * k + i
            if not isinstance(s, int):
                pl.when(pack >= 2)(lambda: self.some(par, slot, 192).wait_send())
            self.put(
                par, slot,
                self.part.at[yy * 2 + 1 - self.c, rows, lanes_of(self.lane_pack(pack))],
                self.buf_c.at[par, yy, rows], self.cn,
            )

    def launch(self):
        self.ahead(0)
        self.ahead(1)
        self.load(0)

    def load(self, pack):
        for r in self.loads(pack):
            r.start()

    def sent(self, pack, first, last):
        for slot in range(first, last):
            self.some(pack % 2, slot, R_ROWS[slot]).wait_send()

    def core(self, pack, k):
        par = pack % 2
        sh = self.shards(k)

        @pl.when(k == ORDER[0])
        def _():
            for r in self.loads(pack):
                r.wait()
            pl.when(pack >= 2)(lambda: pl.semaphore_wait(self.credit.at[pack - 2, 1], 5))

        for i, (zz, xx, yy) in enumerate(sh):
            self.got(par, R_C + 4 * k + i, 192)
            add_rows(self.at(par, sh[i], 0, 192), self.buf_c.at[par, yy, rows_of(zz, xx, 0, 192)], 192)
        pl.when((k == ORDER[3]) & (pack + 2 < self.packs))(lambda: self.free(pack, 0, self.cn))
        v = self.buf_v
        self.put(par, R_V + 4 * k, self.at(par, sh[0], 0, 96), v.at[par, k, 0], self.yn)
        self.put(par, R_V + 4 * k + 1, self.at(par, sh[0], 96, 96), v.at[par, k, 1], self.xn)
        self.put(par, R_V + 4 * k + 2, self.at(par, sh[1], 0, 96), v.at[par, k, 2], self.yn)
        self.put(par, R_V + 4 * k + 3, self.at(par, sh[2], 96, 96), v.at[par, k, 3], self.xn)

    def free(self, pack, kind, target):
        pl.semaphore_signal(
            self.credit.at[pack, kind], inc=1, device_id=device(*target), device_id_type=MESH_ID
        )

    def vees(self, pack, k):
        par = pack % 2
        sh = self.shards(k)
        zz = self.dest(k)
        end = (self.z == 0) | (self.z == 3)
        v = self.buf_v
        self.got(par, R_V + 4 * k, 96)
        add_rows(self.at(par, sh[2], 0, 96), v.at[par, k, 0], 96)

        @pl.when(k > 0)
        def _():
            self.put(par, R_U + 2 * (k - 1), self.at(par, sh[2], 0, 32), self.buf_u.at[par, k - 1, 0], self.xn)
            pl.when(end)(lambda: self.onward(par, R_ZC, self.buf_zc, 0, zz, self.at(par, sh[2], 32, 64)))

        self.got(par, R_V + 4 * k + 1, 96)
        add_rows(self.at(par, sh[1], 96, 96), v.at[par, k, 1], 96)

        @pl.when(k > 0)
        def _():
            self.put(par, R_U + 2 * (k - 1) + 1, self.at(par, sh[1], 160, 32), self.buf_u.at[par, k - 1, 1], self.yn)
            pl.when(end)(lambda: self.onward(par, R_ZC, self.buf_zc, 1, zz, self.at(par, sh[1], 96, 64)))
            self.got(par, R_V + 4 * k + 2, 96)
            add_rows(self.at(par, sh[3], 0, 96), v.at[par, k, 2], 96)
            self.got(par, R_V + 4 * k + 3, 96)
            add_rows(self.at(par, sh[3], 96, 96), v.at[par, k, 3], 96)

    def yous(self, pack, k):
        par = pack % 2
        sh = self.shards(k)
        zz = self.dest(k)
        end = (self.z == 0) | (self.z == 3)

        @pl.when((self.z > 0) & (self.z < 3))
        def _():
            for j, (shard, first) in enumerate(((sh[2], 32), (sh[1], 96))):
                self.got(par, R_ZC + 2 * zz + j, 64)
                add_rows(self.at(par, shard, first, 64), self.buf_zc.at[par, zz, j], 64)
                self.onward(par, R_ZC, self.buf_zc, j, zz, self.at(par, shard, first, 64))

        self.got(par, R_U + 2 * (k - 1), 32)
        add_rows(self.at(par, sh[3], 0, 32), self.buf_u.at[par, k - 1, 0], 32)
        self.got(par, R_U + 2 * (k - 1) + 1, 32)
        add_rows(self.at(par, sh[3], 160, 32), self.buf_u.at[par, k - 1, 1], 32)
        pl.when(end)(lambda: self.onward(par, R_Z, self.buf_z, None, zz, self.at(par, sh[3], 0, 192)))

    def chain(self, pack, k):
        par = pack % 2
        sh = self.shards(k)
        zz = self.dest(k)

        @pl.when((self.z > 0) & (self.z < 3))
        def _():
            self.got(par, R_Z + zz, 192)
            add_rows(self.at(par, sh[3], 0, 192), self.buf_z.at[par, zz], 192)
            self.onward(par, R_Z, self.buf_z, None, zz, self.at(par, sh[3], 0, 192))

    def near(self, pack):
        par = pack % 2
        sh = self.shards(0)
        z = self.z
        for j, (shard, first, whole, nb) in enumerate(((sh[2], 32, 0, self.xn), (sh[1], 96, 96, self.yn))):
            into = self.at(par, shard, first, 64)

            @pl.when(z > 0)
            def _(j=j, into=into):
                self.got(par, R_ZC + 2 * z + j, 64)
                add_rows(into, self.buf_zc.at[par, z, j], 64)

            @pl.when(z < 3)
            def _(j=j, into=into):
                self.got(par, R_ZC + 8 + j, 64)
                add_rows(into, self.buf_zc.at[par, 4, j], 64)

            self.put(par, R_F + j, self.at(par, shard, whole, 96), self.buf_f.at[par, j], nb)

    def out_copy(self, pack):
        return pltpu.make_async_copy(self.stage, self.out.at[:, lanes_of(self.lane_pack(pack))], self.out_sem)

    def final(self, pack):
        par = pack % 2
        own = self.at(par, self.shards(0)[3], 0, 192)
        self.got(par, R_V + 2, 96)
        self.got(par, R_V + 3, 96)
        for j in range(2):
            self.got(par, R_F + j, 96)

        pl.when(pack > 0)(lambda: self.out_copy(pack).wait())
        for j in range(2):
            def one(t, carry, j=j):
                r = pl.ds(pl.multiple_of(t * TILE, TILE), TILE)
                rr = pl.ds(pl.multiple_of(j * 96 + t * TILE, TILE), TILE)
                total = own[rr].astype(jnp.float32) + self.buf_v[par, 0, 2 + j, r].astype(jnp.float32)
                total = total + self.buf_f[par, j, r].astype(jnp.float32)
                self.stage[rr] = total
                return carry
            lax.fori_loop(0, 96 // TILE, one, 0)
        def more(slot):
            self.got(par, R_Z + slot, 192)

            def one(t, carry):
                rr = pl.ds(pl.multiple_of(t * TILE, TILE), TILE)
                self.stage[rr] += self.buf_z[par, slot, rr].astype(jnp.float32)
                return carry

            lax.fori_loop(0, ROWS // TILE, one, 0)

        pl.when(self.z > 0)(lambda: more(self.z))
        pl.when(self.z < 3)(lambda: more(4))
        self.out_copy(pack).start()
        self.sent(pack, R_V, R_ZC)
        self.sent(pack, R_F, R_COUNT)
        for k in (1, 2, 3):
            slot = self.slot_to(self.dest(k))
            self.some(par, R_Z + slot, 192).wait_send()
            for j in range(2):
                self.some(par, R_ZC + 2 * slot + j, 64).wait_send()

        @pl.when(pack + 2 < self.packs)
        def _():
            z, x, y, c = self.z, self.x, self.y, self.c
            for t in (self.xn, self.yn) + tuple(((z + k) % 4, x, y, c) for k in (1, 2, 3)):
                self.free(pack, 1, t)

    def step(self, s):
        total = 4 * self.packs
        pl.when(s < total)(lambda: self.core(s // 4, 3 - s % 4))
        pl.when((s >= 1) & (s <= total))(lambda: self.vees((s + 3) // 4 - 1, 3 - (s + 3) % 4))

        @pl.when((s >= 2) & (s <= total + 1))
        def _():
            before = (s + 2) // 4 - 1
            k = 3 - (s + 2) % 4
            pl.when(k > 0)(lambda: self.yous(before, k))
            pl.when(k == 0)(lambda: self.near(before))

        @pl.when((s >= 3) & (s <= total + 2))
        def _():
            before = (s + 1) // 4 - 1
            k = 3 - (s + 1) % 4
            pl.when(k > 0)(lambda: self.chain(before, k))
            pl.when(k == 0)(lambda: self.final(before))

        more = s + 2
        due = (more < total - 4) | ((more >= total - 2) & (more < total))
        if not isinstance(s, int):
            pl.when(due)(lambda: self.ahead(more))
        elif due:
            self.ahead(jnp.int32(more))
        later = s // 4 + 1
        pl.when((s % 4 == 3) & (later < self.packs))(lambda: self.load(later))

    def finish(self):
        self.out_copy(self.packs - 1).wait()
        for pack in (self.packs - 2, self.packs - 1):
            self.sent(pack, R_C, R_V)


def scatter_scratch(packs):
    bf = jnp.bfloat16
    return [
        pltpu.VMEM((2, 2, 8 * ROWS, LANES), bf),
        pltpu.VMEM((2, 2, 8 * ROWS, LANES), bf),
        pltpu.VMEM((2, 4, 4, 96, LANES), bf),
        pltpu.VMEM((2, 3, 2, 32, LANES), bf),
        pltpu.VMEM((2, 5, 2, 64, LANES), bf),
        pltpu.VMEM((2, 5, 192, LANES), bf),
        pltpu.VMEM((2, 2, 96, LANES), bf),
        pltpu.SemaphoreType.DMA((2, R_COUNT)),
        pltpu.SemaphoreType.DMA((2, R_COUNT)),
        pltpu.SemaphoreType.DMA((2,)),
        pltpu.SemaphoreType.REGULAR((packs, 2)),
        pltpu.VMEM((ROWS, LANES), jnp.float32),
        pltpu.SemaphoreType.DMA,
    ]


BF = jnp.bfloat16
F32 = jnp.float32
CHUNK = 256


def gain_rows(table, line, into):
    lines = [None] * 13
    for i in range(32):
        first = (48 * i) // 128
        for j in range(2):
            got = table[i, line + j : line + j + 1, :]
            lines[first + j] = got if lines[first + j] is None else lines[first + j] + got
    for r in range(12):
        into[:, 128 * r : 128 * (r + 1)] = lines[r]


def loop(count, body):
    def one(t, carry):
        body(t)
        return carry

    lax.fori_loop(0, count, one, 0)


def tile_rows(t, size):
    return pl.ds(pl.multiple_of(t * size, size), size)


def norm_rows(src, gain, into, tokens):
    def one(t):
        r = tile_rows(t, 32)
        v = src[r].astype(F32)
        scale = lax.rsqrt(jnp.mean(v * v, axis=-1, keepdims=True) + EPS)
        into[r] = (v * scale * gain[...]).astype(BF)

    loop(tokens // 32, one)


def turn(src, into, tokens):
    def one(t):
        r = tile_rows(t, 128)
        into[:, r] = jnp.transpose(src[r])

    loop(tokens // 128, one)


def gelu_parts(u):
    root = 0.7978845608028654
    t = jnp.tanh(root * (u + 0.044715 * (u * u * u)))
    return 0.5 * u * (1.0 + t), t


def nt(a, b):
    return lax.dot_general(a, b, (((1,), (1,)), ((), ())), preferred_element_type=F32)


def tn(a, b):
    return lax.dot_general(a, b, (((0,), (0,)), ((), ())), preferred_element_type=F32)


def nn(a, b):
    return jnp.dot(a, b, preferred_element_type=F32)


def forward_kernel(
    packs, tokens, width, seq, heads, scale,
    own, tile, x_any, teacher_any, cotangent_any, buckets, bias_smem, blocks_row, blocks_col, valid_row, valid_col,
    whole, table, n1_out, n2_out, qkv_out, probs_out, pre_out, act_out, middle_out, layer_out, grad_out, gffn_out, loss_out,
    x, n1, n2, turned, acc, bias, mask, wbuf, qs, ps, pre, act, tabv, gain1, gain2, teach, cot, lossv,
    send, recv, local, tile_send, tile_recv, tile_local, in_sem, w_sem, p_sem, q_sem, pre_sem, act_sem, out_sem,
):
    f = lax.axis_index("fsdp")
    d = lax.axis_index("dp")
    micro = tokens // seq
    per = heads // 4
    size = 192 // per
    start_barrier()
    g = Gather(own, whole, send, recv, packs)
    g.launch(0)
    tiles = exchange(lambda other: tile, table, tile_send, tile_recv)
    tile_keep = pltpu.make_async_copy(tile, table.at[f * 4 + d], tile_local)
    tile_keep.start()
    bounce = [
        pltpu.make_async_copy(own.at[:, pl.ds(p * LANES, LANES)], wbuf.at[1, pl.ds(p * ROWS, ROWS)], local.at[p])
        for p in range(packs)
    ]
    keep = [
        pltpu.make_async_copy(
            wbuf.at[1, pl.ds(p * ROWS, ROWS)],
            whole.at[d, pl.ds(pl.multiple_of(f * ROWS, ROWS), ROWS), pl.ds(p * LANES, LANES)],
            local.at[p],
        )
        for p in range(packs)
    ]
    for r in bounce:
        r.start()
    load_x = pltpu.make_async_copy(x_any, x, in_sem.at[0])
    load_x.start()
    g.step(0)
    for a, b in zip(bounce, keep):
        a.wait()
        b.start()
    rows_i = lax.broadcasted_iota(jnp.int32, (seq, seq), 0)
    cols_i = lax.broadcasted_iota(jnp.int32, (seq, seq), 1)
    for m in range(micro):
        ok = (blocks_row[m : m + 1, :] <= blocks_col[m * seq : (m + 1) * seq, :]) & (valid_row[m : m + 1, :] == 1)
        mask[m] = jnp.where(ok | (rows_i == cols_i), 1.0, 0.0)

    def bias_tile(t):
        r = tile_rows(t, 8)
        b = buckets[r]
        totals = [jnp.zeros((8, seq), F32)] * heads
        for k in range(32):
            here = b == k
            totals = [jnp.where(here, bias_smem[k, h], v) for h, v in enumerate(totals)]
        for h in range(heads):
            bias[h, r] = totals[h]

    step_tiles = -(-(seq // 8) // 7)

    def early(s):
        def some(i):
            t = s * step_tiles + i
            pl.when(t < seq // 8)(lambda: bias_tile(t))

        loop(step_tiles, some)
        g.step(s + 1)

    loop(7, early)
    tile_keep.wait()
    tiles.wait()
    load_table = pltpu.make_async_copy(table, tabv, in_sem.at[1])
    load_table.start()
    load_x.wait()
    load_table.wait()
    gain_rows(tabv, 0, gain1)
    gain_rows(tabv, 2, gain2)
    load_t = pltpu.make_async_copy(teacher_any, teach, in_sem.at[2])
    load_t.start()
    load_c = pltpu.make_async_copy(cotangent_any, cot, in_sem.at[3])
    load_c.start()
    norm_rows(x, gain1, n1, tokens)

    def copy_x(t):
        r = tile_rows(t, 32)
        acc[r] = x[r].astype(F32)

    loop(tokens // 32, copy_x)
    turn(n1, turned, tokens)
    n1_copy = pltpu.make_async_copy(turned, n1_out, out_sem.at[0])
    n1_copy.start()
    for r in keep:
        r.wait()
    g.arrived(0)

    def load_w(i, slot):
        return pltpu.make_async_copy(
            whole.at[i % 4, :, lanes_of(i // 4)], wbuf.at[slot], w_sem.at[slot]
        )

    load_w(0, 0).start()

    def probs_copy(dd, m, slot):
        return pltpu.make_async_copy(ps.at[slot], probs_out.at[dd * micro + m], p_sem.at[slot])

    def attention(dd):
        slot = dd % 2
        pl.when(dd < 3)(lambda: load_w(dd + 1, 1 - slot).start())
        load_w(dd, slot).wait()
        pl.when(dd > 0)(lambda: pltpu.make_async_copy(qs, qkv_out.at[dd], q_sem).wait())
        qs[:, 0:576] = nn(n1[...], wbuf[slot, :, 0:576]).astype(BF)
        g.step(8 + 2 * dd)
        for m in range(micro):
            r = slice(m * seq, (m + 1) * seq)
            pl.when(dd > 0)(lambda: probs_copy(dd, m, m).wait())
            for hh in range(per):
                a = hh * size
                s = nt(qs[r, a : a + size], qs[r, 192 + a : 192 + a + size]) + bias[dd * per + hh]
                s = jnp.where(mask[m] > 0.0, s, NEG)
                top = jnp.max(s, axis=-1, keepdims=True)
                e = jnp.exp(s - top)
                p = e * (1.0 / jnp.sum(e, axis=-1, keepdims=True))
                ps[m, hh] = p
                qs[r, 576 + a : 576 + a + size] = nn(p.astype(BF), qs[r, 384 + a : 384 + a + size]).astype(BF)
            probs_copy(dd, m, m).start()
        g.step(9 + 2 * dd)
        for m in range(micro):
            r = slice(m * seq, (m + 1) * seq)
            acc[r] += nt(qs[r, 576:768], wbuf[slot, :, 576:768])
        pltpu.make_async_copy(qs, qkv_out.at[dd], q_sem).start()

    loop(4, attention)
    pltpu.make_async_copy(qs, qkv_out.at[0], q_sem).wait()
    for m in range(micro):
        probs_copy(3, m, m).wait()
    mid_copy = pltpu.make_async_copy(acc, middle_out, out_sem.at[1])
    mid_copy.start()
    norm_rows(acc, gain2, n2, tokens)
    n1_copy.wait()
    turn(n2, turned, tokens)
    n2_copy = pltpu.make_async_copy(turned, n2_out, out_sem.at[2])
    n2_copy.start()
    mid_copy.wait()

    def pre_copy(t, slot):
        return pltpu.make_async_copy(pre.at[slot], pre_out.at[t], pre_sem.at[slot])

    def act_copy(t, slot):
        return pltpu.make_async_copy(act.at[slot], act_out.at[t], act_sem.at[slot])

    def feed(t):
        slot = t % 2

        @pl.when(t % 4 == 0)
        def _():
            g.arrived(1 + t // 4)
            load_w(4 + t, slot).start()

        pl.when(t % 4 < 3)(lambda: load_w(5 + t, 1 - slot).start())
        load_w(4 + t, slot).wait()

        @pl.when(t > 1)
        def _():
            pre_copy(t, slot).wait()
            act_copy(t, slot).wait()

        for m in range(micro):
            r = slice(m * seq, (m + 1) * seq)
            gu = nn(n2[r], wbuf[slot, :, 0 : 2 * CHUNK])
            pre[slot, r] = gu
            ge, _ = gelu_parts(gu[:, 0:CHUNK])
            act[slot, r] = (ge * gu[:, CHUNK:]).astype(BF)
        pre_copy(t, slot).start()
        act_copy(t, slot).start()

        @pl.when(t < 8)
        def _():
            pl.when(t % 2 == 1)(lambda: g.step(16 + t // 2))

        pl.when((t >= 8) & (t < 12))(lambda: g.step(12 + t))
        for m in range(micro):
            r = slice(m * seq, (m + 1) * seq)
            acc[r] += nt(act[slot, r], wbuf[slot, :, 2 * CHUNK :])

    loop(16, feed)
    load_t.wait()
    load_c.wait()
    n2_copy.wait()
    for slot in range(2):
        pre_copy(14 + slot, slot).wait()
        act_copy(14 + slot, slot).wait()
    total = tabv[0, 4:5, 0:1]
    for i in range(1, 32):
        total = total + tabv[i, 4:5, 0:1]
    factor = (2.0 * scale / width) / total
    lossv[...] = jnp.zeros_like(lossv)

    def ends(t):
        r = tile_rows(t, 16)
        full = acc[r]
        gap = full - teach[r].astype(F32)
        weighted = valid_col[r] * gap
        grad = scale * cot[r].astype(F32) + factor * weighted
        acc[r] = grad
        x[r] = grad.astype(BF)
        n1[r] = full.astype(BF)
        lossv[...] += weighted * gap

    loop(tokens // 16, ends)
    copies = [
        pltpu.make_async_copy(n1, layer_out, out_sem.at[0]),
        pltpu.make_async_copy(acc, grad_out, out_sem.at[1]),
        pltpu.make_async_copy(x, gffn_out, out_sem.at[2]),
    ]
    for r in copies:
        r.start()
    loss_out[...] = jnp.zeros_like(loss_out) + jnp.sum(lossv[...])
    g.finish()
    for r in copies:
        r.wait()


def forward(own, tile, x, teacher, cotangent, buckets, bias_table, blocks_row, blocks_col, valid_row, valid_col, scale):
    packs = own.shape[1] // LANES
    tokens, width = x.shape
    seq = buckets.shape[0]
    heads = bias_table.shape[1]
    micro = tokens // seq
    any_ = pl.BlockSpec(memory_space=pl.ANY)
    vmem = pl.BlockSpec(memory_space=pltpu.VMEM)
    smem = pl.BlockSpec(memory_space=pltpu.SMEM)
    S = jax.ShapeDtypeStruct
    dma = pltpu.SemaphoreType.DMA
    outs = (
        S((4, 8 * ROWS, own.shape[1]), BF), S((32, 8, 128), F32), S((width, tokens), BF), S((width, tokens), BF),
        S((4, tokens, 768), BF), S((4 * micro, heads // 4, seq, seq), F32), S((16, tokens, 2 * CHUNK), F32),
        S((16, tokens, CHUNK), BF), S((tokens, width), F32), S((tokens, width), BF), S((tokens, width), F32), S((tokens, width), BF), S((8, 128), F32),
    )
    return pl.pallas_call(
        functools.partial(forward_kernel, packs, tokens, width, seq, heads, scale),
        out_shape=outs,
        in_specs=[any_] * 5 + [vmem, smem] + [vmem] * 4,
        out_specs=[any_] * 12 + [vmem],
        scratch_shapes=[
            pltpu.VMEM((tokens, width), BF), pltpu.VMEM((tokens, width), BF), pltpu.VMEM((tokens, width), BF),
            pltpu.VMEM((width, tokens), BF), pltpu.VMEM((tokens, width), F32), pltpu.VMEM((heads, seq, seq), F32), pltpu.VMEM((micro, seq, seq), F32),
            pltpu.VMEM((2, 8 * ROWS, LANES), BF), pltpu.VMEM((tokens, 768), BF), pltpu.VMEM((micro, heads // 4, seq, seq), F32),
            pltpu.VMEM((2, tokens, 2 * CHUNK), F32), pltpu.VMEM((2, tokens, CHUNK), BF), pltpu.VMEM((32, 8, 128), F32),
            pltpu.VMEM((1, width), F32), pltpu.VMEM((1, width), F32), pltpu.VMEM((tokens, width), BF),
            pltpu.VMEM((tokens, width), BF), pltpu.VMEM((16, width), F32),
            dma((packs, G_COUNT)), dma((packs, G_COUNT)), dma((packs,)), dma, dma, dma, dma((4,)), dma((2,)), dma((2,)), dma,
            dma((2,)), dma((2,)), dma((3,)),
        ],
        compiler_params=pltpu.CompilerParams(collective_id=1, has_side_effects=True, vmem_limit_bytes=63 * 1024 * 1024),
    )(own, tile, x, teacher, cotangent, buckets, bias_table, blocks_row, blocks_col, valid_row, valid_col)


def prepare(weights, gain_one, gain_two, valid):
    part = weights[4].shape[1]
    blank = jnp.zeros((ROWS, 4 * CHUNK - part), BF)
    pieces = list(weights[:4])
    for j in range(4):
        for w in weights[4:]:
            pieces.append(w[:, j * CHUNK : min((j + 1) * CHUNK, part)])
            if j == 3:
                pieces.append(blank)
    own = jnp.concatenate(pieces, axis=1)
    me = lax.axis_index("fsdp") * 4 + lax.axis_index("dp")
    first = (me * 48) % 128

    def lines(gain):
        return lax.dynamic_update_slice(jnp.zeros((256,), F32), gain.astype(F32), (first,)).reshape(2, 128)

    count = jnp.zeros((4, 128), F32) + jnp.sum(valid.astype(F32))
    return own, jnp.concatenate([lines(gain_one), lines(gain_two), count])


def gelu_slope(u, t):
    root = 0.7978845608028654
    return 0.5 * (1.0 + t) + 0.5 * u * (1.0 - t * t) * root * (1.0 + 3.0 * 0.044715 * (u * u))


def norm_back(src_row, up_row, gain, gain_sum):
    v, u = src_row, up_row
    scale = lax.rsqrt(jnp.mean(v * v, axis=-1, keepdims=True) + EPS)
    scaled = u * gain
    mean = jnp.mean(scaled * v, axis=-1, keepdims=True)
    term = u * v * scale
    total = term[0:8]
    for i in range(1, term.shape[0] // 8):
        total = total + term[8 * i : 8 * i + 8]
    gain_sum[...] += total
    return scale * scaled - v * (scale * scale * scale) * mean


def backward_kernel(
    packs, tokens, width, seq, heads,
    whole, table, x_any, n1_any, n2_any, qkv_any, probs_any, pre_any, act_any, mid_any, gout_any, gffn_any, buckets, loss,
    part, out, hidden_out, tiles_out, sums_out, gs_out,
    low, src, acc, acc2, wbuf, pre, act, ggu, gst, qs, ps, gqkv, bsum, gain1, gain2, sum1, sum2, tilev,
    in_sem, w_sem, pre_sem, act_sem, g_sem, s_sem, q_sem, p_sem, out2_sem, gs_sem, tile_send, tile_recv, tile_local, *scatter_refs,
):
    micro = tokens // seq
    per = heads // 4
    size = 192 // per
    me = lax.axis_index("fsdp") * 4 + lax.axis_index("dp")
    tell_all()
    rs = Scatter(part, out, *scatter_refs, packs)

    def fetch(a, b, sem):
        r = pltpu.make_async_copy(a, b, sem)
        r.start()
        return r

    loads = [fetch(gffn_any, low, in_sem.at[0]), fetch(n2_any, src, in_sem.at[1]), fetch(table, tilev, in_sem.at[2])]

    def load_w(i, slot):
        return pltpu.make_async_copy(whole.at[i % 4, :, lanes_of(i // 4)], wbuf.at[slot], w_sem.at[slot])

    def load_pre(t, slot):
        return pltpu.make_async_copy(pre_any.at[t], pre.at[slot], pre_sem.at[slot])

    def load_act(t, slot):
        return pltpu.make_async_copy(act_any.at[t], act.at[slot], act_sem.at[slot])

    def put_g(dd, lane_pack):
        return pltpu.make_async_copy(gst, part.at[dd, :, lanes_of(lane_pack)], g_sem)

    for r in (load_w(4, 0), load_pre(0, 0), load_act(0, 0)):
        r.start()
    mid_load = fetch(mid_any, acc2, in_sem.at[3])
    wide = 2 * CHUNK
    gout_loads = [
        pltpu.make_async_copy(gout_any.at[:, pl.ds(i * wide, wide)], pre.at[i], s_sem.at[i]) for i in range(2)
    ]
    for m in range(micro):
        rows = pl.ds(m * seq, seq)
        gout_loads.append(pltpu.make_async_copy(gout_any.at[rows, pl.ds(2 * wide, seq)], ps.at[m, 0], s_sem.at[2 + 2 * m]))
        gout_loads.append(
            pltpu.make_async_copy(
                gout_any.at[rows, pl.ds(2 * wide + seq, 128)], ps.at[m, 1, :, pl.ds(0, 128)], s_sem.at[3 + 2 * m]
            )
        )
    for r in gout_loads[2:]:
        r.start()
    sum1[...] = jnp.zeros_like(sum1)
    sum2[...] = jnp.zeros_like(sum2)

    def clear(t):
        r = tile_rows(t, 32)
        acc[r] = jnp.zeros((32, width), F32)

    loop(tokens // 32, clear)
    for r in loads:
        r.wait()
    gain_rows(tilev, 0, gain1)
    gain_rows(tilev, 2, gain2)
    half = width // 2

    def feed(t):
        slot = t % 2

        @pl.when(t < 15)
        def _():
            load_w(5 + t, 1 - slot).start()
            load_pre(t + 1, 1 - slot).start()
            load_act(t + 1, 1 - slot).start()

        load_w(4 + t, slot).wait()
        load_pre(t, slot).wait()
        load_act(t, slot).wait()
        for m in range(micro):
            r = slice(m * seq, (m + 1) * seq)
            gh = nn(low[r], wbuf[slot, :, 2 * CHUNK :])
            u = pre[slot, r, 0:CHUNK]
            ge, th = gelu_parts(u)
            ggu[r, 0:CHUNK] = (gh * pre[slot, r, CHUNK:] * gelu_slope(u, th)).astype(BF)
            ggu[r, CHUNK:] = (gh * ge).astype(BF)
        pl.when((t > 0) & (t != 4))(lambda: put_g(0, 0).wait())
        for h in range(2):
            c = slice(h * half, (h + 1) * half)
            gst[c, 0 : 2 * CHUNK] = nn(src[c], ggu[...]).astype(BF)
            gst[c, 2 * CHUNK :] = tn(low[:, c], act[slot]).astype(BF)
        put_g(t % 4, 1 + t // 4).start()
        for m in range(micro):
            r = slice(m * seq, (m + 1) * seq)
            acc[r] += nt(ggu[r], wbuf[slot, :, 0 : 2 * CHUNK])

        @pl.when(t == 3)
        def _():
            put_g(0, 0).wait()
            hear_all()
            rs.launch()

        pl.when((t == 4) | (t == 6))(lambda: rs.step(t // 2 - 2))
        pl.when(t >= 8)(lambda: rs.step(t - 6))

    loop(16, feed)
    put_g(0, 0).wait()
    n1_load = fetch(n1_any, src, in_sem.at[1])
    load_w(0, 0).start()

    def probs_load(dd, m):
        return pltpu.make_async_copy(probs_any.at[dd * micro + m], ps.at[m], p_sem.at[m])

    def q_load(dd):
        return pltpu.make_async_copy(qkv_any.at[dd], qs, q_sem)

    for r in gout_loads[:2]:
        r.start()
    q_load(0).start()
    mid_load.wait()
    for r in gout_loads:
        r.wait()
    for m in range(micro):

        def norm_two(t, m=m):
            r = tile_rows(m * (seq // 32) + t, 32)
            h = tile_rows(t, 32)
            gout = jnp.concatenate([pre[0, r], pre[1, r], ps[m, 0, h], ps[m, 1, h, 0:128]], axis=1)
            grad = gout + norm_back(acc2[r], acc[r], gain2[...], sum2)
            acc[r] = grad
            acc2[r] = jnp.zeros((32, width), F32)
            low[r] = grad.astype(BF)

        loop(seq // 32, norm_two)
        probs_load(0, m).start()
    n1_load.wait()
    rs.step(10)

    def gs_copy(dd):
        return pltpu.make_async_copy(ps.at[micro - 1], gs_out.at[dd], gs_sem.at[0])

    def gs_load(dd):
        return pltpu.make_async_copy(gs_out.at[dd], ps.at[dd % 2], gs_sem.at[dd % 2])

    def attention(dd):
        slot = dd % 2
        pl.when(dd < 3)(lambda: load_w(dd + 1, 1 - slot).start())
        load_w(dd, slot).wait()
        gqkv[:, 576:768] = nn(low[...], wbuf[slot, :, 576:768]).astype(BF)
        q_load(dd).wait()

        @pl.when(dd > 0)
        def _():
            gs_copy(dd).wait()
            probs_load(dd, micro - 1).start()
            put_g(0, 0).wait()

        gst[:, 576:768] = tn(low[...], qs[:, 576:768]).astype(BF)
        for m in range(micro):
            r = slice(m * seq, (m + 1) * seq)
            probs_load(dd, m).wait()
            for hh in range(per):
                a = hh * size
                p = ps[m, hh]
                go = gqkv[r, 576 + a : 576 + a + size]
                gp = nt(go, qs[r, 384 + a : 384 + a + size])
                gs = p * (gp - jnp.sum(p * gp, axis=-1, keepdims=True))
                gs = gs.astype(BF)
                gqkv[r, a : a + size] = nn(gs, qs[r, 192 + a : 192 + a + size]).astype(BF)
                gqkv[r, 192 + a : 192 + a + size] = tn(gs, qs[r, a : a + size]).astype(BF)
                gqkv[r, 384 + a : 384 + a + size] = tn(p.astype(BF), go).astype(BF)
                ps[m, hh] = gs.astype(F32) if m == 0 else ps[m - 1, hh] + gs.astype(F32)
        gs_copy(dd).start()

        @pl.when(dd < 3)
        def _():
            q_load(dd + 1).start()
            probs_load(dd + 1, 0).start()

        rs.step(11 + dd)
        for h in range(2):
            c = slice(h * half, (h + 1) * half)
            gst[c, 0:576] = nn(src[c], gqkv[:, 0:576]).astype(BF)
        put_g(dd, 0).start()
        for m in range(micro):
            r = slice(m * seq, (m + 1) * seq)
            acc2[r] += nt(gqkv[r, 0:576], wbuf[slot, :, 0:576])


    loop(4, attention)
    put_g(0, 0).wait()
    gs_copy(0).wait()
    rs.ahead(jnp.int32(4 * packs - 4))
    rs.ahead(jnp.int32(4 * packs - 3))
    gs_load(0).start()
    rs.step(15)
    x_load = fetch(x_any, low, in_sem.at[1])
    x_load.wait()

    def norm_one(t):
        r = tile_rows(t, 32)
        term = norm_back(low[r].astype(F32), acc2[r], gain1[...], sum1)
        low[r] = (acc[r] + term).astype(BF)

    loop(tokens // 32, norm_one)
    hidden_copy = fetch(low, hidden_out, out2_sem)
    rs.step(16)

    def buckets_of(dd):
        gs_load(dd).wait()
        pl.when(dd < 3)(lambda: gs_load(dd + 1).start())

        def by_bucket(group):
            def some(t, totals):
                r = tile_rows(t, 8)
                b = buckets[r]
                v = [ps[dd % 2, hh, r] for hh in range(per)]
                new = []
                for j in range(4):
                    here = b == group * 4 + j
                    new += [totals[j * per + hh] + jnp.where(here, v[hh], 0.0) for hh in range(per)]
                return tuple(new)

            totals = lax.fori_loop(0, seq // 8, some, (jnp.zeros((8, seq), F32),) * (4 * per))
            for j in range(4):
                for hh in range(per):
                    bsum[dd * per + hh, pl.ds(group * 4 + j, 1)] = jnp.sum(totals[j * per + hh], axis=0, keepdims=True)

        loop(8, by_bucket)
        rs.step(17 + dd)

    loop(4, buckets_of)
    one = jnp.sum(sum1[...], axis=0, keepdims=True)
    two = jnp.sum(sum2[...], axis=0, keepdims=True)
    biases = lax.dot_general(
        jnp.ones((8, seq), F32), bsum[...].reshape(heads * 32, seq), (((1,), (1,)), ((), ())),
        precision=lax.Precision.HIGHEST, preferred_element_type=F32,
    )
    lines = [biases[0:1, 128 * i : 128 * (i + 1)] for i in range(3)]
    none = jnp.zeros((1, 128), F32)
    for i in range(32):
        first = 128 * ((48 * i) // 128)
        rows = []
        for v in (one, two):
            rows.append(v[:, first : first + 128])
            rows.append(v[:, first + 128 : first + 256] if first + 128 < width else none)
        tilev[i] = jnp.concatenate(rows + [loss[0:1, :]] + lines, axis=0)
    tile_copy = fetch(tilev, tiles_out, in_sem.at[0])
    tile_copy.wait()
    tiles = exchange(lambda other: tiles_out.at[other], sums_out, tile_send, tile_recv)
    tile_keep = fetch(tilev.at[me], sums_out.at[me], tile_local)
    lax.fori_loop(21, 4 * packs + 4, lambda s, carry: (rs.step(s), carry)[1], 0)
    rs.finish()
    hidden_copy.wait()
    tile_keep.wait()
    tiles.wait()


def backward(whole, table, x, n1, n2, qkv, probs, pre, act, mid, gout, gffn, buckets, loss, heads):
    packs = whole.shape[2] // LANES
    tokens, width = x.shape
    seq = buckets.shape[0]
    micro = tokens // seq
    any_ = pl.BlockSpec(memory_space=pl.ANY)
    vmem = pl.BlockSpec(memory_space=pltpu.VMEM)
    S = jax.ShapeDtypeStruct
    V = pltpu.VMEM
    dma = pltpu.SemaphoreType.DMA
    outs = (
        S(whole.shape, BF), S((ROWS, whole.shape[2]), F32), S((tokens, width), BF), S((32, 8, 128), F32), S((32, 8, 128), F32),
        S((4, heads // 4, seq, seq), F32),
    )
    return pl.pallas_call(
        functools.partial(backward_kernel, packs, tokens, width, seq, heads),
        out_shape=outs,
        in_specs=[any_] * 12 + [vmem] * 2,
        out_specs=[any_] * 6,
        scratch_shapes=[
            V((tokens, width), BF), V((width, tokens), BF), V((tokens, width), F32), V((tokens, width), F32),
            V((2, 8 * ROWS, LANES), BF), V((2, tokens, 2 * CHUNK), F32), V((2, tokens, CHUNK), BF), V((tokens, 2 * CHUNK), BF),
            V((8 * ROWS, LANES), BF), V((tokens, 768), BF), V((micro, heads // 4, seq, seq), F32),
            V((tokens, 768), BF), V((heads, 32, seq), F32), V((1, width), F32), V((1, width), F32),
            V((8, width), F32), V((8, width), F32), V((32, 8, 128), F32),
            dma((4,)), dma((2,)), dma((2,)), dma((2,)), dma, dma((6,)), dma, dma((micro,)), dma, dma((2,)), dma, dma, dma,
        ] + scatter_scratch(packs),
        compiler_params=pltpu.CompilerParams(collective_id=2, has_side_effects=True, vmem_limit_bytes=67043328),
    )(whole, table, x, n1, n2, qkv, probs, pre, act, mid, gout, gffn, buckets, loss)


def tuned_body(
    hidden, teacher, cotangent, valid_mask, blocks, buckets, first_gain, query_weight, key_weight, value_weight,
    output_weight, second_gain, gate_weight, up_weight, down_weight, bias_table,
):
    micro, _, seq, width = hidden.shape
    tokens = micro * seq
    bucket_count, heads = bias_table.shape
    part = gate_weight.shape[1]
    cols = query_weight.shape[1]
    per = first_gain.shape[0]
    scale = float(tokens * 32 * width)
    valid = valid_mask.reshape(micro, seq)
    block_ids = blocks.reshape(micro, seq)
    weights = (query_weight, key_weight, value_weight, output_weight, gate_weight, up_weight, down_weight)
    own, tile = prepare(weights, first_gain, second_gain, valid)
    x = hidden.reshape(tokens, width)
    whole, table, n1, n2, qkv, probs, pre, act, mid, layer, gout, gffn, loss = forward(
        own, tile, x, teacher.reshape(tokens, width), cotangent.reshape(tokens, width), buckets, bias_table.astype(F32),
        block_ids, block_ids.reshape(tokens, 1), valid, valid.reshape(tokens, 1).astype(F32), scale,
    )
    _, shard, hidden_grad, _, sums, _ = backward(
        whole, table, x, n1, n2, qkv, probs, pre, act, mid, gout, gffn, buckets, loss, heads
    )
    sums = jnp.sum(sums, axis=0)
    me = lax.axis_index("fsdp") * 4 + lax.axis_index("dp")
    first = (me * per) % 128
    gain_one = lax.dynamic_slice(sums[0:2].reshape(256), (first,), (per,))
    gain_two = lax.dynamic_slice(sums[2:4].reshape(256), (first,), (per,))
    valid_total = jnp.sum(table[:, 4, 0])
    ff = [
        jnp.concatenate([shard[:, LANES * (j + 1) + i * CHUNK : LANES * (j + 1) + (i + 1) * CHUNK] for j in range(4)], axis=1)[:, :part]
        for i in range(3)
    ]
    at = [shard[:, i * cols : (i + 1) * cols] for i in range(4)]
    return (
        layer.reshape(hidden.shape),
        sums[4, 0] / (valid_total * width),
        hidden_grad.reshape(hidden.shape),
        gain_one, at[0], at[1], at[2], at[3], gain_two, ff[0], ff[1], ff[2],
        sums[5:8].reshape(heads, bucket_count).T,
    )


def solution(mesh):
    in_specs = (
        P(None, ("fsdp", "dp"), None, None),
        P(None, ("fsdp", "dp"), None, None),
        P(None, ("fsdp", "dp"), None, None),
        P(None, ("fsdp", "dp"), None),
        P(None, ("fsdp", "dp"), None),
        P(),
        P(("fsdp", "dp")),
        P("fsdp", "dp"),
        P("fsdp", "dp"),
        P("fsdp", "dp"),
        P("fsdp", "dp"),
        P(("fsdp", "dp")),
        P("fsdp", "dp"),
        P("fsdp", "dp"),
        P("fsdp", "dp"),
        P(),
    )
    out_specs = (
        P(None, ("fsdp", "dp"), None, None),
        P(),
        P(None, ("fsdp", "dp"), None, None),
        P(("fsdp", "dp")),
        P("fsdp", "dp"),
        P("fsdp", "dp"),
        P("fsdp", "dp"),
        P("fsdp", "dp"),
        P(("fsdp", "dp")),
        P("fsdp", "dp"),
        P("fsdp", "dp"),
        P("fsdp", "dp"),
        P(),
    )
    chosen = tuned_body if dict(mesh.shape) == {"fsdp": 8, "dp": 4} else body
    return jax.shard_map(chosen, mesh=mesh, in_specs=in_specs, out_specs=out_specs, check_vma=False)
```
